32 devices in a mesh: dp: 16 (over z, x, core), fsdp: 2 (over y).
Axes of the slice: x: 2, y: 2, z: 4, core: 2. Of those that a mesh axis runs over, the one named last changes fastest.
Arguments:
- hidden_in: bfloat16 [32, 1024, 1024], P(('dp', 'fsdp')), may hold values from -6 to 6
- segment_ids: int32 [32, 1024], P(('dp', 'fsdp')), may hold values from 0 to 7, as said below
- out_grad: bfloat16 [32, 1024, 1024], P(('dp', 'fsdp')), may hold values from -6 to 6
- norm1_gain: bfloat16 [1024], P(('dp', 'fsdp')), may hold values from 0.099609375 to 1.8984375
- norm1_bias: bfloat16 [1024], P(('dp', 'fsdp')), may hold values from -1.75 to 1.75
- norm2_gain: bfloat16 [1024], P(('dp', 'fsdp')), may hold values from 0.099609375 to 1.8984375
- norm2_bias: bfloat16 [1024], P(('dp', 'fsdp')), may hold values from -1.75 to 1.75
- qkv_weight: bfloat16 [1024, 3072], P(('dp', 'fsdp')), may hold values from -0.25 to 0.25
- qkv_bias: bfloat16 [3072], P(('dp', 'fsdp')), may hold values from -1.75 to 1.75
- proj_weight: bfloat16 [1024, 1024], P(('dp', 'fsdp')), may hold values from -0.75 to 0.75
- proj_bias: bfloat16 [1024], P(('dp', 'fsdp')), may hold values from -1.75 to 1.75
- up_weight: bfloat16 [1024, 4096], P(('dp', 'fsdp')), may hold values from -0.1875 to 0.1875
- up_bias: bfloat16 [4096], P(('dp', 'fsdp')), may hold values from -1.75 to 1.75
- down_weight: bfloat16 [4096, 1024], P(('dp', 'fsdp')), may hold values from -0.09375 to 0.09375
- down_bias: bfloat16 [1024], P(('dp', 'fsdp')), may hold values from -1.75 to 1.75
Outputs:
- layer_out: bfloat16 [32, 1024, 1024], P(('dp', 'fsdp'))
- input_grad: bfloat16 [32, 1024, 1024], P(('dp', 'fsdp'))
- norm1_gain_grad: float32 [1024], P(('dp', 'fsdp'))
- norm1_bias_grad: float32 [1024], P(('dp', 'fsdp'))
- norm2_gain_grad: float32 [1024], P(('dp', 'fsdp'))
- norm2_bias_grad: float32 [1024], P(('dp', 'fsdp'))
- qkv_weight_grad: float32 [1024, 3072], P(('dp', 'fsdp'))
- qkv_bias_grad: float32 [3072], P(('dp', 'fsdp'))
- proj_weight_grad: float32 [1024, 1024], P(('dp', 'fsdp'))
- proj_bias_grad: float32 [1024], P(('dp', 'fsdp'))
- up_weight_grad: float32 [1024, 4096], P(('dp', 'fsdp'))
- up_bias_grad: float32 [4096], P(('dp', 'fsdp'))
- down_weight_grad: float32 [4096, 1024], P(('dp', 'fsdp'))
- down_bias_grad: float32 [1024], P(('dp', 'fsdp'))
The draws below stay inside these ranges and needn't reach their ends.
Inputs may be any that keep to these rules, and one draw needn't show every extreme that they name: `segment_ids`: within a sequence the ids never fall. A sequence holds 3 to 7 documents with ids 0, 1, 2 and so on, each of 60 to 800 tokens, followed by 0 to 64 padding tokens with id 8 - 1; ids between the last document's and 7 are unused. In every draw some document has exactly 800 tokens and some sequence exactly 64 padding tokens.
All inputs are finite; a program needn't handle non-finite values.
Results may differ from the reference program's by a relative error of at most 0.012.
The reference program's roundings to bfloat16 on the way count: a program that leaves them out, or rounds other values in their place, can miss the bound.
Values may be sent and summed in bfloat16 or wider, within the bound.
No kernel may reach another device: no remote copies, remote signals or barrier semaphores. Data moves between devices by JAX's collectives and lax.ppermute only.
A program may use at most 384 MiB of HBM per device.

```python
import jax
import jax.numpy as jnp
from jax import lax

D = 1024
HEADS = 16
HEAD = 64
FF = 4096
ROT = 16
LEN = 1024
DOCS = 8
DOC_MOST = 800
DOC_LEAST = 60
PAD_MOST = 64
SEQS = 32


def draw_segment_ids(key, part):
    count_key = jax.random.fold_in(key, 11)
    weight_key = jax.random.fold_in(key, 12)
    padding_key = jax.random.fold_in(key, 13)
    doc_count = jax.random.randint(count_key, (SEQS,), 3, DOCS).astype(jnp.int32)
    weights = jax.random.randint(weight_key, (SEQS, DOCS - 1), 1, 5).astype(jnp.int32)
    padding = jax.random.randint(padding_key, (SEQS,), 0, PAD_MOST + 1).astype(jnp.int32)
    slots = jnp.arange(DOCS - 1, dtype=jnp.int32)
    active = slots[None, :] < doc_count[:, None]
    weights = jnp.where(active, weights, 0)
    spare = LEN - padding - doc_count * DOC_LEAST
    extra = weights * spare[:, None] // jnp.sum(weights, axis=1, keepdims=True)
    is_last = slots[None, :] == doc_count[:, None] - 1
    extra_total = jnp.sum(extra, axis=1, keepdims=True)
    extra = jnp.where(is_last, extra + spare[:, None] - extra_total, extra)
    lengths = jnp.where(active, DOC_LEAST + extra, 0).astype(jnp.int32)
    rest_tokens = LEN - PAD_MOST - DOC_MOST
    second_len = rest_tokens // 2
    third_len = rest_tokens - second_len
    fixed_row = jnp.where(slots == 0, DOC_MOST, jnp.where(slots == 1, second_len, jnp.where(slots == 2, third_len, 0))).astype(jnp.int32)
    lengths = lengths.at[0].set(fixed_row)
    padding = padding.at[0].set(PAD_MOST)
    ends = jnp.cumsum(lengths, axis=1)
    position = jnp.arange(LEN, dtype=jnp.int32)
    segment = jnp.sum((position[None, :, None] >= ends[:, None, :]).astype(jnp.int32), axis=2)
    used = LEN - padding
    segment = jnp.where(position[None, :] >= used[:, None], DOCS - 1, segment)
    return segment.astype(jnp.int32)


def block_scale(own_key, extent, cuts, smallest, largest):
    loudness = 1.0
    for dim, blocks in cuts:
        draws = jax.random.uniform(jax.random.fold_in(jax.random.fold_in(own_key, 6), dim), (blocks,), jnp.float32, smallest / len(cuts), largest / len(cuts))
        loudness = loudness * jnp.repeat(jnp.exp(draws), extent[dim] // blocks).reshape((-1,) + (1,) * (len(extent) - 1 - dim))
    return loudness


def scatter_about(key, dims, deviation, most, split=(), kind=jnp.bfloat16):
    drawn = deviation * jax.random.normal(key, dims, jnp.float32)
    if split:
        drawn = drawn * block_scale(key, dims, split, -0.22, 0.18)
    return jnp.clip(drawn, -most, most).astype(kind)


def setup_inputs(seed: int = 0) -> dict:
    seeds = jax.random.split(jax.random.key(seed), 16)
    return {
        "hidden_in": scatter_about(seeds[0], (SEQS, LEN, D), 1.0, 6.0, ((0, 32),)),
        "segment_ids": draw_segment_ids(jax.random.fold_in(seeds[15], 71), 0),
        "out_grad": scatter_about(seeds[2], (SEQS, LEN, D), 1.0, 6.0, ((0, 32),)),
        "norm1_gain": jnp.clip(1.0 + 0.18 * jax.random.normal(seeds[3], (D,), jnp.float32), 0.099609375, 1.8984375).astype(jnp.bfloat16),
        "norm1_bias": scatter_about(seeds[4], (D,), 0.3, 1.75, ((0, 32),)),
        "norm2_gain": jnp.clip(1.0 + 0.18 * jax.random.normal(seeds[5], (D,), jnp.float32), 0.099609375, 1.8984375).astype(jnp.bfloat16),
        "norm2_bias": scatter_about(seeds[6], (D,), 0.3, 1.75, ((0, 32),)),
        "qkv_weight": scatter_about(seeds[7], (D, 3 * D), (D // 2) ** -0.5, 0.25, ((0, 32),)),
        "qkv_bias": scatter_about(seeds[8], (3 * D,), 0.3, 1.75, ((0, 32),)),
        "proj_weight": scatter_about(seeds[9], (D, D), (D // 16) ** -0.5, 0.75, ((0, 32),)),
        "proj_bias": scatter_about(seeds[10], (D,), 0.3, 1.75, ((0, 32),)),
        "up_weight": scatter_about(seeds[11], (D, FF), D ** -0.5, 0.1875, ((0, 32),)),
        "up_bias": scatter_about(seeds[12], (FF,), 0.3, 1.75, ((0, 32),)),
        "down_weight": scatter_about(seeds[13], (FF, D), FF ** -0.5, 0.09375, ((0, 32),)),
        "down_bias": scatter_about(seeds[14], (D,), 0.3, 1.75, ((0, 32),)),
    }


@jax.custom_vjp
def low(v):
    return lax.optimization_barrier(v.astype(jnp.bfloat16)).astype(jnp.float32)

@jax.custom_vjp
def low_back(v):
    return v

def low_keep(v):
    return (low(v), None)

def low_pass(kept, grad):
    return (grad,)

def back_keep(v):
    return (v, None)

def back_low(kept, grad):
    return (low(grad),)
low.defvjp(low_keep, low_pass)
low_back.defvjp(back_keep, back_low)
norm_eps = 1e-05
masked_score = -1e+30

def matmul(left, right):
    return jnp.dot(left, right, precision=lax.Precision.HIGHEST, preferred_element_type=jnp.float32)

def normed(values, gain):
    center = values - lax.optimization_barrier(jnp.mean(values, axis=-1, keepdims=True))
    spread = lax.optimization_barrier(jnp.mean(center * center, axis=-1, keepdims=True))
    return center * lax.rsqrt(spread + norm_eps) * gain

def rotate(part, cosine, sine):
    half_rot = ROT // 2
    first = part[..., :half_rot]
    second = part[..., half_rot:ROT]
    cos_wide = cosine[..., None, :]
    sin_wide = sine[..., None, :]
    return jnp.concatenate([first * cos_wide - second * sin_wide, second * cos_wide + first * sin_wide, part[..., ROT:]], axis=-1)

def angles(segments):
    last_axis = segments.ndim - 1
    position = lax.broadcasted_iota(jnp.int32, segments.shape, last_axis)
    change = jnp.concatenate([jnp.ones(segments.shape[:-1] + (1,), jnp.bool_), segments[..., 1:] != segments[..., :-1]], axis=-1)
    first_index = lax.cummax(jnp.where(change, position, jnp.zeros_like(position)), axis=last_axis)
    place = (position - first_index).astype(jnp.float32)
    freqs = 10000.0 ** (-(jnp.arange(ROT // 2) * 2).astype(jnp.float32) / ROT)
    theta = place[..., None] * freqs
    return (jnp.cos(theta), jnp.sin(theta))

def layer_forward(hidden, params, segments, cosine, sine, valid):
    gain_one, shift_one, gain_two, shift_two, w_qkv, b_qkv, w_proj, b_proj, w_up, b_up, w_down, b_down = params
    groups, length = segments.shape
    normed_one = low(normed(hidden, gain_one) + shift_one)
    mixed = low_back(matmul(normed_one, low(w_qkv)) + b_qkv)
    raw = mixed.reshape(groups, length, 3, HEADS, HEAD)
    query = low(rotate(raw[:, :, 0], cosine, sine) * HEAD ** (-0.5))
    keys = low(rotate(raw[:, :, 1], cosine, sine))
    values = low(raw[:, :, 2])
    scores = low_back(jnp.einsum('bqhe,bkhe->bhqk', query, keys, precision=lax.Precision.HIGHEST))
    position = jnp.arange(length)
    allowed = (position[None, None, :] <= position[None, :, None]) & (segments[:, :, None] == segments[:, None, :])
    scores = jnp.where(allowed[:, None], scores, masked_score)
    row_max = lax.optimization_barrier(jnp.max(scores, axis=-1, keepdims=True))
    exponent = jnp.exp(scores - row_max)
    probs = low(exponent / lax.optimization_barrier(jnp.sum(exponent, axis=-1, keepdims=True)))
    attended = jnp.einsum('bhqk,bkhe->bqhe', probs, values, precision=lax.Precision.HIGHEST).reshape(groups, length, HEADS * HEAD)
    attended = low(low_back(attended * valid[..., None]))
    projected = matmul(attended, low(w_proj)) + b_proj
    normed_two = low(normed(hidden, gain_two) + shift_two)
    before = low_back(matmul(normed_two, low(w_up)) + b_up)
    after = low(jax.nn.gelu(before, approximate=False))
    return hidden + projected + matmul(after, low(w_down)) + b_down

def add_up(left, right):
    return left + right

def reference(hidden_in, segment_ids, out_grad, norm1_gain, norm1_bias, norm2_gain, norm2_bias, qkv_weight, qkv_bias, proj_weight, proj_bias, up_weight, up_bias, down_weight, down_bias):
    params = tuple((entry.astype(jnp.float32) for entry in (norm1_gain, norm1_bias, norm2_gain, norm2_bias, qkv_weight, qkv_bias, proj_weight, proj_bias, up_weight, up_bias, down_weight, down_bias)))
    cosine, sine = angles(segment_ids)
    valid = (segment_ids != DOCS - 1).astype(jnp.float32)
    group_count = SEQS // 4

    def grouped(values):
        return values.reshape((group_count, 4) + values.shape[1:])

    def group_step(totals, pieces):
        hidden, segments, grads, cos_part, sin_part, valid_part = pieces

        def forward(values, weights):
            return layer_forward(values, weights, segments, cos_part, sin_part, valid_part)
        result, pull = jax.vjp(forward, hidden.astype(jnp.float32), params)
        d_hidden, d_params = pull(grads.astype(jnp.float32))
        totals = jax.tree.map(add_up, totals, d_params)
        return (totals, (result.astype(jnp.bfloat16), d_hidden.astype(jnp.bfloat16)))
    zeros = tuple((jnp.zeros_like(entry) for entry in params))
    stacked = tuple((grouped(entry) for entry in (hidden_in, segment_ids, out_grad, cosine, sine, valid)))
    totals, (result, d_hidden) = lax.scan(group_step, zeros, stacked)
    layer_out = result.reshape(SEQS, LEN, D)
    input_grad = d_hidden.reshape(SEQS, LEN, D)
    return (layer_out, input_grad, totals[0], totals[1], totals[2], totals[3], totals[4], totals[5], totals[6], totals[7], totals[8], totals[9], totals[10], totals[11])
```

```python
from functools import partial

import jax
import jax.numpy as jnp
from jax import lax
from jax.experimental import pallas as pl
from jax.experimental.pallas import tpu as pltpu
from jax.sharding import PartitionSpec as P

AXES = ("dp", "fsdp")

HEADS = 16
HEAD = 64
ROT = 16
DOCS = 8


norm_eps = 1e-05
masked_score = -1e30


def normed(values, gain):
    center = values - jnp.mean(values, axis=-1, keepdims=True)
    spread = jnp.mean(center * center, axis=-1, keepdims=True)
    return center * lax.rsqrt(spread + norm_eps) * gain


def rotate(part, cosine, sine):
    half_rot = ROT // 2
    first = part[..., :half_rot]
    second = part[..., half_rot:ROT]
    cos_wide = cosine[..., None, :]
    sin_wide = sine[..., None, :]
    return jnp.concatenate(
        [
            first * cos_wide - second * sin_wide,
            second * cos_wide + first * sin_wide,
            part[..., ROT:],
        ],
        axis=-1,
    )


def angles(segments):
    last_axis = segments.ndim - 1
    position = lax.broadcasted_iota(jnp.int32, segments.shape, last_axis)
    change = jnp.concatenate(
        [jnp.ones(segments.shape[:-1] + (1,), jnp.bool_), segments[..., 1:] != segments[..., :-1]],
        axis=-1,
    )
    first_index = lax.cummax(jnp.where(change, position, jnp.zeros_like(position)), axis=last_axis)
    place = (position - first_index).astype(jnp.float32)
    freqs = 10000.0 ** (-(jnp.arange(ROT // 2) * 2).astype(jnp.float32) / ROT)
    theta = place[..., None] * freqs
    return (jnp.cos(theta), jnp.sin(theta))


def block_mask(segments, block_start, block_rows):
    length = segments.shape[0]
    query_pos = block_start + lax.broadcasted_iota(jnp.int32, (block_rows, length), 0)
    key_pos = lax.broadcasted_iota(jnp.int32, (block_rows, length), 1)
    same = segments[block_start : block_start + block_rows][:, None] == segments[None, :]
    return ((key_pos <= query_pos) & same)[None]


def attend_forward(pieces):
    query, keys, values, segments = pieces
    length = segments.shape[0]
    block_rows = min(512, length)
    outputs = []
    log_sums = []
    for block_start in range(0, length, block_rows):
        allowed = block_mask(segments, block_start, block_rows)
        scores = jnp.einsum(
            "qhe,khe->hqk",
            query[block_start : block_start + block_rows],
            keys,
            preferred_element_type=jnp.float32,
        )
        scores = jnp.where(allowed, scores, masked_score)
        row_max = jnp.max(scores, axis=-1, keepdims=True)
        exponent = jnp.exp(scores - row_max)
        total = jnp.sum(exponent, axis=-1, keepdims=True)
        weights = (exponent / total).astype(jnp.bfloat16)
        outputs.append(
            jnp.einsum("hqk,khe->qhe", weights, values, preferred_element_type=jnp.float32)
        )
        log_sums.append(row_max + jnp.log(total))
    return (jnp.concatenate(outputs, axis=0), jnp.concatenate(log_sums, axis=1))


def attend_backward(pieces):
    query, keys, values, segments, log_sums, d_out = pieces
    length = segments.shape[0]
    block_rows = min(512, length)
    query_parts = []
    d_keys = jnp.zeros(keys.shape, jnp.float32)
    d_values = jnp.zeros(values.shape, jnp.float32)
    for block_start in range(0, length, block_rows):
        block_end = block_start + block_rows
        allowed = block_mask(segments, block_start, block_rows)
        scores = jnp.einsum(
            "qhe,khe->hqk", query[block_start:block_end], keys, preferred_element_type=jnp.float32
        )
        scores = jnp.where(allowed, scores, masked_score)
        probs = jnp.exp(scores - log_sums[:, block_start:block_end])
        d_probs = jnp.einsum(
            "qhe,khe->hqk", d_out[block_start:block_end], values, preferred_element_type=jnp.float32
        )
        inner = jnp.sum(d_probs * probs, axis=-1, keepdims=True)
        d_scores = (probs * (d_probs - inner)).astype(jnp.bfloat16)
        d_values = d_values + jnp.einsum(
            "hqk,qhe->khe",
            probs.astype(jnp.bfloat16),
            d_out[block_start:block_end],
            preferred_element_type=jnp.float32,
        )
        query_parts.append(
            jnp.einsum("hqk,khe->qhe", d_scores, keys, preferred_element_type=jnp.float32)
        )
        d_keys = d_keys + jnp.einsum(
            "hqk,qhe->khe",
            d_scores,
            query[block_start:block_end],
            preferred_element_type=jnp.float32,
        )
    return (jnp.concatenate(query_parts, axis=0), d_keys, d_values)


class Grid:
    def __init__(self, sizes):
        dp, fsdp = sizes
        self.total = dp * fsdp
        self.low = fsdp.bit_length() - 1
        self.bits = self.total.bit_length() - 1
        self.core = self.low
        self.x = self.low + 1
        self.y = self.low - 1
        stages = [(self.core, self.core), (self.x, self.y), (self.y, self.x)]
        stages += [(b, b) for b in range(self.low - 2, -1, -1)]
        stages += [(b, b) for b in range(self.x + 1, self.bits)]
        self.stages = stages

    def here(self):
        return lax.axis_index("dp") * (1 << self.low) + lax.axis_index("fsdp")

    def pairs(self, stage):
        found = []
        for device in range(self.total):
            bit = stage[(device >> self.core) & 1]
            found.append((device, device ^ (1 << bit)))
        return found

    def swap(self, value, stage):
        return lax.ppermute(value, AXES, self.pairs(stage))

    def plan(self, step):
        here = self.here()
        core = (here >> self.core) & 1
        chosen = []
        for which in (0, 1):
            bit = self.stages[step][which]
            gone = [s[which] for s in self.stages[:step]]
            chosen.append((bit - sum(1 for g in gone if g < bit), (here >> bit) & 1))
        place = jnp.where(core == 0, chosen[0][0], chosen[1][0])
        value = jnp.where(core == 0, chosen[0][1], chosen[1][1])
        return jnp.stack([place, value]).astype(jnp.int32)


def insert_bit(index, place, value):
    low = index & ((1 << place) - 1)
    return ((index >> place) << (place + 1)) | (value << place) | low


def split_kernel(plan, own_keep, own_send, keep, send):
    keep[...] = own_keep[...]
    send[...] = own_send[...]


def join_kernel(plan, own_keep, own_send, come_keep, come_send, keep, send):
    keep[...] = (own_keep[...].astype(jnp.float32) + come_keep[...].astype(jnp.float32)).astype(keep.dtype)
    send[...] = (own_send[...].astype(jnp.float32) + come_send[...].astype(jnp.float32)).astype(send.dtype)


def last_kernel(own, come, out):
    out[...] = own[...].astype(jnp.float32) + come[...].astype(jnp.float32)


def halves(plan, own, come):
    blocks, rows, columns = own.shape
    shape = jax.ShapeDtypeStruct((blocks // 2, rows, columns), own.dtype)
    keep_map = lambda i, plan: (insert_bit(i, plan[0], plan[1]), 0, 0)
    send_map = lambda i, plan: (insert_bit(i, plan[0], 1 - plan[1]), 0, 0)
    block = (1, rows, columns)
    taken = [own, own] if come is None else [own, own, come, come]
    maps = [keep_map, send_map] * (len(taken) // 2)
    cost = pl.CostEstimate(flops=own.size, transcendentals=0, bytes_accessed=len(taken) * own.size * 2)
    return pl.pallas_call(
        split_kernel if come is None else join_kernel,
        grid_spec=pltpu.PrefetchScalarGridSpec(
            num_scalar_prefetch=1,
            grid=(blocks // 2,),
            in_specs=[pl.BlockSpec(block, m) for m in maps],
            out_specs=[pl.BlockSpec(block, lambda i, plan: (i, 0, 0))] * 2,
        ),
        out_shape=(shape, shape),
        cost_estimate=cost,
    )(plan, *taken)


def scatter_sum(grid, value):
    rows = value.shape[0] // grid.total
    held = value.reshape(grid.total, rows, value.shape[1])
    come = None
    for step, stage in enumerate(grid.stages):
        keep, send = halves(grid.plan(step), held, come)
        come = grid.swap(send, stage)
        held = keep
    out = pl.pallas_call(
        last_kernel,
        out_shape=jax.ShapeDtypeStruct(held.shape, jnp.float32),
        cost_estimate=pl.CostEstimate(flops=held.size, transcendentals=0, bytes_accessed=8 * held.size),
    )(held, come)
    return out.reshape(rows, value.shape[1])


def gather_small(grid, value):
    here = grid.here()
    held = value[None]
    for bit in range(grid.bits):
        come = grid.swap(held, (bit, bit))
        mine = (here >> bit) & 1
        held = jnp.where(mine == 0, jnp.concatenate([held, come]), jnp.concatenate([come, held]))
    return held


def scatter_small(grid, value):
    here = grid.here()
    held = value
    for bit in range(grid.bits - 1, -1, -1):
        mine = (here >> bit) & 1
        half = held.shape[0] // 2
        upper = mine == 1
        send = jnp.where(upper, held[:half], held[half:])
        keep = jnp.where(upper, held[half:], held[:half])
        held = keep + grid.swap(send, (bit, bit))
    return held


def body(
    grid,
    hidden_in,
    segment_ids,
    out_grad,
    norm1_gain,
    norm1_bias,
    norm2_gain,
    norm2_bias,
    qkv_weight,
    qkv_bias,
    proj_weight,
    proj_bias,
    up_weight,
    up_bias,
    down_weight,
    down_bias,
):
    small = (norm1_gain, norm1_bias, norm2_gain, norm2_bias, qkv_bias, proj_bias, up_bias, down_bias)
    widths = [entry.shape[0] for entry in small]
    packed = jnp.concatenate(small)
    packed = jnp.pad(packed, (0, -packed.shape[0] % 128))
    spread = gather_small(grid, packed)
    pieces, at = [], 0
    for width in widths:
        pieces.append(spread[:, at : at + width].reshape(-1))
        at += width
    gain_one, shift_one, gain_two, shift_two, b_qkv, b_proj, b_up, b_down = pieces
    w_qkv, w_proj, w_up, w_down = (
        lax.all_gather(entry, AXES, axis=0, tiled=True) for entry in (qkv_weight, proj_weight, up_weight, down_weight)
    )
    seq_count, length, model_width = hidden_in.shape
    row_count = seq_count * length
    scale = HEAD ** (-0.5)
    flat = hidden_in.reshape(row_count, model_width).astype(jnp.float32)
    grad_rows = out_grad.reshape(row_count, model_width)
    valid = (segment_ids != DOCS - 1).astype(jnp.float32).reshape(row_count, 1)
    cosine, sine = angles(segment_ids)
    normed_one = (
        normed(flat, gain_one.astype(jnp.float32)) + shift_one.astype(jnp.float32)
    ).astype(jnp.bfloat16)
    mixed = jnp.dot(normed_one, w_qkv, preferred_element_type=jnp.float32) + b_qkv.astype(
        jnp.float32
    )
    raw = mixed.reshape(seq_count, length, 3, HEADS, HEAD)
    raw_query = raw[:, :, 0]
    raw_keys = raw[:, :, 1]

    def rope_pair(first_part, second_part):
        return (rotate(first_part, cosine, sine), rotate(second_part, cosine, sine))

    (turned_query, turned_keys), rope_pull = jax.vjp(rope_pair, raw_query, raw_keys)
    query = (turned_query * scale).astype(jnp.bfloat16)
    keys = turned_keys.astype(jnp.bfloat16)
    values = raw[:, :, 2].astype(jnp.bfloat16)
    heads_out, log_sums = lax.map(attend_forward, (query, keys, values, segment_ids))
    attended = (heads_out.reshape(row_count, model_width) * valid).astype(jnp.bfloat16)
    projected = jnp.dot(attended, w_proj, preferred_element_type=jnp.float32) + b_proj.astype(
        jnp.float32
    )
    normed_two = (
        normed(flat, gain_two.astype(jnp.float32)) + shift_two.astype(jnp.float32)
    ).astype(jnp.bfloat16)
    before = jnp.dot(normed_two, w_up, preferred_element_type=jnp.float32) + b_up.astype(
        jnp.float32
    )
    after = jax.nn.gelu(before, approximate=False).astype(jnp.bfloat16)
    branch = jnp.dot(after, w_down, preferred_element_type=jnp.float32) + b_down.astype(jnp.float32)
    layer_out = (
        (flat + projected + branch).astype(jnp.bfloat16).reshape(seq_count, length, model_width)
    )
    back_gain_one, back_gain_two, back_qkv, back_proj, back_up, back_down = (
        gain_one, gain_two, w_qkv, w_proj, w_up, w_down
    )
    grad_wide = grad_rows.astype(jnp.float32)
    bias_grad = jnp.sum(grad_wide, axis=0)
    grad_down = jnp.einsum("rf,rd->fd", after, grad_rows, preferred_element_type=jnp.float32)
    d_after = jnp.einsum("rd,fd->rf", grad_rows, back_down, preferred_element_type=jnp.float32)
    gelu_value, gelu_pull = jax.vjp(partial(jax.nn.gelu, approximate=False), before)
    d_before = gelu_pull(d_after)[0].astype(jnp.bfloat16)
    grad_up_bias = jnp.sum(d_before.astype(jnp.float32), axis=0)
    grad_up = jnp.einsum("rd,rf->df", normed_two, d_before, preferred_element_type=jnp.float32)
    d_normed_two = jnp.einsum("rf,df->rd", d_before, back_up, preferred_element_type=jnp.float32)
    norm_value_two, pull_two = jax.vjp(normed, flat, back_gain_two.astype(jnp.float32))
    dx_two, grad_gain_two = pull_two(d_normed_two)
    grad_shift_two = jnp.sum(d_normed_two, axis=0)
    grad_proj = jnp.einsum("rd,re->de", attended, grad_rows, preferred_element_type=jnp.float32)
    d_attended = (
        jnp.einsum("re,de->rd", grad_rows, back_proj, preferred_element_type=jnp.float32) * valid
    ).astype(jnp.bfloat16)
    d_attended = d_attended.reshape(seq_count, length, HEADS, HEAD)
    d_query, d_keys, d_values = lax.map(
        attend_backward, (query, keys, values, segment_ids, log_sums, d_attended)
    )
    d_raw_query, d_raw_keys = rope_pull((d_query * scale, d_keys))
    d_mixed = (
        jnp.stack([d_raw_query, d_raw_keys, d_values], axis=2)
        .reshape(row_count, 3 * model_width)
        .astype(jnp.bfloat16)
    )
    grad_qkv_bias = jnp.sum(d_mixed.astype(jnp.float32), axis=0)
    grad_qkv = jnp.einsum("rd,rc->dc", normed_one, d_mixed, preferred_element_type=jnp.float32)
    d_normed_one = jnp.einsum("rc,dc->rd", d_mixed, back_qkv, preferred_element_type=jnp.float32)
    norm_value_one, pull_one = jax.vjp(normed, flat, back_gain_one.astype(jnp.float32))
    dx_one, grad_gain_one = pull_one(d_normed_one)
    grad_shift_one = jnp.sum(d_normed_one, axis=0)
    input_grad = (
        (grad_wide + dx_one + dx_two).astype(jnp.bfloat16).reshape(seq_count, length, model_width)
    )
    n = grid.total
    sums = (grad_gain_one, grad_shift_one, grad_gain_two, grad_shift_two, grad_qkv_bias, bias_grad, grad_up_bias)
    vectors = jnp.concatenate([entry.reshape(n, -1) for entry in sums], axis=1)
    vectors = jnp.pad(vectors, ((0, 0), (0, -vectors.shape[1] % 128)))
    total = scatter_small(grid, vectors)
    outs, at = [], 0
    for entry in sums:
        width = entry.shape[0] // n
        outs.append(total[0, at : at + width])
        at += width
    low = [scatter_sum(grid, entry.astype(jnp.bfloat16)) for entry in (grad_qkv, grad_proj, grad_up, grad_down)]
    return (
        layer_out,
        input_grad,
        outs[0],
        outs[1],
        outs[2],
        outs[3],
        low[0],
        outs[4],
        low[1],
        outs[5],
        low[2],
        outs[6],
        low[3],
        outs[5],
    )


def solution(mesh):
    in_specs = (
        P(("dp", "fsdp"), None, None),
        P(("dp", "fsdp"), None),
        P(("dp", "fsdp"), None, None),
        P(("dp", "fsdp")),
        P(("dp", "fsdp")),
        P(("dp", "fsdp")),
        P(("dp", "fsdp")),
        P(("dp", "fsdp"), None),
        P(("dp", "fsdp")),
        P(("dp", "fsdp"), None),
        P(("dp", "fsdp")),
        P(("dp", "fsdp"), None),
        P(("dp", "fsdp")),
        P(("dp", "fsdp"), None),
        P(("dp", "fsdp")),
    )
    out_specs = (
        P(("dp", "fsdp"), None, None),
        P(("dp", "fsdp"), None, None),
        P(("dp", "fsdp")),
        P(("dp", "fsdp")),
        P(("dp", "fsdp")),
        P(("dp", "fsdp")),
        P(("dp", "fsdp"), None),
        P(("dp", "fsdp")),
        P(("dp", "fsdp"), None),
        P(("dp", "fsdp")),
        P(("dp", "fsdp"), None),
        P(("dp", "fsdp")),
        P(("dp", "fsdp"), None),
        P(("dp", "fsdp")),
    )
    grid = Grid((mesh.shape["dp"], mesh.shape["fsdp"]))
    return jax.shard_map(partial(body, grid), mesh=mesh, in_specs=in_specs, out_specs=out_specs, check_vma=False)
```

```python
from functools import partial

import jax
import jax.numpy as jnp
from jax import lax
from jax.experimental import pallas as pl
from jax.experimental.pallas import tpu as pltpu
from jax.sharding import Mesh
from jax.sharding import PartitionSpec as P

AXES = ("dp", "fsdp")

HEADS = 16
HEAD = 64
ROT = 16
DOCS = 8


norm_eps = 1e-05
masked_score = -1e30


def normed(values, gain):
    center = values - jnp.mean(values, axis=-1, keepdims=True)
    spread = jnp.mean(center * center, axis=-1, keepdims=True)
    return center * lax.rsqrt(spread + norm_eps) * gain


def rotate(part, cosine, sine):
    half_rot = ROT // 2
    first = part[..., :half_rot]
    second = part[..., half_rot:ROT]
    cos_wide = cosine[..., None, :]
    sin_wide = sine[..., None, :]
    return jnp.concatenate(
        [
            first * cos_wide - second * sin_wide,
            second * cos_wide + first * sin_wide,
            part[..., ROT:],
        ],
        axis=-1,
    )


def angles(segments):
    last_axis = segments.ndim - 1
    position = lax.broadcasted_iota(jnp.int32, segments.shape, last_axis)
    change = jnp.concatenate(
        [jnp.ones(segments.shape[:-1] + (1,), jnp.bool_), segments[..., 1:] != segments[..., :-1]],
        axis=-1,
    )
    first_index = lax.cummax(jnp.where(change, position, jnp.zeros_like(position)), axis=last_axis)
    place = (position - first_index).astype(jnp.float32)
    freqs = 10000.0 ** (-(jnp.arange(ROT // 2) * 2).astype(jnp.float32) / ROT)
    theta = place[..., None] * freqs
    return (jnp.cos(theta), jnp.sin(theta))


def block_mask(segments, block_start, block_rows):
    length = segments.shape[0]
    query_pos = block_start + lax.broadcasted_iota(jnp.int32, (block_rows, length), 0)
    key_pos = lax.broadcasted_iota(jnp.int32, (block_rows, length), 1)
    same = segments[block_start : block_start + block_rows][:, None] == segments[None, :]
    return ((key_pos <= query_pos) & same)[None]


def attend_forward(pieces):
    query, keys, values, segments = pieces
    length = segments.shape[0]
    block_rows = min(512, length)
    outputs = []
    log_sums = []
    for block_start in range(0, length, block_rows):
        allowed = block_mask(segments, block_start, block_rows)
        scores = jnp.einsum(
            "qhe,khe->hqk",
            query[block_start : block_start + block_rows],
            keys,
            preferred_element_type=jnp.float32,
        )
        scores = jnp.where(allowed, scores, masked_score)
        row_max = jnp.max(scores, axis=-1, keepdims=True)
        exponent = jnp.exp(scores - row_max)
        total = jnp.sum(exponent, axis=-1, keepdims=True)
        weights = (exponent / total).astype(jnp.bfloat16)
        outputs.append(
            jnp.einsum("hqk,khe->qhe", weights, values, preferred_element_type=jnp.float32)
        )
        log_sums.append(row_max + jnp.log(total))
    return (jnp.concatenate(outputs, axis=0), jnp.concatenate(log_sums, axis=1))


def attend_backward(pieces):
    query, keys, values, segments, log_sums, d_out = pieces
    length = segments.shape[0]
    block_rows = min(512, length)
    query_parts = []
    d_keys = jnp.zeros(keys.shape, jnp.float32)
    d_values = jnp.zeros(values.shape, jnp.float32)
    for block_start in range(0, length, block_rows):
        block_end = block_start + block_rows
        allowed = block_mask(segments, block_start, block_rows)
        scores = jnp.einsum(
            "qhe,khe->hqk", query[block_start:block_end], keys, preferred_element_type=jnp.float32
        )
        scores = jnp.where(allowed, scores, masked_score)
        probs = jnp.exp(scores - log_sums[:, block_start:block_end])
        d_probs = jnp.einsum(
            "qhe,khe->hqk", d_out[block_start:block_end], values, preferred_element_type=jnp.float32
        )
        inner = jnp.sum(d_probs * probs, axis=-1, keepdims=True)
        d_scores = (probs * (d_probs - inner)).astype(jnp.bfloat16)
        d_values = d_values + jnp.einsum(
            "hqk,qhe->khe",
            probs.astype(jnp.bfloat16),
            d_out[block_start:block_end],
            preferred_element_type=jnp.float32,
        )
        query_parts.append(
            jnp.einsum("hqk,khe->qhe", d_scores, keys, preferred_element_type=jnp.float32)
        )
        d_keys = d_keys + jnp.einsum(
            "hqk,qhe->khe",
            d_scores,
            query[block_start:block_end],
            preferred_element_type=jnp.float32,
        )
    return (jnp.concatenate(query_parts, axis=0), d_keys, d_values)


class Grid:
    def __init__(self, sizes):
        dp, fsdp = sizes
        self.total = dp * fsdp
        self.low = fsdp.bit_length() - 1
        self.bits = self.total.bit_length() - 1
        self.core = self.low
        self.x = self.low + 1
        self.y = self.low - 1
        stages = [(self.core, self.core), (self.x, self.y), (self.y, self.x)]
        stages += [(b, b) for b in range(self.low - 2, -1, -1)]
        stages += [(b, b) for b in range(self.x + 1, self.bits)]
        self.stages = stages

    def here(self):
        return lax.axis_index("dp") * (1 << self.low) + lax.axis_index("fsdp")

    def pairs(self, stage):
        found = []
        for device in range(self.total):
            bit = stage[(device >> self.core) & 1]
            found.append((device, device ^ (1 << bit)))
        return found

    def swap(self, value, stage):
        return lax.ppermute(value, AXES, self.pairs(stage))

    def plan(self, step):
        here = self.here()
        core = (here >> self.core) & 1
        chosen = []
        for which in (0, 1):
            bit = self.stages[step][which]
            gone = [s[which] for s in self.stages[:step]]
            chosen.append((bit - sum(1 for g in gone if g < bit), (here >> bit) & 1))
        place = jnp.where(core == 0, chosen[0][0], chosen[1][0])
        value = jnp.where(core == 0, chosen[0][1], chosen[1][1])
        return jnp.stack([place, value]).astype(jnp.int32)


def insert_bit(index, place, value):
    low = index & ((1 << place) - 1)
    return ((index >> place) << (place + 1)) | (value << place) | low


def split_kernel(plan, own_keep, own_send, keep, send):
    keep[...] = own_keep[...]
    send[...] = own_send[...]


def join_kernel(plan, own_keep, own_send, come_keep, come_send, keep, send):
    keep[...] = (own_keep[...].astype(jnp.float32) + come_keep[...].astype(jnp.float32)).astype(keep.dtype)
    send[...] = (own_send[...].astype(jnp.float32) + come_send[...].astype(jnp.float32)).astype(send.dtype)


def last_kernel(own, come, out):
    out[...] = own[...].astype(jnp.float32) + come[...].astype(jnp.float32)


def halves(plan, own, come):
    blocks, rows, columns = own.shape
    shape = jax.ShapeDtypeStruct((blocks // 2, rows, columns), own.dtype)
    keep_map = lambda i, plan: (insert_bit(i, plan[0], plan[1]), 0, 0)
    send_map = lambda i, plan: (insert_bit(i, plan[0], 1 - plan[1]), 0, 0)
    block = (1, rows, columns)
    taken = [own, own] if come is None else [own, own, come, come]
    maps = [keep_map, send_map] * (len(taken) // 2)
    cost = pl.CostEstimate(flops=own.size, transcendentals=0, bytes_accessed=len(taken) * own.size * 2)
    return pl.pallas_call(
        split_kernel if come is None else join_kernel,
        grid_spec=pltpu.PrefetchScalarGridSpec(
            num_scalar_prefetch=1,
            grid=(blocks // 2,),
            in_specs=[pl.BlockSpec(block, m) for m in maps],
            out_specs=[pl.BlockSpec(block, lambda i, plan: (i, 0, 0))] * 2,
        ),
        out_shape=(shape, shape),
        cost_estimate=cost,
    )(plan, *taken)


def scatter_sum(grid, value):
    rows = value.shape[0] // grid.total
    held = value.reshape(grid.total, rows, value.shape[1])
    come = None
    for step, stage in enumerate(grid.stages):
        keep, send = halves(grid.plan(step), held, come)
        come = grid.swap(send, stage)
        held = keep
    out = pl.pallas_call(
        last_kernel,
        out_shape=jax.ShapeDtypeStruct(held.shape, jnp.float32),
        cost_estimate=pl.CostEstimate(flops=held.size, transcendentals=0, bytes_accessed=8 * held.size),
    )(held, come)
    return out.reshape(rows, value.shape[1])


def gather_small(grid, value):
    here = grid.here()
    held = value[None]
    for bit in range(grid.bits):
        come = grid.swap(held, (bit, bit))
        mine = (here >> bit) & 1
        held = jnp.where(mine == 0, jnp.concatenate([held, come]), jnp.concatenate([come, held]))
    return held


def scatter_small(grid, value):
    here = grid.here()
    held = value
    for bit in range(grid.bits - 1, -1, -1):
        mine = (here >> bit) & 1
        half = held.shape[0] // 2
        upper = mine == 1
        send = jnp.where(upper, held[:half], held[half:])
        keep = jnp.where(upper, held[half:], held[:half])
        held = keep + grid.swap(send, (bit, bit))
    return held


def body(
    grid,
    hidden_in,
    segment_ids,
    out_grad,
    norm1_gain,
    norm1_bias,
    norm2_gain,
    norm2_bias,
    qkv_weight,
    qkv_bias,
    proj_weight,
    proj_bias,
    up_weight,
    up_bias,
    down_weight,
    down_bias,
):
    small = (norm1_gain, norm1_bias, norm2_gain, norm2_bias, qkv_bias, proj_bias, up_bias, down_bias)
    widths = [entry.shape[0] for entry in small]
    packed = jnp.concatenate(small)
    packed = jnp.pad(packed, (0, -packed.shape[0] % 128))
    spread = gather_small(grid, packed)
    pieces, at = [], 0
    for width in widths:
        pieces.append(spread[:, at : at + width].reshape(-1))
        at += width
    gain_one, shift_one, gain_two, shift_two, b_qkv, b_proj, b_up, b_down = pieces
    w_qkv, w_proj, w_up, w_down = (
        lax.all_gather(entry, AXES, axis=0, tiled=True) for entry in (qkv_weight, proj_weight, up_weight, down_weight)
    )
    seq_count, length, model_width = hidden_in.shape
    row_count = seq_count * length
    scale = HEAD ** (-0.5)
    flat = hidden_in.reshape(row_count, model_width).astype(jnp.float32)
    grad_rows = out_grad.reshape(row_count, model_width)
    valid = (segment_ids != DOCS - 1).astype(jnp.float32).reshape(row_count, 1)
    cosine, sine = angles(segment_ids)
    normed_one = (
        normed(flat, gain_one.astype(jnp.float32)) + shift_one.astype(jnp.float32)
    ).astype(jnp.bfloat16)
    mixed = jnp.dot(normed_one, w_qkv, preferred_element_type=jnp.float32) + b_qkv.astype(
        jnp.float32
    )
    raw = mixed.reshape(seq_count, length, 3, HEADS, HEAD)
    raw_query = raw[:, :, 0]
    raw_keys = raw[:, :, 1]

    def rope_pair(first_part, second_part):
        return (rotate(first_part, cosine, sine), rotate(second_part, cosine, sine))

    (turned_query, turned_keys), rope_pull = jax.vjp(rope_pair, raw_query, raw_keys)
    query = (turned_query * scale).astype(jnp.bfloat16)
    keys = turned_keys.astype(jnp.bfloat16)
    values = raw[:, :, 2].astype(jnp.bfloat16)
    heads_out, log_sums = lax.map(attend_forward, (query, keys, values, segment_ids))
    attended = (heads_out.reshape(row_count, model_width) * valid).astype(jnp.bfloat16)
    projected = jnp.dot(attended, w_proj, preferred_element_type=jnp.float32) + b_proj.astype(
        jnp.float32
    )
    normed_two = (
        normed(flat, gain_two.astype(jnp.float32)) + shift_two.astype(jnp.float32)
    ).astype(jnp.bfloat16)
    before = jnp.dot(normed_two, w_up, preferred_element_type=jnp.float32) + b_up.astype(
        jnp.float32
    )
    after = jax.nn.gelu(before, approximate=False).astype(jnp.bfloat16)
    branch = jnp.dot(after, w_down, preferred_element_type=jnp.float32) + b_down.astype(jnp.float32)
    layer_out = (
        (flat + projected + branch).astype(jnp.bfloat16).reshape(seq_count, length, model_width)
    )
    back_gain_one, back_gain_two, back_qkv, back_proj, back_up, back_down = (
        gain_one, gain_two, w_qkv, w_proj, w_up, w_down
    )
    grad_wide = grad_rows.astype(jnp.float32)
    bias_grad = jnp.sum(grad_wide, axis=0)
    grad_down = jnp.einsum("rf,rd->fd", after, grad_rows, preferred_element_type=jnp.float32)
    d_after = jnp.einsum("rd,fd->rf", grad_rows, back_down, preferred_element_type=jnp.float32)
    gelu_value, gelu_pull = jax.vjp(partial(jax.nn.gelu, approximate=False), before)
    d_before = gelu_pull(d_after)[0].astype(jnp.bfloat16)
    grad_up_bias = jnp.sum(d_before.astype(jnp.float32), axis=0)
    grad_up = jnp.einsum("rd,rf->df", normed_two, d_before, preferred_element_type=jnp.float32)
    d_normed_two = jnp.einsum("rf,df->rd", d_before, back_up, preferred_element_type=jnp.float32)
    norm_value_two, pull_two = jax.vjp(normed, flat, back_gain_two.astype(jnp.float32))
    dx_two, grad_gain_two = pull_two(d_normed_two)
    grad_shift_two = jnp.sum(d_normed_two, axis=0)
    grad_proj = jnp.einsum("rd,re->de", attended, grad_rows, preferred_element_type=jnp.float32)
    d_attended = (
        jnp.einsum("re,de->rd", grad_rows, back_proj, preferred_element_type=jnp.float32) * valid
    ).astype(jnp.bfloat16)
    d_attended = d_attended.reshape(seq_count, length, HEADS, HEAD)
    d_query, d_keys, d_values = lax.map(
        attend_backward, (query, keys, values, segment_ids, log_sums, d_attended)
    )
    d_raw_query, d_raw_keys = rope_pull((d_query * scale, d_keys))
    d_mixed = (
        jnp.stack([d_raw_query, d_raw_keys, d_values], axis=2)
        .reshape(row_count, 3 * model_width)
        .astype(jnp.bfloat16)
    )
    grad_qkv_bias = jnp.sum(d_mixed.astype(jnp.float32), axis=0)
    grad_qkv = jnp.einsum("rd,rc->dc", normed_one, d_mixed, preferred_element_type=jnp.float32)
    d_normed_one = jnp.einsum("rc,dc->rd", d_mixed, back_qkv, preferred_element_type=jnp.float32)
    norm_value_one, pull_one = jax.vjp(normed, flat, back_gain_one.astype(jnp.float32))
    dx_one, grad_gain_one = pull_one(d_normed_one)
    grad_shift_one = jnp.sum(d_normed_one, axis=0)
    input_grad = (
        (grad_wide + dx_one + dx_two).astype(jnp.bfloat16).reshape(seq_count, length, model_width)
    )
    n = grid.total
    sums = (grad_gain_one, grad_shift_one, grad_gain_two, grad_shift_two, grad_qkv_bias, bias_grad, grad_up_bias)
    vectors = jnp.concatenate([entry.reshape(n, -1) for entry in sums], axis=1)
    vectors = jnp.pad(vectors, ((0, 0), (0, -vectors.shape[1] % 128)))
    total = scatter_small(grid, vectors)
    outs, at = [], 0
    for entry in sums:
        width = entry.shape[0] // n
        outs.append(total[0, at : at + width])
        at += width
    low = [scatter_sum(grid, entry.astype(jnp.bfloat16)) for entry in (grad_qkv, grad_proj, grad_up, grad_down)]
    return (
        layer_out,
        input_grad,
        outs[0],
        outs[1],
        outs[2],
        outs[3],
        low[0],
        outs[4],
        low[1],
        outs[5],
        low[2],
        outs[6],
        low[3],
        outs[5],
    )


NT = (((1,), (1,)), ((), ()))
NN = (((1,), (0,)), ((), ()))
TN = (((0,), (0,)), ((), ()))
PAIR = 2 * HEAD
ROWS = 256


def mul(left, right, dims):
    return lax.dot_general(left, right, dims, preferred_element_type=jnp.float32)


def params(**more):
    return pltpu.CompilerParams(vmem_limit_bytes=60 << 20, **more)


def cost(flops, moved, special=0):
    return pl.CostEstimate(flops=int(flops), transcendentals=int(special), bytes_accessed=int(moved))


def fixed(shape):
    return pl.BlockSpec(shape, lambda *_: (0,) * len(shape), pipeline_mode=pl.Buffered(1))


def middle_swap(value):
    quarter = (lax.broadcasted_iota(jnp.int32, value.shape, 1) % 128) // 32
    width = value.shape[1]
    up, down = pltpu.roll(value, width - 32, 1), pltpu.roll(value, 32, 1)
    return jnp.where(quarter == 1, up, jnp.where(quarter == 2, down, value))


def norm_kernel(mine, theirs, gmine, gtheirs, scales, one, two, grads):
    def work(source, cotangent):
        value = source[...].astype(jnp.float32)
        center = value - jnp.mean(value, axis=1, keepdims=True)
        spread = jnp.mean(center * center, axis=1, keepdims=True)
        hat = center * lax.rsqrt(spread + norm_eps)
        table = scales[...].astype(jnp.float32)
        one[...] = middle_swap(hat * table[0:1] + table[1:2]).astype(jnp.bfloat16)
        two[...] = middle_swap(hat * table[2:3] + table[3:4]).astype(jnp.bfloat16)
        grads[...] = cotangent[...]

    first = pl.program_id(0) == 0
    pl.when(first)(lambda: work(mine, gmine))
    pl.when(jnp.logical_not(first))(lambda: work(theirs, gtheirs))


def norms(mine, theirs, gmine, gtheirs, scales):
    length, width = mine.shape
    block = (ROWS, width)
    steps = length // ROWS
    own = pl.BlockSpec(block, lambda s, i: (jnp.where(s == 0, i, steps - 1), 0))
    other = pl.BlockSpec(block, lambda s, i: (jnp.where(s == 0, 0, i), 0))
    out = pl.BlockSpec(block, lambda s, i: (s * steps + i, 0))
    shape = jax.ShapeDtypeStruct((2 * length, width), jnp.bfloat16)
    return pl.pallas_call(
        norm_kernel,
        grid=(2, steps),
        in_specs=[own, other, own, other, fixed(scales.shape)],
        out_specs=[out] * 3,
        out_shape=[shape] * 3,
        compiler_params=params(),
        cost_estimate=cost(40 * length * width, 20 * length * width),
    )(mine, theirs, gmine, gtheirs, scales)


def turn(value, cosine, sine):
    lane = lax.broadcasted_iota(jnp.int32, value.shape, 1) % HEAD
    half = ROT // 2
    up, down = pltpu.roll(value, value.shape[1] - half, 1), pltpu.roll(value, half, 1)
    return value * cosine + jnp.where(lane < half, up, down) * sine


def project_kernel(normed, grads, weight, bias, cosine, sine, valid, out):
    part = pl.program_id(0)
    tokens = normed.shape[0]
    width = weight.shape[-1]
    held = weight[...].reshape(-1, width)
    for start in range(0, tokens, 2 * ROWS):
        rows = slice(start, start + 2 * ROWS)

        @pl.when(part < 3)
        def _():
            value = mul(normed[rows, :], held, NN) + bias[0].astype(jnp.float32)

            @pl.when(part < 2)
            def _():
                scale = jnp.where(part == 0, HEAD ** (-0.5), 1.0)
                for at in range(0, width, PAIR):
                    turned = turn(value[:, at : at + PAIR], cosine[rows, :], sine[rows, :])
                    out[0, rows, at : at + PAIR] = (turned * scale).astype(out.dtype)

            @pl.when(part == 2)
            def _():
                out[0, rows, :] = value.astype(out.dtype)

        @pl.when(part == 3)
        def _():
            pieces = weight[...].reshape(-1, 2, weight.shape[2] // 2, width)
            total = None
            for half in range(2):
                term = mul(
                    grads[rows, half * width : (half + 1) * width],
                    pieces[:, half].reshape(-1, width),
                    NT,
                )
                total = term if total is None else total + term
            out[0, rows, :] = (total * valid[rows, :]).astype(out.dtype)


def project(normed, grads, packed, bias, cosine, sine, valid):
    tokens, model = normed.shape
    chips, parts, rows, width = packed.shape
    return pl.pallas_call(
        project_kernel,
        grid=(parts,),
        in_specs=[
            fixed(normed.shape),
            fixed(grads.shape),
            pl.BlockSpec((chips, 1, rows, width), lambda p: (0, p, 0, 0)),
            pl.BlockSpec((1, 1, width), lambda p: (jnp.minimum(p, 2), 0, 0)),
            fixed(cosine.shape),
            fixed(sine.shape),
            fixed(valid.shape),
        ],
        out_specs=pl.BlockSpec((1, tokens, width), lambda p: (p, 0, 0)),
        out_shape=jax.ShapeDtypeStruct((parts, tokens, width), jnp.bfloat16),
        compiler_params=params(),
        cost_estimate=cost(7 * tokens * model * width, 40 * tokens * width),
    )(normed, grads, packed, bias, cosine, sine, valid)


def attention_kernel(
    q_ref, k_ref, v_ref, g_ref, cosine, sine, seg_row, seg_col, valid, out, d_out, mask, dk_sum, dv_sum
):
    length = q_ref.shape[1]
    blocks = length // ROWS

    @pl.when(pl.program_id(1) == 0)
    def _():
        for block in range(blocks):
            start = block * ROWS
            end = start + ROWS
            key_pos = lax.broadcasted_iota(jnp.int32, (ROWS, end), 1)
            query_pos = lax.broadcasted_iota(jnp.int32, (ROWS, end), 0) + start
            allowed = (key_pos <= query_pos) & (seg_col[start:end, :] == seg_row[0, :, :end])
            mask[start:end, :end] = jnp.where(allowed, 0.0, masked_score)

    lane = lax.broadcasted_iota(jnp.int32, (ROWS, PAIR), 1)
    for block in range(blocks - 1, -1, -1):
        start = block * ROWS
        end = start + ROWS
        rows = slice(start, end)
        keys, values = k_ref[0, :end, :], v_ref[0, :end, :]
        query, grads = q_ref[0, rows, :], g_ref[0, rows, :]
        hide = mask[rows, :end]
        pieces = []
        for head in range(2):
            mine = lane < HEAD if head == 0 else lane >= HEAD
            own_query = jnp.where(mine, query, jnp.zeros_like(query))
            own_grads = jnp.where(mine, grads, jnp.zeros_like(grads))
            scores = mul(own_query, keys, NT) + hide
            exponent = jnp.exp(scores - jnp.max(scores, axis=1, keepdims=True))
            probs = exponent * (1.0 / jnp.sum(exponent, axis=1, keepdims=True))
            low = probs.astype(jnp.bfloat16)
            mixed = mul(low, values, NN)
            d_probs = mul(own_grads, values, NT)
            inner = jnp.sum(own_grads.astype(jnp.float32) * mixed, axis=1, keepdims=True)
            d_scores = (probs * (d_probs - inner)).astype(jnp.bfloat16)
            pieces.append((mixed, mul(d_scores, keys, NN)))
            d_keys, d_values = mul(d_scores, own_query, TN), mul(low, own_grads, TN)
            if block == blocks - 1 and head == 0:
                dk_sum[:end, :] = d_keys
                dv_sum[:end, :] = d_values
            else:
                dk_sum[:end, :] += d_keys
                dv_sum[:end, :] += d_values
        mine = lane < HEAD
        out[rows, :] = (jnp.where(mine, pieces[0][0], pieces[1][0]) * valid[rows, :]).astype(out.dtype)
        d_query = turn(jnp.where(mine, pieces[0][1], pieces[1][1]), cosine[rows, :], -sine[rows, :])
        d_out[0, rows, :] = (d_query * HEAD ** (-0.5)).astype(d_out.dtype)
    d_out[1] = turn(dk_sum[...], cosine[...], -sine[...]).astype(d_out.dtype)
    d_out[2] = dv_sum[...].astype(d_out.dtype)


def attention(parts, cosine, sine, segments, valid):
    sequences, length = segments.shape
    tokens, width = parts.shape[1:]
    part = lambda p: pl.BlockSpec((1, length, PAIR), lambda s, j: (p, s, j))
    table = lambda n: pl.BlockSpec((length, n), lambda s, j: (s, 0))
    return pl.pallas_call(
        attention_kernel,
        grid=(sequences, width // PAIR),
        in_specs=[
            part(0),
            part(1),
            part(2),
            part(3),
            table(PAIR),
            table(PAIR),
            pl.BlockSpec((1, 1, length), lambda s, j: (s, 0, 0)),
            table(1),
            table(1),
        ],
        out_specs=[
            pl.BlockSpec((length, PAIR), lambda s, j: (s, j)),
            pl.BlockSpec((3, length, PAIR), lambda s, j: (0, s, j)),
        ],
        out_shape=[
            jax.ShapeDtypeStruct((tokens, width), jnp.bfloat16),
            jax.ShapeDtypeStruct((3, tokens, width), jnp.bfloat16),
        ],
        scratch_shapes=[pltpu.VMEM((length, length), jnp.float32)] + [pltpu.VMEM((length, PAIR), jnp.float32)] * 2,
        compiler_params=params(),
        cost_estimate=cost(8 * tokens * length * width * 4, 16 * tokens * width, tokens * length * width // 100),
    )(*[parts] * 4, cosine, sine, segments[:, None, :], segments.reshape(tokens, 1), valid)


def attention_grads_kernel(normed, grads, weight, d_mixed, attended, packed, d_mine, d_send, p_mine, p_send, sums, total):
    part = pl.program_id(0)
    tokens = normed.shape[0]
    half_tokens = tokens // 2
    chips, _, rows, width = weight.shape

    @pl.when(part < 3)
    def _():
        change = d_mixed[0]
        held = weight[...].reshape(-1, width)
        packed[...] = mul(normed[...], change, TN).astype(packed.dtype).reshape(packed.shape)
        sums[0] = jnp.sum(change.astype(jnp.float32), axis=0, keepdims=True)
        for start in range(0, tokens, 2 * ROWS):
            at = slice(start, start + 2 * ROWS)
            term = mul(d_mixed[0, at, :], held, NT)

            @pl.when(part == 0)
            def _():
                total[at, :] = term

            @pl.when(part == 1)
            def _():
                total[at, :] += term

            @pl.when(part == 2)
            def _():
                both = total[at, :] + term
                if start < half_tokens:
                    d_mine[at, :] = both
                else:
                    d_send[start - half_tokens : start - half_tokens + 2 * ROWS, :] = both.astype(d_send.dtype)

    @pl.when(part == 3)
    def _():
        sums[0] = jnp.zeros_like(sums[0])
        pieces = weight[...].reshape(-1, 2, rows // 2, width)
        for half in range(2):
            columns = slice(half * width, (half + 1) * width)
            change = mul(attended[...], grads[:, columns], TN).astype(packed.dtype)
            packed[:, 0, half * rows // 2 : (half + 1) * rows // 2, :] = change.reshape(chips, rows // 2, width)
            term = mul(attended[...], pieces[:, half].reshape(-1, width), NN)
            p_mine[:, columns] = term[:half_tokens]
            p_send[:, columns] = term[half_tokens:].astype(p_send.dtype)


def attention_grads(normed, grads, weights, d_mixed, attended):
    tokens, model = normed.shape
    chips, parts, rows, width = weights.shape
    wide = pl.BlockSpec((chips, 1, rows, width), lambda p: (0, p, 0, 0))
    half = (tokens // 2, model)
    mine, send = jax.ShapeDtypeStruct(half, jnp.float32), jax.ShapeDtypeStruct(half, jnp.bfloat16)
    return pl.pallas_call(
        attention_grads_kernel,
        grid=(parts,),
        in_specs=[
            fixed(normed.shape),
            fixed(grads.shape),
            wide,
            pl.BlockSpec((1, tokens, width), lambda p: (jnp.minimum(p, 2), 0, 0)),
            fixed(attended.shape),
        ],
        out_specs=[wide, fixed(half), fixed(half), fixed(half), fixed(half), pl.BlockSpec((1, 1, width), lambda p: (p, 0, 0))],
        out_shape=[
            jax.ShapeDtypeStruct(weights.shape, jnp.bfloat16),
            mine,
            send,
            mine,
            send,
            jax.ShapeDtypeStruct((parts, 1, width), jnp.float32),
        ],
        scratch_shapes=[pltpu.VMEM((tokens, model), jnp.float32)],
        compiler_params=params(),
        cost_estimate=cost(16 * tokens * model * width, 20 * tokens * model),
    )(normed, grads, weights, d_mixed, attended)


def forward_kernel(begins, ends, *refs):
    normed, grads, up, down, bias = refs[:5]
    rest = refs[5:] if begins else refs[7:]
    packed, bias_sum = rest[:2]
    step = pl.program_id(0)
    if begins:
        out_total, d_total, after, d_before = rest[2:]
    else:
        results = rest[2:6]
        after, d_before, out_total, d_total, arrived = rest[6:]
        loads = [
            pltpu.make_async_copy(source, target, arrived.at[n])
            for n, (source, target) in enumerate(zip(refs[5:7], (out_total, d_total)))
        ]

        @pl.when(step == 0)
        def _():
            for load in loads:
                load.start()

    steps = pl.num_programs(0)
    tokens = normed.shape[0]
    half_tokens = tokens // 2
    chips, _, rows, width = up.shape

    def add(total, at, columns, term):
        if begins:

            @pl.when(step == 0)
            def _():
                total[at, columns] = term

            @pl.when(step > 0)
            def _():
                total[at, columns] += term
        else:
            total[at, columns] += term

    held_up = up[...].reshape(-1, width)
    pieces = down[...].reshape(down.shape[0], 2, -1, width)
    held_down = [pieces[:, half].reshape(-1, width) for half in range(2)]
    offset = bias[0].astype(jnp.float32)
    bias_total = jnp.zeros_like(offset)
    for start in range(0, tokens, ROWS):
        at = slice(start, start + ROWS)
        before = mul(normed[at, :], held_up, NN) + offset
        change = mul(grads[at, :width], held_down[0], NT) + mul(grads[at, width:], held_down[1], NT)
        share = 0.5 + 0.5 * lax.erf(before * 0.7071067811865476)
        density = jnp.exp(-0.5 * before * before) * 0.3989422804014327
        after[at, :] = (before * share).astype(after.dtype)
        low = (change * (share + before * density)).astype(d_before.dtype)
        d_before[at, :] = low
        bias_total += jnp.sum(low.astype(jnp.float32), axis=0, keepdims=True)
    bias_sum[0] = bias_total
    if not begins:

        @pl.when(step == 0)
        def _():
            for load in loads:
                load.wait()

    for start in range(0, tokens, ROWS):
        at = slice(start, start + ROWS)
        for half in range(2):
            columns = slice(half * width, (half + 1) * width)
            term = mul(after[at, :], held_down[half], NN)

            add(out_total, at, columns, term)
        add(d_total, at, slice(None), mul(d_before[at, :], held_up, NT))

    change = mul(normed[...], d_before[...], TN).astype(packed.dtype)
    quads = chips // 4
    for chip in range(chips):
        z, place = chip // 4, chip % 4
        start = (z // 2) * steps * rows + step * rows
        packed[place * 2 + z % 2, pl.ds(pl.multiple_of(start, rows), rows), :] = change[chip * rows : (chip + 1) * rows]
    below = down.shape[1] * rows // 2
    for half in range(2):
        change = mul(after[...], grads[:, half * width : (half + 1) * width], TN).astype(packed.dtype)
        start = quads // 2 * steps * rows + half * below
        for place in range(4):
            packed[place * 2 + step, start : start + below, :] = change[place * below : (place + 1) * below]

    if ends:

        @pl.when(step == steps - 1)
        def _():
            results[0][...] = out_total[:half_tokens, :]
            results[1][...] = out_total[half_tokens:, :].astype(jnp.bfloat16)
            results[2][...] = d_total[:half_tokens, :]
            results[3][...] = d_total[half_tokens:, :].astype(jnp.bfloat16)


def forward_chunk(which, chunks, normed, grads, weights, bias, sums):
    tokens, model = normed.shape
    chips, parts, rows, width = weights.shape
    steps = parts // 2 // chunks
    begins, ends = which == 0, which == chunks - 1
    half, whole = (tokens // 2, model), (tokens, model)
    first = which * steps
    in_specs = [
        fixed(whole),
        fixed(whole),
        pl.BlockSpec((chips, 1, rows, width), lambda i: (0, first + i, 0, 0)),
        pl.BlockSpec((4, parts // 2, rows, width), lambda i: (first + i, 1, 0, 0)),
        pl.BlockSpec((1, 1, width), lambda i: (first + i, 0, 0)),
    ] + ([] if begins else [pl.BlockSpec(memory_space=pl.ANY)] * 2)
    blocks = (8, chips * parts * rows // 2 // chunks // 4, width)
    mine, send = jax.ShapeDtypeStruct(half, jnp.float32), jax.ShapeDtypeStruct(half, jnp.bfloat16)
    results = [mine, send, mine, send] if ends else [jax.ShapeDtypeStruct(whole, jnp.float32)] * 2
    return pl.pallas_call(
        partial(forward_kernel, begins, ends),
        grid=(steps,),
        in_specs=in_specs,
        out_specs=[fixed(blocks), pl.BlockSpec((1, 1, width), lambda i: (i, 0, 0))] + [fixed(r.shape) for r in results],
        out_shape=[jax.ShapeDtypeStruct(blocks, jnp.bfloat16), jax.ShapeDtypeStruct((steps, 1, width), jnp.float32)] + results,
        scratch_shapes=[pltpu.VMEM((tokens, width), jnp.bfloat16)] * 2
        + ([] if begins else [pltpu.VMEM(whole, jnp.float32)] * 2 + [pltpu.SemaphoreType.DMA((2,))]),
        compiler_params=params(),
        cost_estimate=cost(12 * steps * tokens * model * width, 40 * tokens * model, 2 * steps * tokens * width),
    )(normed, grads, weights, weights, bias, *([] if begins else sums))


def finish_kernel(
    hidden, grads, d1a, d1b, d2a, d2b, pa, pb, fa, fb, scales, layer_out, input_grad, sums
):
    value = hidden[...].astype(jnp.float32)
    cotangent = grads[...].astype(jnp.float32)
    table = scales[...].astype(jnp.float32)
    both = pa[...] + pb[...].astype(jnp.float32) + table[2:3]
    both += fa[...] + fb[...].astype(jnp.float32) + table[3:4]
    layer_out[...] = (value + both).astype(layer_out.dtype)
    center = value - jnp.mean(value, axis=1, keepdims=True)
    scale = lax.rsqrt(jnp.mean(center * center, axis=1, keepdims=True) + norm_eps)
    hat = center * scale
    one = middle_swap(d1a[...] + d1b[...].astype(jnp.float32))
    two = middle_swap(d2a[...] + d2b[...].astype(jnp.float32))
    gained = one * table[0:1] + two * table[1:2]
    mean = jnp.mean(gained, axis=1, keepdims=True)
    slope = jnp.mean(gained * hat, axis=1, keepdims=True)
    input_grad[...] = (cotangent + (gained - mean - hat * slope) * scale).astype(input_grad.dtype)

    @pl.when(pl.program_id(0) == 0)
    def _():
        sums[...] = jnp.zeros_like(sums)

    for row, column in enumerate((one * hat, one, two * hat, two, cotangent)):
        sums[row : row + 1, :] += jnp.sum(column, axis=0, keepdims=True)


def finish(hidden, grads, pieces, scales):
    length, width = hidden.shape
    block = pl.BlockSpec((ROWS, width), lambda i: (i, 0))
    shape = jax.ShapeDtypeStruct(hidden.shape, jnp.bfloat16)
    return pl.pallas_call(
        finish_kernel,
        grid=(length // ROWS,),
        in_specs=[block] * 10 + [fixed(scales.shape)],
        out_specs=[block, block, pl.BlockSpec((8, width), lambda i: (0, 0))],
        out_shape=[shape, shape, jax.ShapeDtypeStruct((8, width), jnp.float32)],
        compiler_params=params(),
        cost_estimate=cost(60 * length * width, 32 * length * width),
    )(hidden, grads, *pieces, scales)


BITS = {"y": 0, "core": 1, "x": 2, "z_low": 3, "z_high": 4}
SPLIT = ("zx", "core", "y")


class Pairs:
    def __init__(self, total):
        self.total = total

    def here(self):
        y = lax.axis_size("y")
        return (lax.axis_index("zx") * 2 + lax.axis_index("core")) * y + lax.axis_index("y")

    def bit(self, name):
        return (self.here() >> BITS[name]) & 1

    def swap(self, value, names):
        moves = []
        for device in range(self.total):
            name = names[(device >> BITS["core"]) & 1]
            moves.append((device, device ^ (1 << BITS[name])))
        return lax.ppermute(value, SPLIT, moves)

    def plan(self, names, order, gone):
        places, values = [], []
        for which in (0, 1):
            left = [n for n in order if n not in [g[which] for g in gone]]
            places.append(len(left) - 1 - left.index(names[which]))
            values.append(self.bit(names[which]))
        first = self.bit("core") == 0
        return jnp.stack([jnp.where(first, *places), jnp.where(first, *values)]).astype(jnp.int32)

    def scatter(self, held, order, stages):
        come, gone = None, []
        for names in stages:
            keep, send = halves(self.plan(names, order, gone), held, come)
            come = self.swap(send, names)
            held = keep
            gone.append(names)
        return held, come


PLANE = (("x", "y"), ("y", "x"))


def add_up(held, come):
    return held.astype(jnp.float32) + come.astype(jnp.float32)


def wide_angles(segments):
    cosine, sine = angles(segments)
    tail = cosine.shape[:-1] + (HEAD - ROT,)
    cosine = jnp.concatenate([cosine, cosine, jnp.ones(tail, jnp.float32)], axis=-1)
    sine = jnp.concatenate([-sine, sine, jnp.zeros(tail, jnp.float32)], axis=-1)
    return [jnp.concatenate([t, t], axis=-1).reshape(-1, PAIR) for t in (cosine, sine)]


def paired_body(
    pairs,
    hidden_in,
    segment_ids,
    out_grad,
    norm1_gain,
    norm1_bias,
    norm2_gain,
    norm2_bias,
    qkv_weight,
    qkv_bias,
    proj_weight,
    proj_bias,
    up_weight,
    up_bias,
    down_weight,
    down_bias,
):
    core = lax.axis_index("core")
    cores = ("core", "core")
    heads, model = HEADS // 2, qkv_weight.shape[1] // 3
    rows, width = qkv_weight.shape[0], heads * HEAD
    hidden, grads = hidden_in[0], out_grad[0]
    length = hidden.shape[0]

    def columns(which):
        taken = qkv_weight.reshape(rows, 3, heads, 2, HEAD)
        taken = lax.dynamic_index_in_dim(taken, which, 3, keepdims=False).reshape(rows, 3 * width)
        more = up_weight.reshape(rows, heads, 2, -1)
        more = lax.dynamic_index_in_dim(more, which, 2, keepdims=False).reshape(rows, -1)
        return jnp.concatenate([taken, more], axis=1)

    theirs = pairs.swap(columns(1 - core), cores)
    mine = columns(core)
    both = jnp.where(core == 0, jnp.stack([mine, theirs]), jnp.stack([theirs, mine]))
    both = both.reshape(2 * rows, -1, width).transpose(1, 0, 2)
    low_proj = proj_weight.reshape(rows, 2, width).transpose(1, 0, 2).reshape(1, 2 * rows, width)
    low_down = down_weight.reshape(-1, 2, width).transpose(1, 0, 2).reshape(-1, 2 * rows, width)
    packed_attention = jnp.concatenate([both[:3], low_proj])
    packed_forward = jnp.concatenate([both[3:], low_down])
    w_attention = lax.all_gather(packed_attention.reshape(-1, width), ("zx", "y"), axis=0, tiled=True)
    w_attention = w_attention.reshape((-1,) + packed_attention.shape)
    w_forward = lax.all_gather(packed_forward.reshape(-1, width), ("zx", "y"), axis=0, tiled=True)
    w_forward = w_forward.reshape((-1,) + packed_forward.shape)

    small = (norm1_gain, norm1_bias, norm2_gain, norm2_bias, qkv_bias, proj_bias, up_bias, down_bias)
    sizes = [entry.shape[0] for entry in small]
    line = jnp.concatenate(small)
    line = jnp.pad(line, (0, -line.shape[0] % 128))[None]
    for name in BITS:
        come = pairs.swap(line, (name, name))
        line = jnp.where(pairs.bit(name) == 0, jnp.concatenate([line, come]), jnp.concatenate([come, line]))
    spread, at = [], 0
    for size in sizes:
        spread.append(line[:, at : at + size].reshape(-1))
        at += size
    gain_one, shift_one, gain_two, shift_two, b_qkv, b_proj, b_up, b_down = spread
    own_bias = lax.dynamic_index_in_dim(b_qkv.reshape(3, heads, 2, HEAD), core, 2, keepdims=False).reshape(3, 1, width)
    own_up_bias = lax.dynamic_index_in_dim(b_up.reshape(heads, 2, -1), core, 1, keepdims=False).reshape(-1, 1, width)

    other, other_grads = pairs.swap(hidden, cores), pairs.swap(grads, cores)
    other_ids = pairs.swap(segment_ids, cores)
    segments = jnp.concatenate([segment_ids, other_ids])
    cosine, sine = wide_angles(segments)
    valid = (segments != DOCS - 1).astype(jnp.float32).reshape(-1, 1)
    normed_one, normed_two, both_grads = norms(
        hidden, other, grads, other_grads, jnp.stack([gain_one, shift_one, gain_two, shift_two])
    )

    parts = project(normed_one, both_grads, w_attention, own_bias, cosine, sine, valid)
    attended, d_mixed = attention(parts, cosine, sine, segments, valid)
    packed, d1_mine, d1_send, p_mine, p_send, qkv_sums = attention_grads(
        normed_one, both_grads, w_attention, d_mixed, attended
    )
    d1_come, p_come = pairs.swap(d1_send, cores), pairs.swap(p_send, cores)
    held, come = pairs.scatter(packed.reshape(packed.shape[0], -1, width), ("z_high", "z_low", "x", "y"),
                               PLANE + (("z_low", "z_low"), ("z_high", "z_high")))
    own = add_up(held, come).reshape(4, 2, rows, width)
    low_qkv, grad_proj = own[:3], own[3]

    totals, kept, up_sums = None, [], []
    for which in range(2):
        blocks, sums, *totals = forward_chunk(which, 2, normed_two, both_grads, w_forward, own_up_bias, totals)
        up_sums.append(sums)
        held, come = pairs.scatter(blocks, ("x", "y", "z_low"), PLANE + (("z_low", "z_low"),))
        kept.append(add_up(held, come).astype(jnp.bfloat16)[0])
    f_mine, f_send, d2_mine, d2_send = totals
    f_come, d2_come = pairs.swap(f_send, cores), pairs.swap(d2_send, cores)
    above = kept[0].shape[0] // 2
    ups = jnp.stack([k[:above].reshape(2, -1, width) for k in kept])
    downs = jnp.stack([k[above:] for k in kept])
    high = pairs.bit("z_high")
    pick = lambda value, axis, which: lax.dynamic_index_in_dim(value, which, axis, keepdims=False)
    send = jnp.concatenate([pick(ups, 1, 1 - high).reshape(-1, width), pick(downs, 0, 1 - high)])
    stay = jnp.concatenate([pick(ups, 1, high).reshape(-1, width), pick(downs, 0, high)])
    own = add_up(stay, pairs.swap(send, ("z_high", "z_high")))
    low_up = own[: 2 * above // 2].reshape(-1, 2, rows, width)
    grad_down = own[above:].reshape(2, -1, width).transpose(1, 0, 2).reshape(down_weight.shape)
    grad_proj = grad_proj.transpose(1, 0, 2).reshape(proj_weight.shape)

    def rows_of(value, which):
        return lax.dynamic_index_in_dim(value, which, 1, keepdims=False)

    def interleave(value, unit):
        mine, come = rows_of(value, core), pairs.swap(rows_of(value, 1 - core), cores)
        flat = [v.transpose(1, 0, 2).reshape(rows, -1, 1, unit) for v in (mine, come)]
        joined = jnp.where(core == 0, jnp.concatenate(flat, axis=2), jnp.concatenate(flat[::-1], axis=2))
        return joined.reshape(rows, -1)

    grad_qkv = interleave(low_qkv, HEAD)
    grad_up = interleave(low_up, up_weight.shape[1] // HEADS)

    layer_out, input_grad, sums = finish(
        hidden,
        grads,
        (d1_mine, d1_come, d2_mine, d2_come, p_mine, p_come, f_mine, f_come),
        jnp.stack([gain_one, gain_two, b_proj, b_down]),
    )

    def both_cores(value, unit):
        own = value.reshape(-1, 1, unit)
        none = jnp.zeros_like(own)
        return jnp.where(core == 0, jnp.concatenate([own, none], axis=1), jnp.concatenate([none, own], axis=1)).reshape(-1)

    sum_qkv = both_cores(qkv_sums[:3].reshape(-1), HEAD)
    sum_up = both_cores(jnp.concatenate(up_sums).reshape(-1), up_weight.shape[1] // HEADS)
    entries = [sums[0], sums[1], sums[2], sums[3], sum_qkv, sums[4], sum_up]
    table = jnp.concatenate([entry.reshape(pairs.total, -1) for entry in entries], axis=1)
    table = jnp.pad(table, ((0, 0), (0, -table.shape[1] % 128)))
    for name in reversed(BITS):
        upper = pairs.bit(name) == 1
        half = table.shape[0] // 2
        send = jnp.where(upper, table[:half], table[half:])
        table = jnp.where(upper, table[half:], table[:half]) + pairs.swap(send, (name, name))
    outs, at = [], 0
    for entry in entries:
        size = entry.shape[0] // pairs.total
        outs.append(table[0, at : at + size])
        at += size
    return (
        layer_out[None],
        input_grad[None],
        outs[0],
        outs[1],
        outs[2],
        outs[3],
        grad_qkv,
        outs[4],
        grad_proj,
        outs[5],
        grad_up,
        outs[6],
        grad_down,
        outs[5],
    )


def placed(axes):
    rows, flat = P(axes, None), P(axes)
    whole = P(axes, None, None)
    inside = (whole, rows, whole) + (flat,) * 4 + (rows, flat) * 4
    outside = (whole, whole) + (flat,) * 4 + (rows, flat) * 4
    return inside, outside


def solution(mesh):
    dp, fsdp = mesh.shape["dp"], mesh.shape["fsdp"]
    if (dp, fsdp) == (16, 2):
        split = Mesh(mesh.devices.reshape(dp // 2, 2, fsdp), SPLIT)
        inside, outside = placed(SPLIT)
        step = partial(paired_body, Pairs(dp * fsdp))
        return jax.shard_map(step, mesh=split, in_specs=inside, out_specs=outside, check_vma=False)
    inside, outside = placed(AXES)
    step = partial(body, Grid((dp, fsdp)))
    return jax.shard_map(step, mesh=mesh, in_specs=inside, out_specs=outside, check_vma=False)
```

```python
from functools import partial

import jax
import jax.numpy as jnp
from jax import lax
from jax.experimental import pallas as pl
from jax.experimental.pallas import tpu as pltpu
from jax.sharding import Mesh
from jax.sharding import PartitionSpec as P

AXES = ("dp", "fsdp")

HEADS = 16
HEAD = 64
ROT = 16
DOCS = 8


norm_eps = 1e-05
masked_score = -1e30


def normed(values, gain):
    center = values - jnp.mean(values, axis=-1, keepdims=True)
    spread = jnp.mean(center * center, axis=-1, keepdims=True)
    return center * lax.rsqrt(spread + norm_eps) * gain


def rotate(part, cosine, sine):
    half_rot = ROT // 2
    first = part[..., :half_rot]
    second = part[..., half_rot:ROT]
    cos_wide = cosine[..., None, :]
    sin_wide = sine[..., None, :]
    return jnp.concatenate(
        [
            first * cos_wide - second * sin_wide,
            second * cos_wide + first * sin_wide,
            part[..., ROT:],
        ],
        axis=-1,
    )


def angles(segments):
    last_axis = segments.ndim - 1
    position = lax.broadcasted_iota(jnp.int32, segments.shape, last_axis)
    change = jnp.concatenate(
        [jnp.ones(segments.shape[:-1] + (1,), jnp.bool_), segments[..., 1:] != segments[..., :-1]],
        axis=-1,
    )
    first_index = lax.cummax(jnp.where(change, position, jnp.zeros_like(position)), axis=last_axis)
    place = (position - first_index).astype(jnp.float32)
    freqs = 10000.0 ** (-(jnp.arange(ROT // 2) * 2).astype(jnp.float32) / ROT)
    theta = place[..., None] * freqs
    return (jnp.cos(theta), jnp.sin(theta))


def block_mask(segments, block_start, block_rows):
    length = segments.shape[0]
    query_pos = block_start + lax.broadcasted_iota(jnp.int32, (block_rows, length), 0)
    key_pos = lax.broadcasted_iota(jnp.int32, (block_rows, length), 1)
    same = segments[block_start : block_start + block_rows][:, None] == segments[None, :]
    return ((key_pos <= query_pos) & same)[None]


def attend_forward(pieces):
    query, keys, values, segments = pieces
    length = segments.shape[0]
    block_rows = min(512, length)
    outputs = []
    log_sums = []
    for block_start in range(0, length, block_rows):
        allowed = block_mask(segments, block_start, block_rows)
        scores = jnp.einsum(
            "qhe,khe->hqk",
            query[block_start : block_start + block_rows],
            keys,
            preferred_element_type=jnp.float32,
        )
        scores = jnp.where(allowed, scores, masked_score)
        row_max = jnp.max(scores, axis=-1, keepdims=True)
        exponent = jnp.exp(scores - row_max)
        total = jnp.sum(exponent, axis=-1, keepdims=True)
        weights = (exponent / total).astype(jnp.bfloat16)
        outputs.append(
            jnp.einsum("hqk,khe->qhe", weights, values, preferred_element_type=jnp.float32)
        )
        log_sums.append(row_max + jnp.log(total))
    return (jnp.concatenate(outputs, axis=0), jnp.concatenate(log_sums, axis=1))


def attend_backward(pieces):
    query, keys, values, segments, log_sums, d_out = pieces
    length = segments.shape[0]
    block_rows = min(512, length)
    query_parts = []
    d_keys = jnp.zeros(keys.shape, jnp.float32)
    d_values = jnp.zeros(values.shape, jnp.float32)
    for block_start in range(0, length, block_rows):
        block_end = block_start + block_rows
        allowed = block_mask(segments, block_start, block_rows)
        scores = jnp.einsum(
            "qhe,khe->hqk", query[block_start:block_end], keys, preferred_element_type=jnp.float32
        )
        scores = jnp.where(allowed, scores, masked_score)
        probs = jnp.exp(scores - log_sums[:, block_start:block_end])
        d_probs = jnp.einsum(
            "qhe,khe->hqk", d_out[block_start:block_end], values, preferred_element_type=jnp.float32
        )
        inner = jnp.sum(d_probs * probs, axis=-1, keepdims=True)
        d_scores = (probs * (d_probs - inner)).astype(jnp.bfloat16)
        d_values = d_values + jnp.einsum(
            "hqk,qhe->khe",
            probs.astype(jnp.bfloat16),
            d_out[block_start:block_end],
            preferred_element_type=jnp.float32,
        )
        query_parts.append(
            jnp.einsum("hqk,khe->qhe", d_scores, keys, preferred_element_type=jnp.float32)
        )
        d_keys = d_keys + jnp.einsum(
            "hqk,qhe->khe",
            d_scores,
            query[block_start:block_end],
            preferred_element_type=jnp.float32,
        )
    return (jnp.concatenate(query_parts, axis=0), d_keys, d_values)


class Grid:
    def __init__(self, sizes):
        dp, fsdp = sizes
        self.total = dp * fsdp
        self.low = fsdp.bit_length() - 1
        self.bits = self.total.bit_length() - 1
        self.core = self.low
        self.x = self.low + 1
        self.y = self.low - 1
        stages = [(self.core, self.core), (self.x, self.y), (self.y, self.x)]
        stages += [(b, b) for b in range(self.low - 2, -1, -1)]
        stages += [(b, b) for b in range(self.x + 1, self.bits)]
        self.stages = stages

    def here(self):
        return lax.axis_index("dp") * (1 << self.low) + lax.axis_index("fsdp")

    def pairs(self, stage):
        found = []
        for device in range(self.total):
            bit = stage[(device >> self.core) & 1]
            found.append((device, device ^ (1 << bit)))
        return found

    def swap(self, value, stage):
        return lax.ppermute(value, AXES, self.pairs(stage))

    def plan(self, step):
        here = self.here()
        core = (here >> self.core) & 1
        chosen = []
        for which in (0, 1):
            bit = self.stages[step][which]
            gone = [s[which] for s in self.stages[:step]]
            chosen.append((bit - sum(1 for g in gone if g < bit), (here >> bit) & 1))
        place = jnp.where(core == 0, chosen[0][0], chosen[1][0])
        value = jnp.where(core == 0, chosen[0][1], chosen[1][1])
        return jnp.stack([place, value]).astype(jnp.int32)


def insert_bit(index, place, value):
    low = index & ((1 << place) - 1)
    return ((index >> place) << (place + 1)) | (value << place) | low


def split_kernel(plan, own_keep, own_send, keep, send):
    keep[...] = own_keep[...]
    send[...] = own_send[...]


def join_kernel(plan, own_keep, own_send, come_keep, come_send, keep, send):
    keep[...] = (own_keep[...].astype(jnp.float32) + come_keep[...].astype(jnp.float32)).astype(keep.dtype)
    send[...] = (own_send[...].astype(jnp.float32) + come_send[...].astype(jnp.float32)).astype(send.dtype)


def last_kernel(own, come, out):
    out[...] = own[...].astype(jnp.float32) + come[...].astype(jnp.float32)


def halves(plan, own, come):
    blocks, rows, columns = own.shape
    shape = jax.ShapeDtypeStruct((blocks // 2, rows, columns), own.dtype)
    keep_map = lambda i, plan: (insert_bit(i, plan[0], plan[1]), 0, 0)
    send_map = lambda i, plan: (insert_bit(i, plan[0], 1 - plan[1]), 0, 0)
    block = (1, rows, columns)
    taken = [own, own] if come is None else [own, own, come, come]
    maps = [keep_map, send_map] * (len(taken) // 2)
    cost = pl.CostEstimate(flops=own.size, transcendentals=0, bytes_accessed=len(taken) * own.size * 2)
    return pl.pallas_call(
        split_kernel if come is None else join_kernel,
        grid_spec=pltpu.PrefetchScalarGridSpec(
            num_scalar_prefetch=1,
            grid=(blocks // 2,),
            in_specs=[pl.BlockSpec(block, m) for m in maps],
            out_specs=[pl.BlockSpec(block, lambda i, plan: (i, 0, 0))] * 2,
        ),
        out_shape=(shape, shape),
        cost_estimate=cost,
    )(plan, *taken)


def scatter_sum(grid, value):
    rows = value.shape[0] // grid.total
    held = value.reshape(grid.total, rows, value.shape[1])
    come = None
    for step, stage in enumerate(grid.stages):
        keep, send = halves(grid.plan(step), held, come)
        come = grid.swap(send, stage)
        held = keep
    out = pl.pallas_call(
        last_kernel,
        out_shape=jax.ShapeDtypeStruct(held.shape, jnp.float32),
        cost_estimate=pl.CostEstimate(flops=held.size, transcendentals=0, bytes_accessed=8 * held.size),
    )(held, come)
    return out.reshape(rows, value.shape[1])


def gather_small(grid, value):
    here = grid.here()
    held = value[None]
    for bit in range(grid.bits):
        come = grid.swap(held, (bit, bit))
        mine = (here >> bit) & 1
        held = jnp.where(mine == 0, jnp.concatenate([held, come]), jnp.concatenate([come, held]))
    return held


def scatter_small(grid, value):
    here = grid.here()
    held = value
    for bit in range(grid.bits - 1, -1, -1):
        mine = (here >> bit) & 1
        half = held.shape[0] // 2
        upper = mine == 1
        send = jnp.where(upper, held[:half], held[half:])
        keep = jnp.where(upper, held[half:], held[:half])
        held = keep + grid.swap(send, (bit, bit))
    return held


def body(
    grid,
    hidden_in,
    segment_ids,
    out_grad,
    norm1_gain,
    norm1_bias,
    norm2_gain,
    norm2_bias,
    qkv_weight,
    qkv_bias,
    proj_weight,
    proj_bias,
    up_weight,
    up_bias,
    down_weight,
    down_bias,
):
    small = (norm1_gain, norm1_bias, norm2_gain, norm2_bias, qkv_bias, proj_bias, up_bias, down_bias)
    widths = [entry.shape[0] for entry in small]
    packed = jnp.concatenate(small)
    packed = jnp.pad(packed, (0, -packed.shape[0] % 128))
    spread = gather_small(grid, packed)
    pieces, at = [], 0
    for width in widths:
        pieces.append(spread[:, at : at + width].reshape(-1))
        at += width
    gain_one, shift_one, gain_two, shift_two, b_qkv, b_proj, b_up, b_down = pieces
    w_qkv, w_proj, w_up, w_down = (
        lax.all_gather(entry, AXES, axis=0, tiled=True) for entry in (qkv_weight, proj_weight, up_weight, down_weight)
    )
    seq_count, length, model_width = hidden_in.shape
    row_count = seq_count * length
    scale = HEAD ** (-0.5)
    flat = hidden_in.reshape(row_count, model_width).astype(jnp.float32)
    grad_rows = out_grad.reshape(row_count, model_width)
    valid = (segment_ids != DOCS - 1).astype(jnp.float32).reshape(row_count, 1)
    cosine, sine = angles(segment_ids)
    normed_one = (
        normed(flat, gain_one.astype(jnp.float32)) + shift_one.astype(jnp.float32)
    ).astype(jnp.bfloat16)
    mixed = jnp.dot(normed_one, w_qkv, preferred_element_type=jnp.float32) + b_qkv.astype(
        jnp.float32
    )
    raw = mixed.reshape(seq_count, length, 3, HEADS, HEAD)
    raw_query = raw[:, :, 0]
    raw_keys = raw[:, :, 1]

    def rope_pair(first_part, second_part):
        return (rotate(first_part, cosine, sine), rotate(second_part, cosine, sine))

    (turned_query, turned_keys), rope_pull = jax.vjp(rope_pair, raw_query, raw_keys)
    query = (turned_query * scale).astype(jnp.bfloat16)
    keys = turned_keys.astype(jnp.bfloat16)
    values = raw[:, :, 2].astype(jnp.bfloat16)
    heads_out, log_sums = lax.map(attend_forward, (query, keys, values, segment_ids))
    attended = (heads_out.reshape(row_count, model_width) * valid).astype(jnp.bfloat16)
    projected = jnp.dot(attended, w_proj, preferred_element_type=jnp.float32) + b_proj.astype(
        jnp.float32
    )
    normed_two = (
        normed(flat, gain_two.astype(jnp.float32)) + shift_two.astype(jnp.float32)
    ).astype(jnp.bfloat16)
    before = jnp.dot(normed_two, w_up, preferred_element_type=jnp.float32) + b_up.astype(
        jnp.float32
    )
    after = jax.nn.gelu(before, approximate=False).astype(jnp.bfloat16)
    branch = jnp.dot(after, w_down, preferred_element_type=jnp.float32) + b_down.astype(jnp.float32)
    layer_out = (
        (flat + projected + branch).astype(jnp.bfloat16).reshape(seq_count, length, model_width)
    )
    back_gain_one, back_gain_two, back_qkv, back_proj, back_up, back_down = (
        gain_one, gain_two, w_qkv, w_proj, w_up, w_down
    )
    grad_wide = grad_rows.astype(jnp.float32)
    bias_grad = jnp.sum(grad_wide, axis=0)
    grad_down = jnp.einsum("rf,rd->fd", after, grad_rows, preferred_element_type=jnp.float32)
    d_after = jnp.einsum("rd,fd->rf", grad_rows, back_down, preferred_element_type=jnp.float32)
    gelu_value, gelu_pull = jax.vjp(partial(jax.nn.gelu, approximate=False), before)
    d_before = gelu_pull(d_after)[0].astype(jnp.bfloat16)
    grad_up_bias = jnp.sum(d_before.astype(jnp.float32), axis=0)
    grad_up = jnp.einsum("rd,rf->df", normed_two, d_before, preferred_element_type=jnp.float32)
    d_normed_two = jnp.einsum("rf,df->rd", d_before, back_up, preferred_element_type=jnp.float32)
    norm_value_two, pull_two = jax.vjp(normed, flat, back_gain_two.astype(jnp.float32))
    dx_two, grad_gain_two = pull_two(d_normed_two)
    grad_shift_two = jnp.sum(d_normed_two, axis=0)
    grad_proj = jnp.einsum("rd,re->de", attended, grad_rows, preferred_element_type=jnp.float32)
    d_attended = (
        jnp.einsum("re,de->rd", grad_rows, back_proj, preferred_element_type=jnp.float32) * valid
    ).astype(jnp.bfloat16)
    d_attended = d_attended.reshape(seq_count, length, HEADS, HEAD)
    d_query, d_keys, d_values = lax.map(
        attend_backward, (query, keys, values, segment_ids, log_sums, d_attended)
    )
    d_raw_query, d_raw_keys = rope_pull((d_query * scale, d_keys))
    d_mixed = (
        jnp.stack([d_raw_query, d_raw_keys, d_values], axis=2)
        .reshape(row_count, 3 * model_width)
        .astype(jnp.bfloat16)
    )
    grad_qkv_bias = jnp.sum(d_mixed.astype(jnp.float32), axis=0)
    grad_qkv = jnp.einsum("rd,rc->dc", normed_one, d_mixed, preferred_element_type=jnp.float32)
    d_normed_one = jnp.einsum("rc,dc->rd", d_mixed, back_qkv, preferred_element_type=jnp.float32)
    norm_value_one, pull_one = jax.vjp(normed, flat, back_gain_one.astype(jnp.float32))
    dx_one, grad_gain_one = pull_one(d_normed_one)
    grad_shift_one = jnp.sum(d_normed_one, axis=0)
    input_grad = (
        (grad_wide + dx_one + dx_two).astype(jnp.bfloat16).reshape(seq_count, length, model_width)
    )
    n = grid.total
    sums = (grad_gain_one, grad_shift_one, grad_gain_two, grad_shift_two, grad_qkv_bias, bias_grad, grad_up_bias)
    vectors = jnp.concatenate([entry.reshape(n, -1) for entry in sums], axis=1)
    vectors = jnp.pad(vectors, ((0, 0), (0, -vectors.shape[1] % 128)))
    total = scatter_small(grid, vectors)
    outs, at = [], 0
    for entry in sums:
        width = entry.shape[0] // n
        outs.append(total[0, at : at + width])
        at += width
    low = [scatter_sum(grid, entry.astype(jnp.bfloat16)) for entry in (grad_qkv, grad_proj, grad_up, grad_down)]
    return (
        layer_out,
        input_grad,
        outs[0],
        outs[1],
        outs[2],
        outs[3],
        low[0],
        outs[4],
        low[1],
        outs[5],
        low[2],
        outs[6],
        low[3],
        outs[5],
    )


NT = (((1,), (1,)), ((), ()))
NN = (((1,), (0,)), ((), ()))
TN = (((0,), (0,)), ((), ()))
PAIR = 2 * HEAD
ROWS = 256
TOKENS = 512


def mul(left, right, dims):
    return lax.dot_general(left, right, dims, preferred_element_type=jnp.float32)


def params(mebibytes):
    return pltpu.CompilerParams(vmem_limit_bytes=mebibytes << 20)


def cost(flops, moved, special=0):
    return pl.CostEstimate(flops=int(flops), transcendentals=int(special), bytes_accessed=int(moved))


def fixed(shape, at=None):
    place = (0,) * len(shape) if at is None else at
    return pl.BlockSpec(shape, lambda *_: place, pipeline_mode=pl.Buffered(1))


def middle_swap(value):
    quarter = (lax.broadcasted_iota(jnp.int32, value.shape, 1) % 128) // 32
    width = value.shape[1]
    up, down = pltpu.roll(value, width - 32, 1), pltpu.roll(value, 32, 1)
    return jnp.where(quarter == 1, up, jnp.where(quarter == 2, down, value))


def norm_kernel(mine, theirs, gmine, gtheirs, scales, one, two, grads):
    def work(source, cotangent):
        value = source[...].astype(jnp.float32)
        center = value - jnp.mean(value, axis=1, keepdims=True)
        spread = jnp.mean(center * center, axis=1, keepdims=True)
        hat = middle_swap(center * lax.rsqrt(spread + norm_eps))
        table = scales[...].astype(jnp.float32)
        one[...] = (hat * table[0:1] + table[1:2]).astype(jnp.bfloat16)
        two[...] = (hat * table[2:3] + table[3:4]).astype(jnp.bfloat16)
        grads[...] = cotangent[...]

    first = pl.program_id(0) == 0
    pl.when(first)(lambda: work(mine, gmine))
    pl.when(jnp.logical_not(first))(lambda: work(theirs, gtheirs))


def norms(mine, theirs, gmine, gtheirs, scales):
    length, width = mine.shape
    block = (ROWS, width)
    steps = length // ROWS
    own = pl.BlockSpec(block, lambda s, i: (jnp.where(s == 0, i, steps - 1), 0))
    other = pl.BlockSpec(block, lambda s, i: (jnp.where(s == 0, 0, i), 0))
    out = pl.BlockSpec(block, lambda s, i: (s * steps + i, 0))
    shape = jax.ShapeDtypeStruct((2 * length, width), jnp.bfloat16)
    return pl.pallas_call(
        norm_kernel,
        grid=(2, steps),
        in_specs=[own, other, own, other, fixed(scales.shape)],
        out_specs=[out] * 3,
        out_shape=[shape] * 3,
        compiler_params=params(16),
        cost_estimate=cost(40 * length * width, 20 * length * width),
    )(mine, theirs, gmine, gtheirs, scales)


def turn(value, cosine, sine):
    lane = lax.broadcasted_iota(jnp.int32, value.shape, 1) % HEAD
    half = ROT // 2
    up, down = pltpu.roll(value, value.shape[1] - half, 1), pltpu.roll(value, half, 1)
    return value * cosine + jnp.where(lane < half, up, down) * sine


def chosen(place, chip, near, far, *index):
    spot, half = place[chip], near.shape[0]
    return jnp.where(spot < half, near[(spot % half, *index)], far[(spot % half, *index)])


def arrange(place, half, weights, ordered, ordered_proj):
    chips = 2 * weights[0].shape[0]
    for part in range(3):
        near, far = weights[2 * part : 2 * part + 2]
        rows, width = near.shape[1:]
        for chip in range(chips):
            block = chosen(place, chip, near, far)
            ordered[chip * rows : (chip + 1) * rows, part * width : (part + 1) * width] = block
    near, far = weights[6:]
    below = near.shape[1] // 4
    for chip in range(chips // 2):
        block = chosen(place, half * chips // 2 + chip, near, far)
        for n in range(4):
            ordered_proj[chip * below : (chip + 1) * below, n * width : (n + 1) * width] = block[n * below : (n + 1) * below]


def weight_specs(weights, first):
    chips, _, width = weights[0].shape
    found = [fixed((chips, 64, width), (0, first + part, 0)) for part in range(3) for _ in weights]
    return found + [fixed((chips, 128, width))] * 2


def weight_scratch(weights):
    chips, _, width = weights[0].shape
    return [pltpu.VMEM((128 * chips, 3 * width), jnp.bfloat16), pltpu.VMEM((32 * chips, 4 * width), jnp.bfloat16)]


def project_kernel(half, place, normed, grads, *refs):
    weights = refs[:8]
    bias, cosine, sine, segments, out, ordered, ordered_proj = refs[8:]
    width = out.shape[-1]

    @pl.when(pl.program_id(0) == 0)
    def _():
        arrange(place, half, weights, ordered, ordered_proj)

    for part in range(3):
        columns = slice(part * width, (part + 1) * width)
        value = mul(normed[...], ordered[:, columns], NN) + bias[part].astype(jnp.float32)
        if part == 2:
            out[part] = value.astype(out.dtype)
            continue
        for at in range(0, width, PAIR):
            turned = turn(value[:, at : at + PAIR], cosine[...], sine[...])
            out[part, :, at : at + PAIR] = (turned * (HEAD ** (-0.5) if part == 0 else 1.0)).astype(out.dtype)
    valid = (segments[...] != DOCS - 1).astype(jnp.float32)
    out[3] = (mul(grads[...], ordered_proj[...], NT) * valid).astype(out.dtype)


def project(half, place, normed, grads, weights, first, proj, bias, cosine, sine, segments):
    tokens, model = normed.shape
    width = weights[0].shape[-1]
    rows = lambda n: pl.BlockSpec((TOKENS, n), lambda i, *_: (i, 0))
    return pl.pallas_call(
        partial(project_kernel, half),
        grid_spec=pltpu.PrefetchScalarGridSpec(
            num_scalar_prefetch=1,
            grid=(tokens // TOKENS,),
            in_specs=[rows(model), rows(model)]
            + weight_specs(weights, first)
            + [fixed(bias.shape), rows(PAIR), rows(PAIR), rows(1)],
            out_specs=pl.BlockSpec((4, TOKENS, width), lambda i, *_: (0, i, 0)),
            scratch_shapes=weight_scratch(weights),
        ),
        out_shape=jax.ShapeDtypeStruct((4, tokens, width), jnp.bfloat16),
        compiler_params=params(20),
        cost_estimate=cost(8 * tokens * model * width, 6 * tokens * model),
    )(place, normed, grads, *weights * 3, *proj, bias, cosine, sine, segments)


def attention_kernel(
    q_ref, k_ref, v_ref, g_ref, cosine, sine, seg_row, seg_col, *rest
):
    out, d_out, mask, dk_sum, dv_sum = rest[-5:]
    length = q_ref.shape[1]
    blocks = length // ROWS

    @pl.when(pl.program_id(0) == 0)
    def _():
        for block in range(blocks):
            start = block * ROWS
            end = start + ROWS
            key_pos = lax.broadcasted_iota(jnp.int32, (ROWS, end), 1)
            query_pos = lax.broadcasted_iota(jnp.int32, (ROWS, end), 0) + start
            allowed = (key_pos <= query_pos) & (seg_col[start:end, :] == seg_row[0, :, :end])
            mask[start:end, :end] = jnp.where(allowed, 0.0, masked_score)

    lane = lax.broadcasted_iota(jnp.int32, (ROWS, PAIR), 1)
    for block in range(blocks - 1, -1, -1):
        start = block * ROWS
        end = start + ROWS
        rows = slice(start, end)
        keys, values = k_ref[0, :end, :], v_ref[0, :end, :]
        query, grads = q_ref[0, rows, :], g_ref[0, rows, :]
        hide = mask[rows, :end]
        pieces = []
        for head in range(2):
            mine = lane < HEAD if head == 0 else lane >= HEAD
            own_query = jnp.where(mine, query, jnp.zeros_like(query))
            own_grads = jnp.where(mine, grads, jnp.zeros_like(grads))
            scores = mul(own_query, keys, NT) + hide
            exponent = jnp.exp(scores - jnp.max(scores, axis=1, keepdims=True))
            probs = exponent * (1.0 / jnp.sum(exponent, axis=1, keepdims=True))
            low = probs.astype(jnp.bfloat16)
            mixed = mul(low, values, NN)
            d_probs = mul(own_grads, values, NT)
            inner = jnp.sum(own_grads.astype(jnp.float32) * mixed, axis=1, keepdims=True)
            d_scores = (probs * (d_probs - inner)).astype(jnp.bfloat16)
            pieces.append((mixed, mul(d_scores, keys, NN)))
            d_keys, d_values = mul(d_scores, own_query, TN), mul(low, own_grads, TN)
            if block == blocks - 1 and head == 0:
                dk_sum[:end, :] = d_keys
                dv_sum[:end, :] = d_values
            else:
                dk_sum[:end, :] += d_keys
                dv_sum[:end, :] += d_values
        mine = lane < HEAD
        valid = (seg_col[rows, :] != DOCS - 1).astype(jnp.float32)
        out[rows, :] = (jnp.where(mine, pieces[0][0], pieces[1][0]) * valid).astype(out.dtype)
        d_query = turn(jnp.where(mine, pieces[0][1], pieces[1][1]), cosine[rows, :], -sine[rows, :])
        d_out[0, rows, :] = (d_query * HEAD ** (-0.5)).astype(d_out.dtype)
    d_out[1] = turn(dk_sum[...], cosine[...], -sine[...]).astype(d_out.dtype)
    d_out[2] = dv_sum[...].astype(d_out.dtype)


def attention(sequence, parts, cosine, sine, segments, before):
    length = segments.shape[1]
    tokens, width = parts.shape[1:]
    part = lambda p: pl.BlockSpec((1, length, PAIR), lambda j: (p, sequence, j))
    table = lambda n: pl.BlockSpec((length, n), lambda j: (sequence, 0))
    anywhere = pl.BlockSpec(memory_space=pl.ANY)
    return pl.pallas_call(
        attention_kernel,
        grid=(width // PAIR,),
        in_specs=[
            part(0),
            part(1),
            part(2),
            part(3),
            table(PAIR),
            table(PAIR),
            pl.BlockSpec((1, 1, length), lambda j: (sequence, 0, 0)),
            table(1),
        ]
        + [anywhere] * len(before),
        out_specs=[
            pl.BlockSpec((length, PAIR), lambda j: (sequence, j)),
            pl.BlockSpec((3, length, PAIR), lambda j: (0, sequence, j)),
        ],
        out_shape=[
            jax.ShapeDtypeStruct((tokens, width), jnp.bfloat16),
            jax.ShapeDtypeStruct((3, tokens, width), jnp.bfloat16),
        ],
        input_output_aliases={8 + n: n for n in range(len(before))},
        scratch_shapes=[pltpu.VMEM((length, length), jnp.float32)] + [pltpu.VMEM((length, PAIR), jnp.float32)] * 2,
        compiler_params=params(20),
        cost_estimate=cost(24 * tokens * length * width, 8 * tokens * width, tokens * length * width // 200),
    )(*[parts] * 4, cosine, sine, segments[:, None, :], segments.reshape(tokens, 1), *before)


def put_out(staged, keep, send, done):
    half = keep.shape[0]
    copies = [
        pltpu.make_async_copy(staged.at[pl.ds(n * half, half)], target, done.at[n])
        for n, target in enumerate((keep, send))
    ]
    for copy in copies:
        copy.start()
    for copy in copies:
        copy.wait()


def attention_grads_kernel(place, *refs):
    normed, d_mixed = refs[:2]
    more = refs[2:-7]
    keep, send, sums, totals, proj_total, staged, done = refs[-7:]
    step, last = pl.program_id(0), pl.num_programs(0) - 1
    width = d_mixed.shape[-1]
    chips = staged.shape[0]
    parts = totals.shape[0]
    rows = totals.shape[1] // chips

    @pl.when(step == 0)
    def _():
        totals[...] = jnp.zeros_like(totals)
        sums[...] = jnp.zeros_like(sums)
        if more:
            proj_total[...] = jnp.zeros_like(proj_total)

    for part in range(parts):
        totals[part] += mul(normed[...], d_mixed[part], TN)
        sums[part] += jnp.sum(d_mixed[part].astype(jnp.float32), axis=0, keepdims=True)
    if more:
        for n, attended in enumerate(more[:2]):
            proj_total[n * width : (n + 1) * width, :] += mul(attended[...], more[2][...], TN)

    @pl.when(step == last)
    def _():
        for chip in range(chips):
            spot = place[chip]
            for part in range(parts):
                change = totals[part, chip * rows : (chip + 1) * rows, :]
                staged[spot, part * rows : (part + 1) * rows, :] = change.astype(staged.dtype)
            if more:
                below = proj_total.shape[0] // chips
                for n in range(4):
                    change = proj_total[chip * below : (chip + 1) * below, n * width : (n + 1) * width]
                    start = parts * rows + n * below
                    staged[spot, start : start + below, :] = change.astype(staged.dtype)
        put_out(staged, keep, send, done)


def attention_grads(place, normed, d_mixed, more):
    tokens, model = normed.shape
    parts, _, width = d_mixed.shape
    chips = place.shape[0]
    rows = parts * model // chips + (4 * 2 * width // chips if more else 0)
    token = lambda n: pl.BlockSpec((TOKENS, n), lambda i, *_: (i, 0))
    half = jax.ShapeDtypeStruct((chips // 2, rows, width), jnp.bfloat16)
    anywhere = pl.BlockSpec(memory_space=pl.ANY)
    return pl.pallas_call(
        attention_grads_kernel,
        grid_spec=pltpu.PrefetchScalarGridSpec(
            num_scalar_prefetch=1,
            grid=(tokens // TOKENS,),
            in_specs=[token(model), pl.BlockSpec((parts, TOKENS, width), lambda i, *_: (0, i, 0))]
            + ([token(width), token(width), token(model)] if more else []),
            out_specs=[anywhere, anywhere, pl.BlockSpec((parts, 1, width), lambda i, *_: (0, 0, 0))],
            scratch_shapes=[
                pltpu.VMEM((parts, model, width), jnp.float32),
                pltpu.VMEM((2 * width, model), jnp.float32),
                pltpu.VMEM((chips, rows, width), jnp.bfloat16),
                pltpu.SemaphoreType.DMA((2,)),
            ],
        ),
        out_shape=[half, half, jax.ShapeDtypeStruct((parts, 1, width), jnp.float32)],
        compiler_params=params(26),
        cost_estimate=cost(8 * tokens * model * width, 6 * tokens * model),
    )(place, normed, d_mixed, *more)


def share_out(step, steps, before, mine, send, value):
    for own, ref, earlier in ((True, mine, before[:1]), (False, send, before[1:])):

        @pl.when((step < steps // 2) == own)
        def _():
            total = value
            for one in earlier:
                total = total + one[...].astype(jnp.float32)
            ref[...] = total.astype(ref.dtype)


def attention_back_kernel(half, place, d_mixed, attended, *refs):
    weights, before = refs[:8], refs[8:-6]
    d_mine, d_send, p_mine, p_send, ordered, ordered_proj = refs[-6:]
    step, steps = pl.program_id(0), pl.num_programs(0)

    @pl.when(step == 0)
    def _():
        arrange(place, half, weights, ordered, ordered_proj)

    change = jnp.concatenate([d_mixed[part] for part in range(3)], axis=1)
    share_out(step, steps, before[:2], d_mine, d_send, mul(change, ordered[...], NT))
    share_out(step, steps, before[2:], p_mine, p_send, mul(attended[...], ordered_proj[...], NN))


def attention_back(half, place, d_mixed, attended, weights, first, proj, before):
    parts, tokens, width = d_mixed.shape
    model = 128 * weights[0].shape[0]
    steps = tokens // TOKENS
    own = pl.BlockSpec((TOKENS, model), lambda i, *_: (jnp.minimum(i, steps // 2 - 1), 0))
    other = pl.BlockSpec((TOKENS, model), lambda i, *_: (jnp.maximum(i - steps // 2, 0), 0))
    shape = jax.ShapeDtypeStruct((tokens // 2, model), jnp.bfloat16)
    return pl.pallas_call(
        partial(attention_back_kernel, half),
        grid_spec=pltpu.PrefetchScalarGridSpec(
            num_scalar_prefetch=1,
            grid=(steps,),
            in_specs=[
                pl.BlockSpec((parts, TOKENS, width), lambda i, *_: (0, i, 0)),
                pl.BlockSpec((TOKENS, width), lambda i, *_: (i, 0)),
            ]
            + weight_specs(weights, first)
            + [own, other] * (len(before) // 2),
            out_specs=[own, other] * 2,
            scratch_shapes=weight_scratch(weights),
        ),
        out_shape=[shape] * 4,
        compiler_params=params(24),
        cost_estimate=cost(8 * tokens * model * width, 8 * tokens * model),
    )(place, d_mixed, attended, *weights * 3, *proj, *before)


def forward_kernel(place, normed, grads, near, far, bias, *refs):
    earlier, refs = refs[:-18], refs[-18:]
    keep, send, sums = refs[:3]
    outs = refs[3:7]
    own_normed, own_grads, up, down, after, d_before, results, staged, arrived, shared, left = refs[7:18]
    tokens, model = own_normed.shape
    hidden = up.shape[1]
    half_tokens = tokens // 2
    rows = near.shape[1] // 2
    chips = 2 * near.shape[0]
    blocks = tokens // ROWS

    def pieces(chip):
        at = pl.ds(chip * rows, rows)
        return ((0, up.at[at], 2 * chip), (rows, down.at[at], 2 * chip + 1))

    def row_loads(block):
        at = pl.ds(block * ROWS, ROWS)
        return [
            pltpu.make_async_copy(source.at[at], target.at[at], arrived.at[2 * chips + 2 * block + n])
            for n, (source, target) in enumerate(((normed, own_normed), (grads, own_grads)))
        ]

    loads = [pltpu.make_async_copy(ref, results.at[n], shared.at[n]) for n, ref in enumerate(earlier)]
    for chip in range(chips):
        spot = place[chip]
        for start, target, n in pieces(chip):
            for own, source in ((True, near), (False, far)):

                @pl.when((spot < chips // 2) == own)
                def _():
                    held = source.at[spot % (chips // 2), pl.ds(start, rows)]
                    pltpu.make_async_copy(held, target, arrived.at[n]).start()

    for block in range(blocks):
        for load in row_loads(block):
            load.start()
    for load in loads:
        load.start()
    for chip in range(chips):
        for start, target, n in pieces(chip):
            pltpu.make_async_copy(near.at[0, pl.ds(start, rows)], target, arrived.at[n]).wait()
    offset = bias[...].astype(jnp.float32)
    bias_total = jnp.zeros_like(offset)
    for block in range(blocks):
        at = slice(block * ROWS, (block + 1) * ROWS)
        for load in row_loads(block):
            load.wait()
        before = mul(own_normed[at, :], up[...], NN) + offset
        change = mul(own_grads[at, :], down[...], NT)
        share = 0.5 + 0.5 * lax.erf(before * 0.7071067811865476)
        density = jnp.exp(-0.5 * before * before) * 0.3989422804014327
        after[at, :] = (before * share).astype(after.dtype)
        low = (change * (share + before * density)).astype(d_before.dtype)
        d_before[at, :] = low
        bias_total += jnp.sum(low.astype(jnp.float32), axis=0, keepdims=True)
    sums[...] = bias_total
    for load in loads:
        load.wait()
    stores = []
    for block in range(blocks):
        at = slice(block * ROWS, (block + 1) * ROWS)
        side = 0 if block * ROWS < half_tokens else 1
        own = pl.ds(block * ROWS - side * half_tokens, ROWS)
        for which, value in enumerate((mul(after[at, :], down[...], NN), mul(d_before[at, :], up[...], NT))):
            n = 2 * which + side
            if n < len(earlier):
                value += results[n, own, :].astype(jnp.float32)
            results[n, own, :] = value.astype(results.dtype)
            store = pltpu.make_async_copy(results.at[n, own], outs[n].at[own], left.at[2 + 2 * block + which])
            store.start()
            stores.append(store)
    tile = 256
    for start in range(0, hidden, tile):
        change = mul(own_normed[...], d_before[:, start : start + tile], TN).astype(staged.dtype)
        for chip in range(chips):
            staged[place[chip], :rows, start : start + tile] = change[chip * rows : (chip + 1) * rows]
        change = mul(after[:, start : start + tile], own_grads[...], TN).astype(staged.dtype)
        for n in range(tile // rows):
            staged[place[start // rows + n], rows:, :] = change[n * rows : (n + 1) * rows]
    half = keep.shape[0]
    for n, target in enumerate((keep, send)):
        store = pltpu.make_async_copy(staged.at[pl.ds(n * half, half)], target, left.at[n])
        store.start()
        stores.append(store)
    for store in stores:
        store.wait()


def forward_chunk(place, normed, grads, weights, bias, earlier):
    tokens, model = normed.shape
    chips, both_rows, hidden = weights[0].shape
    chips *= 2
    low = lambda *shape: pltpu.VMEM(shape, jnp.bfloat16)
    blocks = jax.ShapeDtypeStruct((chips // 2, both_rows, model), jnp.bfloat16)
    anywhere = pl.BlockSpec(memory_space=pl.ANY)
    share = jax.ShapeDtypeStruct((tokens // 2, model), jnp.bfloat16)
    small = pl.BlockSpec((1, hidden), lambda i, *_: (0, 0))
    counts = (2 * chips + 2 * (tokens // ROWS), 4, 2 + 2 * (tokens // ROWS))
    return pl.pallas_call(
        forward_kernel,
        grid_spec=pltpu.PrefetchScalarGridSpec(
            num_scalar_prefetch=1,
            grid=(1,),
            in_specs=[anywhere] * 4 + [small] + [anywhere] * len(earlier),
            out_specs=[anywhere, anywhere, small] + [anywhere] * 4,
            scratch_shapes=[
                low(tokens, model),
                low(tokens, model),
                low(model, hidden),
                low(hidden, model),
                low(tokens, hidden),
                low(tokens, hidden),
                low(4, tokens // 2, model),
                low(chips, both_rows, model),
            ]
            + [pltpu.SemaphoreType.DMA((count,)) for count in counts],
        ),
        out_shape=[blocks, blocks, jax.ShapeDtypeStruct((1, hidden), jnp.float32)] + [share] * 4,
        compiler_params=params(44),
        cost_estimate=cost(12 * tokens * model * hidden, 16 * tokens * model, 2 * tokens * hidden),
    )(place, normed, grads, *weights, bias, *earlier)


def both_of(left, right):
    return left[...].astype(jnp.float32) + right[...].astype(jnp.float32)


def finish_out_kernel(hidden, mine, come, scales, layer_out):
    table = scales[...].astype(jnp.float32)
    total = both_of(mine, come) + table[0:1] + table[1:2]
    layer_out[...] = (hidden[...].astype(jnp.float32) + total).astype(layer_out.dtype)


def finish_grad_kernel(hidden, grads, one_mine, one_come, two_mine, two_come, scales, input_grad, sums):
    value = hidden[...].astype(jnp.float32)
    cotangent = grads[...].astype(jnp.float32)
    table = scales[...].astype(jnp.float32)
    center = value - jnp.mean(value, axis=1, keepdims=True)
    scale = lax.rsqrt(jnp.mean(center * center, axis=1, keepdims=True) + norm_eps)
    hat = center * scale
    one, two = middle_swap(both_of(one_mine, one_come)), middle_swap(both_of(two_mine, two_come))
    gained = one * table[0:1] + two * table[1:2]
    mean = jnp.mean(gained, axis=1, keepdims=True)
    slope = jnp.mean(gained * hat, axis=1, keepdims=True)
    input_grad[...] = (cotangent + (gained - mean - hat * slope) * scale).astype(input_grad.dtype)

    @pl.when(pl.program_id(0) == 0)
    def _():
        sums[...] = jnp.zeros_like(sums)

    for row, column in enumerate((one * hat, one, two * hat, two, cotangent)):
        sums[row : row + 1, :] += jnp.sum(column, axis=0, keepdims=True)


def finish(kernel, arrays, scales, with_sums):
    length, width = arrays[0].shape
    block = pl.BlockSpec((ROWS, width), lambda i: (i, 0))
    shape = jax.ShapeDtypeStruct((length, width), jnp.bfloat16)
    more = [pl.BlockSpec((8, width), lambda i: (0, 0))] if with_sums else []
    return pl.pallas_call(
        kernel,
        grid=(length // ROWS,),
        in_specs=[block] * len(arrays) + [fixed(scales.shape)],
        out_specs=[block] + more,
        out_shape=[shape] + [jax.ShapeDtypeStruct((8, width), jnp.float32)] * len(more),
        compiler_params=params(16),
        cost_estimate=cost(40 * length * width, 2 * (len(arrays) + 1) * length * width),
    )(*arrays, scales)


BITS = {"y": 0, "core": 1, "x": 2, "z_low": 3, "z_high": 4}
SPLIT = ("zx", "core", "y")
CORES = ("core", "core")
STAGES = (("x", "y"), ("y", "x"), ("z_low", "z_low"), ("z_high", "z_high"))


class Pairs:
    def __init__(self, total):
        self.total = total

    def here(self):
        y = lax.axis_size("y")
        return (lax.axis_index("zx") * 2 + lax.axis_index("core")) * y + lax.axis_index("y")

    def bit(self, name):
        return (self.here() >> BITS[name]) & 1

    def swap(self, value, names):
        moves = []
        for device in range(self.total):
            name = names[(device >> BITS["core"]) & 1]
            moves.append((device, device ^ (1 << BITS[name])))
        return lax.ppermute(value, SPLIT, moves)

    def places(self):
        chip = jnp.arange(self.total // 2, dtype=jnp.int32)
        bits = {"y": chip & 1, "x": (chip >> 1) & 1, "z_low": (chip >> 2) & 1, "z_high": (chip >> 3) & 1}
        differs = {name: bits[name] ^ self.bit(name) for name in bits}
        place = jnp.zeros_like(chip)
        for first, second in STAGES:
            place = 2 * place + jnp.where(lax.axis_index("core") == 0, differs[first], differs[second])
        return place


class Sum:
    def __init__(self, pairs, keep, send):
        self.pairs, self.arrays, self.stage = pairs, (keep, send), 0

    def ready(self, arrays):
        if self.stage == 0:
            return arrays
        keep, come = arrays
        half = keep.shape[0] // 2
        return add_low(keep[:half], come[:half]), add_low(keep[half:], come[half:])

    def move(self, arrays):
        keep, send = arrays
        self.arrays = keep, self.pairs.swap(send, STAGES[self.stage])
        self.stage += 1

    def result(self):
        keep, come = self.arrays
        return keep[0].astype(jnp.float32) + come[0].astype(jnp.float32)


class Gather:
    def __init__(self, pairs, own):
        self.pairs, self.arrays, self.stage = pairs, (own[None],), 0

    def ready(self, arrays):
        return arrays if self.stage == 0 else (jnp.concatenate(arrays),)

    def move(self, arrays):
        self.stage += 1
        self.arrays = arrays[0], self.pairs.swap(arrays[0], STAGES[-self.stage])

    def result(self):
        return self.arrays


class Trade:
    def __init__(self, pairs, *arrays):
        self.pairs, self.arrays, self.stage = pairs, arrays, 0

    def ready(self, arrays):
        return arrays

    def move(self, arrays):
        if self.stage == 0:
            arrays = tuple(self.pairs.swap(array, CORES) for array in arrays)
        self.arrays = arrays
        self.stage += 1

    def result(self):
        return self.arrays


def hold(value, tasks):
    value, arrays = lax.optimization_barrier((value, [task.arrays for task in tasks]))
    for task, own in zip(tasks, arrays):
        task.arrays = tuple(own)
    return value


def tick(after, value, *tasks, done=()):
    if after is not None:
        after = hold(after, tasks + tuple(done))
    for task in tasks:
        task.arrays = task.ready(task.arrays)
    after, value = hold((after, value), tasks)
    for task in tasks:
        task.move(task.arrays)
    return after, value


def add_low(left, right):
    return (left.astype(jnp.float32) + right.astype(jnp.float32)).astype(jnp.bfloat16)


def wide_angles(segments):
    position = lax.broadcasted_iota(jnp.int32, segments.shape, 1)
    change = jnp.concatenate([jnp.ones_like(segments[:, :1], jnp.bool_), segments[:, 1:] != segments[:, :-1]], axis=1)
    place = position - lax.cummax(jnp.where(change, position, 0), axis=1)
    lane = jnp.arange(PAIR) % HEAD
    half = ROT // 2
    freqs = 10000.0 ** (-((lane % half) * 2).astype(jnp.float32) / ROT)
    freqs = jnp.where(lane < ROT, freqs, 0.0)
    theta = place.reshape(-1, 1).astype(jnp.float32) * freqs
    return jnp.cos(theta), jnp.sin(theta) * jnp.where(lane < half, -1.0, 1.0)


def pick(value, which, axis):
    return lax.dynamic_index_in_dim(value, which, axis, keepdims=False)


def paired_body(
    pairs,
    hidden_in,
    segment_ids,
    out_grad,
    norm1_gain,
    norm1_bias,
    norm2_gain,
    norm2_bias,
    qkv_weight,
    qkv_bias,
    proj_weight,
    proj_bias,
    up_weight,
    up_bias,
    down_weight,
    down_bias,
):
    core = lax.axis_index("core")
    heads = HEADS // 2
    rows, model = qkv_weight.shape[0], proj_weight.shape[1]
    width = heads * HEAD // 2
    unit = down_weight.shape[0] // 2
    hidden, grads = hidden_in[0], out_grad[0]

    def columns(which):
        taken = pick(qkv_weight.reshape(rows, 3, heads, 2, HEAD), which, 3).reshape(rows, 3 * 2 * width)
        more = pick(up_weight.reshape(rows, heads, 2, 2, 2, unit), which, 2).transpose(0, 3, 1, 2, 4).reshape(rows, -1)
        return jnp.concatenate([taken, more], axis=1)

    theirs = pairs.swap(columns(1 - core), CORES)
    mine = columns(core)
    both = jnp.where(core == 0, jnp.stack([mine, theirs]), jnp.stack([theirs, mine])).reshape(2 * rows, -1)
    low_qkv = both[:, : 6 * width].reshape(2 * rows, 3, 2, width).transpose(2, 1, 0, 3)
    low_proj = proj_weight.reshape(rows, 4, width).transpose(1, 0, 2).reshape(2, 2 * rows, width)
    low_up = both[:, 6 * width :].reshape(2 * rows, 2, -1).transpose(1, 0, 2)
    low_down = down_weight.reshape(2, unit, model)

    other, other_grads = pairs.swap(hidden, CORES), pairs.swap(grads, CORES)
    segments = jnp.concatenate([segment_ids, pairs.swap(segment_ids, CORES)])
    column = segments.reshape(-1, 1)
    cosine, sine = wide_angles(segments)
    place = pairs.places()

    small = (norm1_gain, norm1_bias, norm2_gain, norm2_bias, qkv_bias, proj_bias, up_bias, down_bias)
    line = jnp.concatenate(small)
    line = jnp.pad(line, (0, -line.shape[0] % 128))
    come = pairs.swap(line, CORES)
    lines = Gather(pairs, jnp.where(core == 0, jnp.stack([line, come]), jnp.stack([come, line])).reshape(-1))
    first = Gather(pairs, jnp.concatenate([low_proj, low_qkv[0]]).reshape(-1, width))
    chunks = [Gather(pairs, jnp.concatenate([low_up[h], low_down[h]])) for h in range(2)]
    second = Gather(pairs, low_qkv[1].reshape(-1, width))
    tick(None, (), first, lines)
    tick(None, (), first, lines)
    tick(None, (), first, lines, chunks[0])
    tick(None, (), first, lines, chunks[0])
    w_first = first.result()
    table = jnp.concatenate(lines.result())[place]
    table = table.reshape(heads, 2, 2, -1).swapaxes(1, 2).reshape(pairs.total, -1)
    spread, at = [], 0
    for entry in small:
        size = entry.shape[0]
        spread.append(table[:, at : at + size].reshape(-1))
        at += size
    gain_one, shift_one, gain_two, shift_two, b_qkv, b_proj, b_up, b_down = spread
    own_bias = pick(b_qkv.reshape(3, heads, 2, HEAD), core, 2).reshape(3, 2, 1, width)
    own_up_bias = pick(b_up.reshape(heads, 2, 2, 2, unit), core, 1).transpose(2, 0, 1, 3).reshape(2, 1, -1)
    scales = jnp.stack([gain_one, shift_one, gain_two, shift_two])
    normed_one, normed_two, both_grads = norms(
        hidden, other, grads, other_grads, scales.reshape(4, -1, 2, 2, rows).swapaxes(2, 3).reshape(4, model)
    )

    (normed_one, cosine, sine), _ = tick((normed_one, cosine, sine), (), chunks[0], chunks[1])
    parts = project(
        0, place, normed_one, both_grads, w_first, 2, w_first, own_bias[:, 0], cosine, sine, column
    )
    parts, _ = tick(parts, (), chunks[0], chunks[1])
    before = attention(0, parts, cosine, sine, segments, ())
    before, parts = tick(before, parts, chunks[1])
    attended_one, d_mixed = attention(1, parts, cosine, sine, segments, before)
    (attended_one, d_mixed), _ = tick((attended_one, d_mixed), (), chunks[1], second)
    keep, send, qkv_sums_one = attention_grads(place, normed_one, d_mixed, ())
    sum_one = Sum(pairs, keep, send)
    _, d_mixed = tick(None, d_mixed, sum_one, second)
    d1, d1_send, out, out_send = attention_back(0, place, d_mixed, attended_one, w_first, 2, w_first, ())

    sum_forward, up_sums = [], []
    before = (out, out_send)
    for chunk in range(2):
        before, normed_two = tick(before, normed_two, sum_one, second, *sum_forward)
        keep, send, sums, *before = forward_chunk(
            place, normed_two, both_grads, chunks[chunk].result(), own_up_bias[chunk], before
        )
        up_sums.append(sums)
        sum_forward.append(Sum(pairs, keep, send))
    out, out_send, d2, d2_send = before
    (out, out_send, d2_send), normed_one = tick(
        (out, out_send, d2_send), normed_one, sum_one, sum_forward[0], done=(second,)
    )
    w_second = second.result()
    trade_two = Trade(pairs, d2_send)
    parts = project(
        1, place, normed_one, both_grads, w_second, 0, w_first, own_bias[:, 1], cosine, sine, column
    )
    parts, _ = tick(parts, (), sum_forward[0], sum_forward[1], trade_two, done=(sum_one,))
    before = attention(0, parts, cosine, sine, segments, ())
    before, parts = tick(before, parts, sum_forward[0], done=(trade_two,))
    attended_two, d_mixed = attention(1, parts, cosine, sine, segments, before)
    (attended_two, d_mixed), _ = tick((attended_two, d_mixed), (), sum_forward[1], done=sum_forward[:1])
    keep, send, qkv_sums_two = attention_grads(place, normed_one, d_mixed, (attended_one, attended_two, both_grads))
    sum_two = Sum(pairs, keep, send)
    qkv_sums_two, d_mixed = tick(qkv_sums_two, d_mixed, sum_forward[1], sum_two)
    back = attention_back(1, place, d_mixed, attended_two, w_second, 0, w_first, (d1, d1_send, out, out_send))
    (d1, d1_send, out, out_send), _ = tick(back, (), sum_forward[1], sum_two)
    trade = Trade(pairs, d1_send, out_send)
    tick(None, (), trade)
    d1_come, out_come = trade.result()
    input_grad, sums = finish(
        finish_grad_kernel,
        [hidden, grads, d1, d1_come, d2, *trade_two.result()],
        jnp.stack([gain_one, gain_two]),
        True,
    )
    (input_grad, sums), out = tick((input_grad, sums), out, sum_two, done=sum_forward[1:])
    layer_out = finish(finish_out_kernel, [hidden, out, out_come], jnp.stack([b_proj, b_down]), False)[0]
    layer_out, _ = tick(layer_out, (), sum_two)
    low_qkv_one, low_qkv_two = sum_one.result(), sum_two.result()
    low_forward = [task.result() for task in sum_forward]

    def whole_rows(value):
        mine, come = pick(value, core, 0), pairs.swap(pick(value, 1 - core, 0), CORES)
        return jnp.where(core == 0, jnp.stack([mine, come], 2), jnp.stack([come, mine], 2))

    third = 3 * 2 * rows
    both = jnp.stack([low_qkv_one, low_qkv_two[:third]]).reshape(2, 3, 2, rows, heads // 2, HEAD)
    grad_qkv = whole_rows(both.transpose(2, 3, 1, 0, 4, 5).reshape(2, rows, 3 * heads, HEAD)).reshape(rows, -1)
    grad_proj = low_qkv_two[third:].reshape(4, rows, width).transpose(1, 0, 2).reshape(rows, model)
    ups = jnp.stack([entry[: 2 * rows] for entry in low_forward]).reshape(2, 2, rows, heads, 2, unit)
    grad_up = whole_rows(ups.transpose(1, 2, 3, 4, 0, 5).reshape(2, rows, heads, 4 * unit)).reshape(rows, -1)
    grad_down = jnp.concatenate([entry[2 * rows :] for entry in low_forward])

    def both_cores(own):
        own = own[:, None]
        none = jnp.zeros_like(own)
        return jnp.where(core == 0, jnp.concatenate([own, none], axis=1), jnp.concatenate([none, own], axis=1)).reshape(-1)

    sum_qkv = jnp.stack([qkv_sums_one.reshape(3, -1), qkv_sums_two.reshape(3, -1)], axis=1)
    sum_up = jnp.stack([entry.reshape(heads, 2, unit) for entry in up_sums], axis=2)
    entries = [
        sums[0],
        sums[1],
        sums[2],
        sums[3],
        both_cores(sum_qkv.reshape(-1, HEAD)),
        sums[4],
        both_cores(sum_up.reshape(heads, -1)),
    ]
    table = jnp.concatenate([entry.reshape(pairs.total, -1) for entry in entries], axis=1)
    table = jnp.pad(table, ((0, 0), (0, -table.shape[1] % 128)))
    for name in reversed(BITS):
        upper = pairs.bit(name) == 1
        half = table.shape[0] // 2
        send = jnp.where(upper, table[:half], table[half:])
        table = jnp.where(upper, table[half:], table[:half]) + pairs.swap(send, (name, name))
    outs, at = [], 0
    for entry in entries:
        size = entry.shape[0] // pairs.total
        outs.append(table[0, at : at + size])
        at += size
    return (
        layer_out[None],
        input_grad[None],
        outs[0],
        outs[1],
        outs[2],
        outs[3],
        grad_qkv,
        outs[4],
        grad_proj,
        outs[5],
        grad_up,
        outs[6],
        grad_down,
        outs[5],
    )


def placed(axes):
    rows, flat = P(axes, None), P(axes)
    whole = P(axes, None, None)
    inside = (whole, rows, whole) + (flat,) * 4 + (rows, flat) * 4
    outside = (whole, whole) + (flat,) * 4 + (rows, flat) * 4
    return inside, outside


def solution(mesh):
    dp, fsdp = mesh.shape["dp"], mesh.shape["fsdp"]
    if (dp, fsdp) == (16, 2):
        split = Mesh(mesh.devices.reshape(dp // 2, 2, fsdp), SPLIT)
        inside, outside = placed(SPLIT)
        step = partial(paired_body, Pairs(dp * fsdp))
        return jax.shard_map(step, mesh=split, in_specs=inside, out_specs=outside, check_vma=False)
    inside, outside = placed(AXES)
    step = partial(body, Grid((dp, fsdp)))
    return jax.shard_map(step, mesh=mesh, in_specs=inside, out_specs=outside, check_vma=False)
```

```python
from functools import partial

import jax
import jax.numpy as jnp
from jax import lax
from jax.experimental import pallas as pl
from jax.experimental.pallas import tpu as pltpu
from jax.sharding import Mesh
from jax.sharding import PartitionSpec as P

AXES = ("dp", "fsdp")

HEADS = 16
HEAD = 64
ROT = 16
DOCS = 8


norm_eps = 1e-05
masked_score = -1e30


def normed(values, gain):
    center = values - jnp.mean(values, axis=-1, keepdims=True)
    spread = jnp.mean(center * center, axis=-1, keepdims=True)
    return center * lax.rsqrt(spread + norm_eps) * gain


def rotate(part, cosine, sine):
    half_rot = ROT // 2
    first = part[..., :half_rot]
    second = part[..., half_rot:ROT]
    cos_wide = cosine[..., None, :]
    sin_wide = sine[..., None, :]
    return jnp.concatenate(
        [
            first * cos_wide - second * sin_wide,
            second * cos_wide + first * sin_wide,
            part[..., ROT:],
        ],
        axis=-1,
    )


def angles(segments):
    last_axis = segments.ndim - 1
    position = lax.broadcasted_iota(jnp.int32, segments.shape, last_axis)
    change = jnp.concatenate(
        [jnp.ones(segments.shape[:-1] + (1,), jnp.bool_), segments[..., 1:] != segments[..., :-1]],
        axis=-1,
    )
    first_index = lax.cummax(jnp.where(change, position, jnp.zeros_like(position)), axis=last_axis)
    place = (position - first_index).astype(jnp.float32)
    freqs = 10000.0 ** (-(jnp.arange(ROT // 2) * 2).astype(jnp.float32) / ROT)
    theta = place[..., None] * freqs
    return (jnp.cos(theta), jnp.sin(theta))


def block_mask(segments, block_start, block_rows):
    length = segments.shape[0]
    query_pos = block_start + lax.broadcasted_iota(jnp.int32, (block_rows, length), 0)
    key_pos = lax.broadcasted_iota(jnp.int32, (block_rows, length), 1)
    same = segments[block_start : block_start + block_rows][:, None] == segments[None, :]
    return ((key_pos <= query_pos) & same)[None]


def attend_forward(pieces):
    query, keys, values, segments = pieces
    length = segments.shape[0]
    block_rows = min(512, length)
    outputs = []
    log_sums = []
    for block_start in range(0, length, block_rows):
        allowed = block_mask(segments, block_start, block_rows)
        scores = jnp.einsum(
            "qhe,khe->hqk",
            query[block_start : block_start + block_rows],
            keys,
            preferred_element_type=jnp.float32,
        )
        scores = jnp.where(allowed, scores, masked_score)
        row_max = jnp.max(scores, axis=-1, keepdims=True)
        exponent = jnp.exp(scores - row_max)
        total = jnp.sum(exponent, axis=-1, keepdims=True)
        weights = (exponent / total).astype(jnp.bfloat16)
        outputs.append(
            jnp.einsum("hqk,khe->qhe", weights, values, preferred_element_type=jnp.float32)
        )
        log_sums.append(row_max + jnp.log(total))
    return (jnp.concatenate(outputs, axis=0), jnp.concatenate(log_sums, axis=1))


def attend_backward(pieces):
    query, keys, values, segments, log_sums, d_out = pieces
    length = segments.shape[0]
    block_rows = min(512, length)
    query_parts = []
    d_keys = jnp.zeros(keys.shape, jnp.float32)
    d_values = jnp.zeros(values.shape, jnp.float32)
    for block_start in range(0, length, block_rows):
        block_end = block_start + block_rows
        allowed = block_mask(segments, block_start, block_rows)
        scores = jnp.einsum(
            "qhe,khe->hqk", query[block_start:block_end], keys, preferred_element_type=jnp.float32
        )
        scores = jnp.where(allowed, scores, masked_score)
        probs = jnp.exp(scores - log_sums[:, block_start:block_end])
        d_probs = jnp.einsum(
            "qhe,khe->hqk", d_out[block_start:block_end], values, preferred_element_type=jnp.float32
        )
        inner = jnp.sum(d_probs * probs, axis=-1, keepdims=True)
        d_scores = (probs * (d_probs - inner)).astype(jnp.bfloat16)
        d_values = d_values + jnp.einsum(
            "hqk,qhe->khe",
            probs.astype(jnp.bfloat16),
            d_out[block_start:block_end],
            preferred_element_type=jnp.float32,
        )
        query_parts.append(
            jnp.einsum("hqk,khe->qhe", d_scores, keys, preferred_element_type=jnp.float32)
        )
        d_keys = d_keys + jnp.einsum(
            "hqk,qhe->khe",
            d_scores,
            query[block_start:block_end],
            preferred_element_type=jnp.float32,
        )
    return (jnp.concatenate(query_parts, axis=0), d_keys, d_values)


class Grid:
    def __init__(self, sizes):
        dp, fsdp = sizes
        self.total = dp * fsdp
        self.low = fsdp.bit_length() - 1
        self.bits = self.total.bit_length() - 1
        self.core = self.low
        self.x = self.low + 1
        self.y = self.low - 1
        stages = [(self.core, self.core), (self.x, self.y), (self.y, self.x)]
        stages += [(b, b) for b in range(self.low - 2, -1, -1)]
        stages += [(b, b) for b in range(self.x + 1, self.bits)]
        self.stages = stages

    def here(self):
        return lax.axis_index("dp") * (1 << self.low) + lax.axis_index("fsdp")

    def pairs(self, stage):
        found = []
        for device in range(self.total):
            bit = stage[(device >> self.core) & 1]
            found.append((device, device ^ (1 << bit)))
        return found

    def swap(self, value, stage):
        return lax.ppermute(value, AXES, self.pairs(stage))

    def plan(self, step):
        here = self.here()
        core = (here >> self.core) & 1
        chosen = []
        for which in (0, 1):
            bit = self.stages[step][which]
            gone = [s[which] for s in self.stages[:step]]
            chosen.append((bit - sum(1 for g in gone if g < bit), (here >> bit) & 1))
        place = jnp.where(core == 0, chosen[0][0], chosen[1][0])
        value = jnp.where(core == 0, chosen[0][1], chosen[1][1])
        return jnp.stack([place, value]).astype(jnp.int32)


def insert_bit(index, place, value):
    low = index & ((1 << place) - 1)
    return ((index >> place) << (place + 1)) | (value << place) | low


def split_kernel(plan, own_keep, own_send, keep, send):
    keep[...] = own_keep[...]
    send[...] = own_send[...]


def join_kernel(plan, own_keep, own_send, come_keep, come_send, keep, send):
    keep[...] = (own_keep[...].astype(jnp.float32) + come_keep[...].astype(jnp.float32)).astype(keep.dtype)
    send[...] = (own_send[...].astype(jnp.float32) + come_send[...].astype(jnp.float32)).astype(send.dtype)


def last_kernel(own, come, out):
    out[...] = own[...].astype(jnp.float32) + come[...].astype(jnp.float32)


def halves(plan, own, come):
    blocks, rows, columns = own.shape
    shape = jax.ShapeDtypeStruct((blocks // 2, rows, columns), own.dtype)
    keep_map = lambda i, plan: (insert_bit(i, plan[0], plan[1]), 0, 0)
    send_map = lambda i, plan: (insert_bit(i, plan[0], 1 - plan[1]), 0, 0)
    block = (1, rows, columns)
    taken = [own, own] if come is None else [own, own, come, come]
    maps = [keep_map, send_map] * (len(taken) // 2)
    cost = pl.CostEstimate(flops=own.size, transcendentals=0, bytes_accessed=len(taken) * own.size * 2)
    return pl.pallas_call(
        split_kernel if come is None else join_kernel,
        grid_spec=pltpu.PrefetchScalarGridSpec(
            num_scalar_prefetch=1,
            grid=(blocks // 2,),
            in_specs=[pl.BlockSpec(block, m) for m in maps],
            out_specs=[pl.BlockSpec(block, lambda i, plan: (i, 0, 0))] * 2,
        ),
        out_shape=(shape, shape),
        cost_estimate=cost,
    )(plan, *taken)


def scatter_sum(grid, value):
    rows = value.shape[0] // grid.total
    held = value.reshape(grid.total, rows, value.shape[1])
    come = None
    for step, stage in enumerate(grid.stages):
        keep, send = halves(grid.plan(step), held, come)
        come = grid.swap(send, stage)
        held = keep
    out = pl.pallas_call(
        last_kernel,
        out_shape=jax.ShapeDtypeStruct(held.shape, jnp.float32),
        cost_estimate=pl.CostEstimate(flops=held.size, transcendentals=0, bytes_accessed=8 * held.size),
    )(held, come)
    return out.reshape(rows, value.shape[1])


def gather_small(grid, value):
    here = grid.here()
    held = value[None]
    for bit in range(grid.bits):
        come = grid.swap(held, (bit, bit))
        mine = (here >> bit) & 1
        held = jnp.where(mine == 0, jnp.concatenate([held, come]), jnp.concatenate([come, held]))
    return held


def scatter_small(grid, value):
    here = grid.here()
    held = value
    for bit in range(grid.bits - 1, -1, -1):
        mine = (here >> bit) & 1
        half = held.shape[0] // 2
        upper = mine == 1
        send = jnp.where(upper, held[:half], held[half:])
        keep = jnp.where(upper, held[half:], held[:half])
        held = keep + grid.swap(send, (bit, bit))
    return held


def body(
    grid,
    hidden_in,
    segment_ids,
    out_grad,
    norm1_gain,
    norm1_bias,
    norm2_gain,
    norm2_bias,
    qkv_weight,
    qkv_bias,
    proj_weight,
    proj_bias,
    up_weight,
    up_bias,
    down_weight,
    down_bias,
):
    small = (norm1_gain, norm1_bias, norm2_gain, norm2_bias, qkv_bias, proj_bias, up_bias, down_bias)
    widths = [entry.shape[0] for entry in small]
    packed = jnp.concatenate(small)
    packed = jnp.pad(packed, (0, -packed.shape[0] % 128))
    spread = gather_small(grid, packed)
    pieces, at = [], 0
    for width in widths:
        pieces.append(spread[:, at : at + width].reshape(-1))
        at += width
    gain_one, shift_one, gain_two, shift_two, b_qkv, b_proj, b_up, b_down = pieces
    w_qkv, w_proj, w_up, w_down = (
        lax.all_gather(entry, AXES, axis=0, tiled=True) for entry in (qkv_weight, proj_weight, up_weight, down_weight)
    )
    seq_count, length, model_width = hidden_in.shape
    row_count = seq_count * length
    scale = HEAD ** (-0.5)
    flat = hidden_in.reshape(row_count, model_width).astype(jnp.float32)
    grad_rows = out_grad.reshape(row_count, model_width)
    valid = (segment_ids != DOCS - 1).astype(jnp.float32).reshape(row_count, 1)
    cosine, sine = angles(segment_ids)
    normed_one = (
        normed(flat, gain_one.astype(jnp.float32)) + shift_one.astype(jnp.float32)
    ).astype(jnp.bfloat16)
    mixed = jnp.dot(normed_one, w_qkv, preferred_element_type=jnp.float32) + b_qkv.astype(
        jnp.float32
    )
    raw = mixed.reshape(seq_count, length, 3, HEADS, HEAD)
    raw_query = raw[:, :, 0]
    raw_keys = raw[:, :, 1]

    def rope_pair(first_part, second_part):
        return (rotate(first_part, cosine, sine), rotate(second_part, cosine, sine))

    (turned_query, turned_keys), rope_pull = jax.vjp(rope_pair, raw_query, raw_keys)
    query = (turned_query * scale).astype(jnp.bfloat16)
    keys = turned_keys.astype(jnp.bfloat16)
    values = raw[:, :, 2].astype(jnp.bfloat16)
    heads_out, log_sums = lax.map(attend_forward, (query, keys, values, segment_ids))
    attended = (heads_out.reshape(row_count, model_width) * valid).astype(jnp.bfloat16)
    projected = jnp.dot(attended, w_proj, preferred_element_type=jnp.float32) + b_proj.astype(
        jnp.float32
    )
    normed_two = (
        normed(flat, gain_two.astype(jnp.float32)) + shift_two.astype(jnp.float32)
    ).astype(jnp.bfloat16)
    before = jnp.dot(normed_two, w_up, preferred_element_type=jnp.float32) + b_up.astype(
        jnp.float32
    )
    after = jax.nn.gelu(before, approximate=False).astype(jnp.bfloat16)
    branch = jnp.dot(after, w_down, preferred_element_type=jnp.float32) + b_down.astype(jnp.float32)
    layer_out = (
        (flat + projected + branch).astype(jnp.bfloat16).reshape(seq_count, length, model_width)
    )
    back_gain_one, back_gain_two, back_qkv, back_proj, back_up, back_down = (
        gain_one, gain_two, w_qkv, w_proj, w_up, w_down
    )
    grad_wide = grad_rows.astype(jnp.float32)
    bias_grad = jnp.sum(grad_wide, axis=0)
    grad_down = jnp.einsum("rf,rd->fd", after, grad_rows, preferred_element_type=jnp.float32)
    d_after = jnp.einsum("rd,fd->rf", grad_rows, back_down, preferred_element_type=jnp.float32)
    gelu_value, gelu_pull = jax.vjp(partial(jax.nn.gelu, approximate=False), before)
    d_before = gelu_pull(d_after)[0].astype(jnp.bfloat16)
    grad_up_bias = jnp.sum(d_before.astype(jnp.float32), axis=0)
    grad_up = jnp.einsum("rd,rf->df", normed_two, d_before, preferred_element_type=jnp.float32)
    d_normed_two = jnp.einsum("rf,df->rd", d_before, back_up, preferred_element_type=jnp.float32)
    norm_value_two, pull_two = jax.vjp(normed, flat, back_gain_two.astype(jnp.float32))
    dx_two, grad_gain_two = pull_two(d_normed_two)
    grad_shift_two = jnp.sum(d_normed_two, axis=0)
    grad_proj = jnp.einsum("rd,re->de", attended, grad_rows, preferred_element_type=jnp.float32)
    d_attended = (
        jnp.einsum("re,de->rd", grad_rows, back_proj, preferred_element_type=jnp.float32) * valid
    ).astype(jnp.bfloat16)
    d_attended = d_attended.reshape(seq_count, length, HEADS, HEAD)
    d_query, d_keys, d_values = lax.map(
        attend_backward, (query, keys, values, segment_ids, log_sums, d_attended)
    )
    d_raw_query, d_raw_keys = rope_pull((d_query * scale, d_keys))
    d_mixed = (
        jnp.stack([d_raw_query, d_raw_keys, d_values], axis=2)
        .reshape(row_count, 3 * model_width)
        .astype(jnp.bfloat16)
    )
    grad_qkv_bias = jnp.sum(d_mixed.astype(jnp.float32), axis=0)
    grad_qkv = jnp.einsum("rd,rc->dc", normed_one, d_mixed, preferred_element_type=jnp.float32)
    d_normed_one = jnp.einsum("rc,dc->rd", d_mixed, back_qkv, preferred_element_type=jnp.float32)
    norm_value_one, pull_one = jax.vjp(normed, flat, back_gain_one.astype(jnp.float32))
    dx_one, grad_gain_one = pull_one(d_normed_one)
    grad_shift_one = jnp.sum(d_normed_one, axis=0)
    input_grad = (
        (grad_wide + dx_one + dx_two).astype(jnp.bfloat16).reshape(seq_count, length, model_width)
    )
    n = grid.total
    sums = (grad_gain_one, grad_shift_one, grad_gain_two, grad_shift_two, grad_qkv_bias, bias_grad, grad_up_bias)
    vectors = jnp.concatenate([entry.reshape(n, -1) for entry in sums], axis=1)
    vectors = jnp.pad(vectors, ((0, 0), (0, -vectors.shape[1] % 128)))
    total = scatter_small(grid, vectors)
    outs, at = [], 0
    for entry in sums:
        width = entry.shape[0] // n
        outs.append(total[0, at : at + width])
        at += width
    low = [scatter_sum(grid, entry.astype(jnp.bfloat16)) for entry in (grad_qkv, grad_proj, grad_up, grad_down)]
    return (
        layer_out,
        input_grad,
        outs[0],
        outs[1],
        outs[2],
        outs[3],
        low[0],
        outs[4],
        low[1],
        outs[5],
        low[2],
        outs[6],
        low[3],
        outs[5],
    )


NT = (((1,), (1,)), ((), ()))
NN = (((1,), (0,)), ((), ()))
TN = (((0,), (0,)), ((), ()))
PAIR = 2 * HEAD
ROWS = 256
TOKENS = 512


def mul(left, right, dims):
    return lax.dot_general(left, right, dims, preferred_element_type=jnp.float32)


def params(mebibytes):
    return pltpu.CompilerParams(vmem_limit_bytes=mebibytes << 20)


def cost(flops, moved, special=0):
    return pl.CostEstimate(flops=int(flops), transcendentals=int(special), bytes_accessed=int(moved))


def fixed(shape, at=None):
    place = (0,) * len(shape) if at is None else at
    return pl.BlockSpec(shape, lambda *_: place, pipeline_mode=pl.Buffered(1))


def middle_swap(value):
    quarter = (lax.broadcasted_iota(jnp.int32, value.shape, 1) % 128) // 32
    width = value.shape[1]
    up, down = pltpu.roll(value, width - 32, 1), pltpu.roll(value, 32, 1)
    return jnp.where(quarter == 1, up, jnp.where(quarter == 2, down, value))


def norm_kernel(source, cotangent, scales, *refs):
    one, two, grads = refs[-3:]
    value = source[...].astype(jnp.float32)
    center = value - jnp.mean(value, axis=1, keepdims=True)
    spread = jnp.mean(center * center, axis=1, keepdims=True)
    hat = middle_swap(center * lax.rsqrt(spread + norm_eps))
    table = scales[...].astype(jnp.float32)
    one[...] = (hat * table[0:1] + table[1:2]).astype(jnp.bfloat16)
    two[...] = (hat * table[2:3] + table[3:4]).astype(jnp.bfloat16)
    grads[...] = cotangent[...]


def norms(sequence, source, cotangent, scales, before):
    length, width = source.shape
    steps = length // ROWS
    block = pl.BlockSpec((ROWS, width), lambda i: (i, 0))
    out = pl.BlockSpec((ROWS, width), lambda i: (sequence * steps + i, 0))
    shape = jax.ShapeDtypeStruct((2 * length, width), jnp.bfloat16)
    return pl.pallas_call(
        norm_kernel,
        grid=(steps,),
        in_specs=[block, block, fixed(scales.shape)] + [pl.BlockSpec(memory_space=pl.ANY)] * len(before),
        out_specs=[out] * 3,
        out_shape=[shape] * 3,
        input_output_aliases={3 + n: n for n in range(len(before))},
        compiler_params=params(60),
        cost_estimate=cost(20 * length * width, 10 * length * width),
    )(source, cotangent, scales, *before)


def turn(value, cosine, sine):
    lane = lax.broadcasted_iota(jnp.int32, value.shape, 1) % HEAD
    half = ROT // 2
    up, down = pltpu.roll(value, value.shape[1] - half, 1), pltpu.roll(value, half, 1)
    return value * cosine + jnp.where(lane < half, up, down) * sine


def chosen(place, chip, near, far, *index):
    spot, half = place[chip], near.shape[0]
    return jnp.where(spot < half, near[(spot % half, *index)], far[(spot % half, *index)])


def arrange(place, half, weights, ordered, ordered_proj):
    chips = 2 * weights[0].shape[0]
    for part in range(3):
        near, far = weights[2 * part : 2 * part + 2]
        rows, width = near.shape[1:]
        for chip in range(chips):
            block = chosen(place, chip, near, far)
            ordered[chip * rows : (chip + 1) * rows, part * width : (part + 1) * width] = block
    near, far = weights[6:]
    below = near.shape[1] // 4
    for chip in range(chips // 2):
        block = chosen(place, half * chips // 2 + chip, near, far)
        for n in range(4):
            ordered_proj[chip * below : (chip + 1) * below, n * width : (n + 1) * width] = block[n * below : (n + 1) * below]


def weight_specs(weights, first):
    chips, _, width = weights[0].shape
    found = [fixed((chips, 64, width), (0, first + part, 0)) for part in range(3) for _ in weights]
    return found + [fixed((chips, 128, width))] * 2


def weight_scratch(weights):
    chips, _, width = weights[0].shape
    return [pltpu.VMEM((128 * chips, 3 * width), jnp.bfloat16), pltpu.VMEM((32 * chips, 4 * width), jnp.bfloat16)]


def project_kernel(half, place, normed, grads, *refs):
    weights = refs[:8]
    bias, cosine, sine, segments, out, ordered, ordered_proj = refs[8:]
    width = out.shape[-1]

    @pl.when(pl.program_id(0) == 0)
    def _():
        arrange(place, half, weights, ordered, ordered_proj)

    for part in range(3):
        columns = slice(part * width, (part + 1) * width)
        value = mul(normed[...], ordered[:, columns], NN) + bias[part].astype(jnp.float32)
        if part == 2:
            out[part] = value.astype(out.dtype)
            continue
        for at in range(0, width, PAIR):
            turned = turn(value[:, at : at + PAIR], cosine[...], sine[...])
            out[part, :, at : at + PAIR] = (turned * (HEAD ** (-0.5) if part == 0 else 1.0)).astype(out.dtype)
    valid = (segments[...] != DOCS - 1).astype(jnp.float32)
    out[3] = (mul(grads[...], ordered_proj[...], NT) * valid).astype(out.dtype)


def project(half, place, normed, grads, weights, first, proj, bias, cosine, sine, segments):
    tokens, model = normed.shape
    width = weights[0].shape[-1]
    rows = lambda n: pl.BlockSpec((TOKENS, n), lambda i, *_: (i, 0))
    return pl.pallas_call(
        partial(project_kernel, half),
        grid_spec=pltpu.PrefetchScalarGridSpec(
            num_scalar_prefetch=1,
            grid=(tokens // TOKENS,),
            in_specs=[rows(model), rows(model)]
            + weight_specs(weights, first)
            + [fixed(bias.shape), rows(PAIR), rows(PAIR), rows(1)],
            out_specs=pl.BlockSpec((4, TOKENS, width), lambda i, *_: (0, i, 0)),
            scratch_shapes=weight_scratch(weights),
        ),
        out_shape=jax.ShapeDtypeStruct((4, tokens, width), jnp.bfloat16),
        compiler_params=params(60),
        cost_estimate=cost(8 * tokens * model * width, 6 * tokens * model),
    )(place, normed, grads, *weights * 3, *proj, bias, cosine, sine, segments)


def attention_kernel(
    q_ref, k_ref, v_ref, g_ref, cosine, sine, seg_row, seg_col, *rest
):
    out, d_out, mask, dk_sum, dv_sum = rest[-5:]
    length = q_ref.shape[1]
    blocks = length // ROWS

    @pl.when(pl.program_id(0) == 0)
    def _():
        for block in range(blocks):
            start = block * ROWS
            end = start + ROWS
            key_pos = lax.broadcasted_iota(jnp.int32, (ROWS, end), 1)
            query_pos = lax.broadcasted_iota(jnp.int32, (ROWS, end), 0) + start
            allowed = (key_pos <= query_pos) & (seg_col[start:end, :] == seg_row[0, :, :end])
            mask[start:end, :end] = jnp.where(allowed, 0.0, masked_score)

    lane = lax.broadcasted_iota(jnp.int32, (ROWS, PAIR), 1)
    for block in range(blocks - 1, -1, -1):
        start = block * ROWS
        end = start + ROWS
        rows = slice(start, end)
        keys, values = k_ref[0, :end, :], v_ref[0, :end, :]
        query, grads = q_ref[0, rows, :], g_ref[0, rows, :]
        hide = mask[rows, :end]
        pieces = []
        for head in range(2):
            mine = lane < HEAD if head == 0 else lane >= HEAD
            own_query = jnp.where(mine, query, jnp.zeros_like(query))
            own_grads = jnp.where(mine, grads, jnp.zeros_like(grads))
            scores = mul(own_query, keys, NT) + hide
            exponent = jnp.exp(scores - jnp.max(scores, axis=1, keepdims=True))
            probs = exponent * (1.0 / jnp.sum(exponent, axis=1, keepdims=True))
            low = probs.astype(jnp.bfloat16)
            mixed = mul(low, values, NN)
            d_probs = mul(own_grads, values, NT)
            inner = jnp.sum(own_grads.astype(jnp.float32) * mixed, axis=1, keepdims=True)
            d_scores = (probs * (d_probs - inner)).astype(jnp.bfloat16)
            pieces.append((mixed, mul(d_scores, keys, NN)))
            d_keys, d_values = mul(d_scores, own_query, TN), mul(low, own_grads, TN)
            if block == blocks - 1 and head == 0:
                dk_sum[:end, :] = d_keys
                dv_sum[:end, :] = d_values
            else:
                dk_sum[:end, :] += d_keys
                dv_sum[:end, :] += d_values
        mine = lane < HEAD
        valid = (seg_col[rows, :] != DOCS - 1).astype(jnp.float32)
        out[rows, :] = (jnp.where(mine, pieces[0][0], pieces[1][0]) * valid).astype(out.dtype)
        d_query = turn(jnp.where(mine, pieces[0][1], pieces[1][1]), cosine[rows, :], -sine[rows, :])
        d_out[0, rows, :] = (d_query * HEAD ** (-0.5)).astype(d_out.dtype)
    d_out[1] = turn(dk_sum[...], cosine[...], -sine[...]).astype(d_out.dtype)
    d_out[2] = dv_sum[...].astype(d_out.dtype)


def attention(sequence, parts, cosine, sine, segments, before):
    length = segments.shape[1]
    tokens, width = parts.shape[1:]
    part = lambda p: pl.BlockSpec((1, length, PAIR), lambda j: (p, sequence, j))
    table = lambda n: pl.BlockSpec((length, n), lambda j: (sequence, 0))
    anywhere = pl.BlockSpec(memory_space=pl.ANY)
    return pl.pallas_call(
        attention_kernel,
        grid=(width // PAIR,),
        in_specs=[
            part(0),
            part(1),
            part(2),
            part(3),
            table(PAIR),
            table(PAIR),
            pl.BlockSpec((1, 1, length), lambda j: (sequence, 0, 0)),
            table(1),
        ]
        + [anywhere] * len(before),
        out_specs=[
            pl.BlockSpec((length, PAIR), lambda j: (sequence, j)),
            pl.BlockSpec((3, length, PAIR), lambda j: (0, sequence, j)),
        ],
        out_shape=[
            jax.ShapeDtypeStruct((tokens, width), jnp.bfloat16),
            jax.ShapeDtypeStruct((3, tokens, width), jnp.bfloat16),
        ],
        input_output_aliases={8 + n: n for n in range(len(before))},
        scratch_shapes=[pltpu.VMEM((length, length), jnp.float32)] + [pltpu.VMEM((length, PAIR), jnp.float32)] * 2,
        compiler_params=params(20),
        cost_estimate=cost(24 * tokens * length * width, 8 * tokens * width, tokens * length * width // 200),
    )(*[parts] * 4, cosine, sine, segments[:, None, :], segments.reshape(tokens, 1), *before)


def put_out(staged, keep, send, done):
    half = keep.shape[0]
    copies = [
        pltpu.make_async_copy(staged.at[pl.ds(n * half, half)], target, done.at[n])
        for n, target in enumerate((keep, send))
    ]
    for copy in copies:
        copy.start()
    for copy in copies:
        copy.wait()


def attention_grads_kernel(place, *refs):
    normed, d_mixed = refs[:2]
    more = refs[2:-7]
    keep, send, sums, totals, proj_total, staged, done = refs[-7:]
    step, last = pl.program_id(0), pl.num_programs(0) - 1
    width = d_mixed.shape[-1]
    chips = staged.shape[0]
    parts = totals.shape[0]
    rows = totals.shape[1] // chips

    @pl.when(step == 0)
    def _():
        totals[...] = jnp.zeros_like(totals)
        sums[...] = jnp.zeros_like(sums)
        if more:
            proj_total[...] = jnp.zeros_like(proj_total)

    for part in range(parts):
        totals[part] += mul(normed[...], d_mixed[part], TN)
        sums[part] += jnp.sum(d_mixed[part].astype(jnp.float32), axis=0, keepdims=True)
    if more:
        for n, attended in enumerate(more[:2]):
            proj_total[n * width : (n + 1) * width, :] += mul(attended[...], more[2][...], TN)

    @pl.when(step == last)
    def _():
        for chip in range(chips):
            spot = place[chip]
            for part in range(parts):
                change = totals[part, chip * rows : (chip + 1) * rows, :]
                staged[spot, part * rows : (part + 1) * rows, :] = change.astype(staged.dtype)
            if more:
                below = proj_total.shape[0] // chips
                for n in range(4):
                    change = proj_total[chip * below : (chip + 1) * below, n * width : (n + 1) * width]
                    start = parts * rows + n * below
                    staged[spot, start : start + below, :] = change.astype(staged.dtype)
        put_out(staged, keep, send, done)


def attention_grads(place, normed, d_mixed, more):
    tokens, model = normed.shape
    parts, _, width = d_mixed.shape
    chips = place.shape[0]
    rows = parts * model // chips + (4 * 2 * width // chips if more else 0)
    token = lambda n: pl.BlockSpec((TOKENS, n), lambda i, *_: (i, 0))
    half = jax.ShapeDtypeStruct((chips // 2, rows, width), jnp.bfloat16)
    anywhere = pl.BlockSpec(memory_space=pl.ANY)
    return pl.pallas_call(
        attention_grads_kernel,
        grid_spec=pltpu.PrefetchScalarGridSpec(
            num_scalar_prefetch=1,
            grid=(tokens // TOKENS,),
            in_specs=[token(model), pl.BlockSpec((parts, TOKENS, width), lambda i, *_: (0, i, 0))]
            + ([token(width), token(width), token(model)] if more else []),
            out_specs=[anywhere, anywhere, pl.BlockSpec((parts, 1, width), lambda i, *_: (0, 0, 0))],
            scratch_shapes=[
                pltpu.VMEM((parts, model, width), jnp.float32),
                pltpu.VMEM((2 * width, model), jnp.float32),
                pltpu.VMEM((chips, rows, width), jnp.bfloat16),
                pltpu.SemaphoreType.DMA((2,)),
            ],
        ),
        out_shape=[half, half, jax.ShapeDtypeStruct((parts, 1, width), jnp.float32)],
        compiler_params=params(60 if more else 26),
        cost_estimate=cost(8 * tokens * model * width, 6 * tokens * model),
    )(place, normed, d_mixed, *more)


def share_out(step, steps, earlier, mine, sends, value):
    each = steps // 2 // len(sends)
    for start, end, ref, more in [(0, steps // 2, mine, earlier[:1])] + [
        (steps // 2 + n * each, steps // 2 + (n + 1) * each, send, earlier[1:]) for n, send in enumerate(sends)
    ]:

        @pl.when((step >= start) & (step < end))
        def _():
            total = value
            for one in more:
                total = total + one[...].astype(jnp.float32)
            ref[...] = total.astype(ref.dtype)


def attention_back_kernel(half, pieces, place, d_mixed, attended, *refs):
    count = 2 * (1 + pieces) + 2
    weights, before, results = refs[:8], refs[8:-count], refs[-count:-2]
    ordered, ordered_proj = refs[-2:]
    step, steps = pl.program_id(0), pl.num_programs(0)

    @pl.when(step == 0)
    def _():
        arrange(place, half, weights, ordered, ordered_proj)

    change = jnp.concatenate([d_mixed[part] for part in range(3)], axis=1)
    share_out(step, steps, before[:2], results[0], results[1 : 1 + pieces], mul(change, ordered[...], NT))
    share_out(step, steps, before[2:], results[1 + pieces], results[2 + pieces :], mul(attended[...], ordered_proj[...], NN))


def attention_back(half, pieces, place, d_mixed, attended, weights, first, proj, before):
    parts, tokens, width = d_mixed.shape
    model = 128 * weights[0].shape[0]
    steps = tokens // TOKENS
    own = pl.BlockSpec((TOKENS, model), lambda i, *_: (jnp.minimum(i, steps // 2 - 1), 0))
    other = pl.BlockSpec((TOKENS, model), lambda i, *_: (jnp.maximum(i - steps // 2, 0), 0))
    each = steps // 2 // pieces
    shape = lambda n: jax.ShapeDtypeStruct((n * TOKENS, model), jnp.bfloat16)
    sent = [
        pl.BlockSpec((TOKENS, model), lambda i, *_, n=n: (jnp.clip(i - steps // 2 - n * each, 0, each - 1), 0))
        for n in range(pieces)
    ]
    return pl.pallas_call(
        partial(attention_back_kernel, half, pieces),
        grid_spec=pltpu.PrefetchScalarGridSpec(
            num_scalar_prefetch=1,
            grid=(steps,),
            in_specs=[
                pl.BlockSpec((parts, TOKENS, width), lambda i, *_: (0, i, 0)),
                pl.BlockSpec((TOKENS, width), lambda i, *_: (i, 0)),
            ]
            + weight_specs(weights, first)
            + [own, other] * (len(before) // 2),
            out_specs=([own] + sent) * 2,
            scratch_shapes=weight_scratch(weights),
        ),
        out_shape=([shape(steps // 2)] + [shape(each)] * pieces) * 2,
        compiler_params=params(60),
        cost_estimate=cost(8 * tokens * model * width, 8 * tokens * model),
    )(place, d_mixed, attended, *weights * 3, *proj, *before)


def forward_kernel(place, normed, grads, near, far, bias, *refs):
    earlier, refs = refs[:-18], refs[-18:]
    keep, send, sums = refs[:3]
    outs = refs[3:7]
    own_normed, own_grads, up, down, after, d_before, results, staged, arrived, shared, left = refs[7:18]
    tokens, model = own_normed.shape
    hidden = up.shape[1]
    half_tokens = tokens // 2
    rows = near.shape[1] // 2
    chips = 2 * near.shape[0]
    blocks = tokens // ROWS

    def pieces(chip):
        at = pl.ds(chip * rows, rows)
        return ((0, up.at[at], 2 * chip), (rows, down.at[at], 2 * chip + 1))

    def row_loads(block):
        at = pl.ds(block * ROWS, ROWS)
        return [
            pltpu.make_async_copy(source.at[at], target.at[at], arrived.at[2 * chips + 2 * block + n])
            for n, (source, target) in enumerate(((normed, own_normed), (grads, own_grads)))
        ]

    loads = [pltpu.make_async_copy(ref, results.at[n], shared.at[n]) for n, ref in enumerate(earlier)]
    for chip in range(chips):
        spot = place[chip]
        for start, target, n in pieces(chip):
            for own, source in ((True, near), (False, far)):

                @pl.when((spot < chips // 2) == own)
                def _():
                    held = source.at[spot % (chips // 2), pl.ds(start, rows)]
                    pltpu.make_async_copy(held, target, arrived.at[n]).start()

    for block in range(blocks):
        for load in row_loads(block):
            load.start()
    for load in loads:
        load.start()
    for chip in range(chips):
        for start, target, n in pieces(chip):
            pltpu.make_async_copy(near.at[0, pl.ds(start, rows)], target, arrived.at[n]).wait()
    offset = bias[...].astype(jnp.float32)
    bias_total = jnp.zeros_like(offset)
    for block in range(blocks):
        at = slice(block * ROWS, (block + 1) * ROWS)
        for load in row_loads(block):
            load.wait()
        before = mul(own_normed[at, :], up[...], NN) + offset
        change = mul(own_grads[at, :], down[...], NT)
        share = 0.5 + 0.5 * lax.erf(before * 0.7071067811865476)
        density = jnp.exp(-0.5 * before * before) * 0.3989422804014327
        after[at, :] = (before * share).astype(after.dtype)
        low = (change * (share + before * density)).astype(d_before.dtype)
        d_before[at, :] = low
        bias_total += jnp.sum(low.astype(jnp.float32), axis=0, keepdims=True)
    sums[...] = bias_total
    for load in loads:
        load.wait()
    stores = []
    for block in range(blocks):
        at = slice(block * ROWS, (block + 1) * ROWS)
        side = 0 if block * ROWS < half_tokens else 1
        own = pl.ds(block * ROWS - side * half_tokens, ROWS)
        for which, value in enumerate((mul(after[at, :], down[...], NN), mul(d_before[at, :], up[...], NT))):
            n = 2 * which + side
            if n < len(earlier):
                value += results[n, own, :].astype(jnp.float32)
            results[n, own, :] = value.astype(results.dtype)
            store = pltpu.make_async_copy(results.at[n, own], outs[n].at[own], left.at[2 + 2 * block + which])
            store.start()
            stores.append(store)
    tile = 256
    for start in range(0, hidden, tile):
        change = mul(own_normed[...], d_before[:, start : start + tile], TN).astype(staged.dtype)
        for chip in range(chips):
            staged[place[chip], :rows, start : start + tile] = change[chip * rows : (chip + 1) * rows]
        change = mul(after[:, start : start + tile], own_grads[...], TN).astype(staged.dtype)
        for n in range(tile // rows):
            staged[place[start // rows + n], rows:, :] = change[n * rows : (n + 1) * rows]
    half = keep.shape[0]
    for n, target in enumerate((keep, send)):
        store = pltpu.make_async_copy(staged.at[pl.ds(n * half, half)], target, left.at[n])
        store.start()
        stores.append(store)
    for store in stores:
        store.wait()


def forward_chunk(place, normed, grads, weights, bias, earlier):
    tokens, model = normed.shape
    chips, both_rows, hidden = weights[0].shape
    chips *= 2
    low = lambda *shape: pltpu.VMEM(shape, jnp.bfloat16)
    blocks = jax.ShapeDtypeStruct((chips // 2, both_rows, model), jnp.bfloat16)
    anywhere = pl.BlockSpec(memory_space=pl.ANY)
    share = jax.ShapeDtypeStruct((tokens // 2, model), jnp.bfloat16)
    small = pl.BlockSpec((1, hidden), lambda i, *_: (0, 0))
    counts = (2 * chips + 2 * (tokens // ROWS), 4, 2 + 2 * (tokens // ROWS))
    return pl.pallas_call(
        forward_kernel,
        grid_spec=pltpu.PrefetchScalarGridSpec(
            num_scalar_prefetch=1,
            grid=(1,),
            in_specs=[anywhere] * 4 + [small] + [anywhere] * len(earlier),
            out_specs=[anywhere, anywhere, small] + [anywhere] * 4,
            scratch_shapes=[
                low(tokens, model),
                low(tokens, model),
                low(model, hidden),
                low(hidden, model),
                low(tokens, hidden),
                low(tokens, hidden),
                low(4, tokens // 2, model),
                low(chips, both_rows, model),
            ]
            + [pltpu.SemaphoreType.DMA((count,)) for count in counts],
        ),
        out_shape=[blocks, blocks, jax.ShapeDtypeStruct((1, hidden), jnp.float32)] + [share] * 4,
        compiler_params=params(44),
        cost_estimate=cost(12 * tokens * model * hidden, 16 * tokens * model, 2 * tokens * hidden),
    )(place, normed, grads, *weights, bias, *earlier)


def both_of(left, *right):
    come = right[0][...]
    if len(right) > 1:
        come = jnp.where(pl.program_id(0) < pl.num_programs(0) // 2, come, right[1][...])
    return left[...].astype(jnp.float32) + come.astype(jnp.float32)


def finish_out_kernel(hidden, mine, come, scales, layer_out):
    table = scales[...].astype(jnp.float32)
    total = both_of(mine, come) + table[0:1] + table[1:2]
    layer_out[...] = (hidden[...].astype(jnp.float32) + total).astype(layer_out.dtype)


def finish_grad_kernel(hidden, grads, one_mine, one_come, two_mine, two_come, scales, input_grad, sums):
    value = hidden[...].astype(jnp.float32)
    cotangent = grads[...].astype(jnp.float32)
    table = scales[...].astype(jnp.float32)
    center = value - jnp.mean(value, axis=1, keepdims=True)
    scale = lax.rsqrt(jnp.mean(center * center, axis=1, keepdims=True) + norm_eps)
    hat = center * scale
    one, two = middle_swap(both_of(one_mine, one_come)), middle_swap(both_of(two_mine, two_come))
    gained = one * table[0:1] + two * table[1:2]
    mean = jnp.mean(gained, axis=1, keepdims=True)
    slope = jnp.mean(gained * hat, axis=1, keepdims=True)
    input_grad[...] = (cotangent + (gained - mean - hat * slope) * scale).astype(input_grad.dtype)

    @pl.when(pl.program_id(0) == 0)
    def _():
        sums[...] = jnp.zeros_like(sums)

    for row, column in enumerate((one * hat, one, two * hat, two, cotangent)):
        sums[row : row + 1, :] += jnp.sum(column, axis=0, keepdims=True)


def finish(kernel, arrays, scales, with_sums):
    length, width = arrays[0].shape
    block = pl.BlockSpec((ROWS, width), lambda i: (i, 0))
    steps, specs = length // ROWS, []
    for array in arrays:
        if isinstance(array, tuple):
            specs.append(pl.BlockSpec((ROWS, width), lambda i: (jnp.minimum(i, steps // 2 - 1), 0)))
            specs.append(pl.BlockSpec((ROWS, width), lambda i: (jnp.maximum(i - steps // 2, 0), 0)))
        else:
            specs.append(block)
    arrays = jax.tree.leaves(arrays)
    shape = jax.ShapeDtypeStruct((length, width), jnp.bfloat16)
    more = [pl.BlockSpec((8, width), lambda i: (0, 0))] if with_sums else []
    return pl.pallas_call(
        kernel,
        grid=(length // ROWS,),
        in_specs=specs + [fixed(scales.shape)],
        out_specs=[block] + more,
        out_shape=[shape] + [jax.ShapeDtypeStruct((8, width), jnp.float32)] * len(more),
        compiler_params=params(60),
        cost_estimate=cost(40 * length * width, 2 * (len(arrays) + 1) * length * width),
    )(*arrays, scales)


def by_core(core, mine, come):
    return jnp.where(core == 0, mine, come), jnp.where(core == 0, come, mine)


def qkv_rows_kernel(core, mine_one, come_one, mine_two, come_two, out):
    parts, _, width = mine_one.shape
    for part in range(parts):
        for half, (mine, come) in enumerate(((mine_one, come_one), (mine_two, come_two))):
            even, odd = by_core(core[0], mine[part], come[part])
            for head in range(width // HEAD):
                at = slice(head * HEAD, (head + 1) * HEAD)
                start = (part * 2 + half) * 2 * width + head * PAIR
                out[:, start : start + PAIR] = jnp.concatenate([even[:, at], odd[:, at]], axis=1)


def up_rows_kernel(core, mine_one, come_one, mine_two, come_two, out):
    width = mine_one.shape[2]
    first, second = by_core(core[0], mine_one[0], come_one[0]), by_core(core[0], mine_two[0], come_two[0])
    for chip in range(width // 64):
        at = slice(chip * 64, (chip + 1) * 64)
        for which in range(2):
            start = ((chip // 2) * 2 + which) * 256 + (chip % 2) * 128
            out[:, start : start + 128] = jnp.concatenate([first[which][:, at], second[which][:, at]], axis=1)


def whole_rows(kernel, core, halves, shape):
    operands = [array for half in halves for array in half]
    return pl.pallas_call(
        kernel,
        grid_spec=pltpu.PrefetchScalarGridSpec(
            num_scalar_prefetch=1,
            grid=(1,),
            in_specs=[fixed(array.shape) for array in operands],
            out_specs=pl.BlockSpec(shape, lambda i, *_: (0, 0)),
        ),
        out_shape=jax.ShapeDtypeStruct(shape, jnp.float32),
        compiler_params=params(16),
        cost_estimate=cost(0, 16 * shape[0] * shape[1]),
    )(core, *operands)


BITS = {"y": 0, "core": 1, "x": 2, "z_low": 3, "z_high": 4}
SPLIT = ("zx", "core", "y")
CORES = ("core", "core")
STAGES = (("x", "y"), ("y", "x"), ("z_low", "z_low"), ("z_high", "z_high"))


class Pairs:
    def __init__(self, total):
        self.total = total

    def here(self):
        y = lax.axis_size("y")
        return (lax.axis_index("zx") * 2 + lax.axis_index("core")) * y + lax.axis_index("y")

    def bit(self, name):
        return (self.here() >> BITS[name]) & 1

    def swap(self, value, names):
        moves = []
        for device in range(self.total):
            name = names[(device >> BITS["core"]) & 1]
            moves.append((device, device ^ (1 << BITS[name])))
        return lax.ppermute(value, SPLIT, moves)

    def places(self):
        chip = jnp.arange(self.total // 2, dtype=jnp.int32)
        bits = {"y": chip & 1, "x": (chip >> 1) & 1, "z_low": (chip >> 2) & 1, "z_high": (chip >> 3) & 1}
        differs = {name: bits[name] ^ self.bit(name) for name in bits}
        place = jnp.zeros_like(chip)
        for first, second in STAGES:
            place = 2 * place + jnp.where(lax.axis_index("core") == 0, differs[first], differs[second])
        return place


class Sum:
    def __init__(self, pairs, keep, send):
        self.pairs, self.arrays, self.stage = pairs, (keep, send), 0

    def ready(self, arrays):
        if self.stage == 0:
            return arrays
        keep, come = arrays
        half = keep.shape[0] // 2
        return add_low(keep[:half], come[:half]), add_low(keep[half:], come[half:])

    def move(self, arrays):
        keep, send = arrays
        self.arrays = keep, self.pairs.swap(send, STAGES[self.stage])
        self.stage += 1

    def result(self):
        keep, come = self.arrays
        return keep[0].astype(jnp.float32) + come[0].astype(jnp.float32)


class Gather:
    def __init__(self, pairs, own):
        self.pairs, self.arrays, self.stage = pairs, (own[None],), 0

    def ready(self, arrays):
        return arrays if self.stage == 0 else (jnp.concatenate(arrays),)

    def move(self, arrays):
        self.stage += 1
        self.arrays = arrays[0], self.pairs.swap(arrays[0], STAGES[-self.stage])

    def result(self):
        return self.arrays


class Trade:
    def __init__(self, pairs, *arrays):
        self.pairs, self.arrays, self.stage = pairs, arrays, 0

    def ready(self, arrays):
        return arrays

    def move(self, arrays):
        if self.stage == 0:
            arrays = tuple(self.pairs.swap(array, CORES) for array in arrays)
        self.arrays = arrays
        self.stage += 1

    def result(self):
        return self.arrays


def hold(value, tasks):
    value, arrays = lax.optimization_barrier((value, [task.arrays for task in tasks]))
    for task, own in zip(tasks, arrays):
        task.arrays = tuple(own)
    return value


def tick(after, value, *tasks, done=()):
    if after is not None:
        after = hold(after, tasks + tuple(done))
    for task in tasks:
        task.arrays = task.ready(task.arrays)
    after, value = hold((after, value), tasks)
    for task in tasks:
        task.move(task.arrays)
    return after, value


def add_low(left, right):
    return (left.astype(jnp.float32) + right.astype(jnp.float32)).astype(jnp.bfloat16)


def wide_angles(segments):
    position = lax.broadcasted_iota(jnp.int32, segments.shape, 1)
    change = jnp.concatenate([jnp.ones_like(segments[:, :1], jnp.bool_), segments[:, 1:] != segments[:, :-1]], axis=1)
    place = position - lax.cummax(jnp.where(change, position, 0), axis=1)
    lane = jnp.arange(PAIR) % HEAD
    half = ROT // 2
    freqs = 10000.0 ** (-((lane % half) * 2).astype(jnp.float32) / ROT)
    freqs = jnp.where(lane < ROT, freqs, 0.0)
    theta = place.reshape(-1, 1).astype(jnp.float32) * freqs
    return jnp.cos(theta), jnp.sin(theta) * jnp.where(lane < half, -1.0, 1.0)


def pick(value, which, axis):
    return lax.dynamic_index_in_dim(value, which, axis, keepdims=False)


def paired_body(
    pairs,
    hidden_in,
    segment_ids,
    out_grad,
    norm1_gain,
    norm1_bias,
    norm2_gain,
    norm2_bias,
    qkv_weight,
    qkv_bias,
    proj_weight,
    proj_bias,
    up_weight,
    up_bias,
    down_weight,
    down_bias,
):
    core = lax.axis_index("core")
    heads = HEADS // 2
    rows, model = qkv_weight.shape[0], proj_weight.shape[1]
    width = heads * HEAD // 2
    unit = down_weight.shape[0] // 2
    hidden, grads = hidden_in[0], out_grad[0]

    def columns(which):
        taken = pick(qkv_weight.reshape(rows, 3, heads, 2, HEAD), which, 3).reshape(rows, 3 * 2 * width)
        more = pick(up_weight.reshape(rows, heads, 2, 2, 2, unit), which, 2).transpose(0, 3, 1, 2, 4).reshape(rows, -1)
        return jnp.concatenate([taken, more], axis=1)

    theirs = pairs.swap(columns(1 - core), CORES)
    mine = columns(core)
    both = jnp.where(core == 0, jnp.stack([mine, theirs]), jnp.stack([theirs, mine])).reshape(2 * rows, -1)
    low_qkv = both[:, : 6 * width].reshape(2 * rows, 3, 2, width).transpose(2, 1, 0, 3)
    low_proj = proj_weight.reshape(rows, 4, width).transpose(1, 0, 2).reshape(2, 2 * rows, width)
    low_up = both[:, 6 * width :].reshape(2 * rows, 2, -1).transpose(1, 0, 2)
    low_down = down_weight.reshape(2, unit, model)

    other, other_grads = pairs.swap(hidden, CORES), pairs.swap(grads, CORES)
    segments = jnp.concatenate([segment_ids, pairs.swap(segment_ids, CORES)])
    column = segments.reshape(-1, 1)
    cosine, sine = wide_angles(segments)
    place = pairs.places()

    small = (norm1_gain, norm1_bias, norm2_gain, norm2_bias, qkv_bias, proj_bias, up_bias, down_bias)
    ends = [sum(entry.shape[0] for entry in small[: n + 1]) for n in range(len(small))]
    long = ends[-1] + -ends[-1] % 128
    line = sum(jnp.pad(entry, (end - entry.shape[0], long - end)) for entry, end in zip(small, ends))
    come = pairs.swap(line, CORES)
    lines = Gather(pairs, jnp.where(core == 0, jnp.stack([line, come]), jnp.stack([come, line])).reshape(-1))
    first = Gather(pairs, jnp.concatenate([low_proj, low_qkv[0]]).reshape(-1, width))
    chunks = [Gather(pairs, jnp.concatenate([low_up[h], low_down[h]])) for h in range(2)]
    second = Gather(pairs, low_qkv[1].reshape(-1, width))
    tick(None, (), first, lines)
    tick(None, (), lines)
    tick(None, (), first, lines)
    tick(None, (), lines)
    table = jnp.concatenate(lines.result())[place]
    table = table.reshape(heads, 2, 2, -1).swapaxes(1, 2).reshape(pairs.total, -1)
    spread, at = [], 0
    for entry in small:
        size = entry.shape[0]
        spread.append(table[:, at : at + size].reshape(-1))
        at += size
    gain_one, shift_one, gain_two, shift_two, b_qkv, b_proj, b_up, b_down = spread
    own_bias = pick(b_qkv.reshape(3, heads, 2, HEAD), core, 2).reshape(3, 2, 1, width)
    own_up_bias = pick(b_up.reshape(heads, 2, 2, 2, unit), core, 1).transpose(2, 0, 1, 3).reshape(2, 1, -1)
    scales = jnp.stack([gain_one, shift_one, gain_two, shift_two])
    scales = scales.reshape(4, -1, 2, 2, rows).swapaxes(2, 3).reshape(4, model)
    _, scales = tick(None, scales, first)
    before = norms(0, hidden, grads, scales, ())
    before, (scales, segments) = tick(before, (scales, segments), first, chunks[0])
    column = segments.reshape(-1, 1)
    cosine, sine = wide_angles(segments)
    normed_one, normed_two, both_grads = norms(1, other, other_grads, scales, before)
    (normed_one, cosine, sine), _ = tick((normed_one, cosine, sine), (), chunks[0], done=(first,))
    w_first = first.result()

    parts = project(
        0, place, normed_one, both_grads, w_first, 2, w_first, own_bias[:, 0], cosine, sine, column
    )
    parts, _ = tick(parts, (), chunks[0], chunks[1])
    before = attention(0, parts, cosine, sine, segments, ())
    before, parts = tick(before, parts, chunks[0], chunks[1])
    attended_one, d_mixed = attention(1, parts, cosine, sine, segments, before)
    (attended_one, d_mixed), _ = tick((attended_one, d_mixed), (), chunks[1], second)
    keep, send, qkv_sums_one = attention_grads(place, normed_one, d_mixed, ())
    sum_one = Sum(pairs, keep, send)
    qkv_sums_one, d_mixed = tick(qkv_sums_one, d_mixed, sum_one, second)
    d1, d1_send, out, out_send = attention_back(0, 1, place, d_mixed, attended_one, w_first, 2, w_first, ())

    sum_forward, up_sums = [], []
    before = (out, out_send)
    for chunk in range(2):
        more = [] if chunk else chunks[1:]
        before, normed_two = tick(before, normed_two, *more, sum_one, second, *sum_forward, done=(chunks[chunk],))
        keep, send, sums, *before = forward_chunk(
            place,
            normed_two,
            both_grads,
            chunks[chunk].result(),
            own_up_bias[chunk],
            before,
        )
        up_sums.append(sums)
        sum_forward.append(Sum(pairs, keep, send))
    out, out_send, d2, d2_send = before

    (out, out_send, d2_send), normed_one = tick(
        (out, out_send, d2_send), normed_one, sum_one, sum_forward[0], done=(second,)
    )
    w_second = second.result()
    trade_two = Trade(pairs, d2_send)
    parts = project(
        1, place, normed_one, both_grads, w_second, 0, w_first, own_bias[:, 1], cosine, sine, column
    )
    parts, _ = tick(parts, (), sum_forward[0], sum_forward[1], trade_two, done=(sum_one,))
    before = attention(0, parts, cosine, sine, segments, ())
    before, parts = tick(before, parts, sum_forward[0], done=(trade_two,))
    attended_two, d_mixed = attention(1, parts, cosine, sine, segments, before)
    (attended_two, d_mixed), _ = tick((attended_two, d_mixed), (), sum_forward[1], done=sum_forward[:1])
    d1, d1_send, out, out_send = attention_back(
        1, 1, place, d_mixed, attended_two, w_second, 0, w_first, (d1, d1_send, out, out_send)
    )
    trade = Trade(pairs, d1_send, out_send)
    (d1, out), d_mixed = tick((d1, out), d_mixed, sum_forward[1], trade)
    keep, send, qkv_sums_two = attention_grads(place, normed_one, d_mixed, (attended_one, attended_two, both_grads))
    sum_two = Sum(pairs, keep, send)
    (qkv_sums_two, d1, out), _ = tick((qkv_sums_two, d1, out), (), sum_two, done=(trade,))
    d1_come, out_come = trade.result()
    input_grad, sums = finish(
        finish_grad_kernel,
        [hidden, grads, d1, d1_come, d2, *trade_two.result()],
        jnp.stack([gain_one, gain_two]),
        True,
    )
    (input_grad, sums, qkv_sums_one, qkv_sums_two, up_sums), _ = tick(
        (input_grad, sums, qkv_sums_one, qkv_sums_two, up_sums), (), sum_two, sum_forward[1]
    )
    def both_cores(own):
        own = own[:, None]
        none = jnp.zeros_like(own)
        return jnp.where(core == 0, jnp.concatenate([own, none], axis=1), jnp.concatenate([none, own], axis=1)).reshape(-1)

    def halve(table, name):
        upper = pairs.bit(name) == 1
        half = table.shape[0] // 2
        send = jnp.where(upper, table[:half], table[half:])
        return jnp.where(upper, table[half:], table[:half]) + pairs.swap(send, (name, name))

    sum_qkv = jnp.stack([qkv_sums_one.reshape(3, -1), qkv_sums_two.reshape(3, -1)], axis=1)
    sum_up = jnp.stack([entry.reshape(heads, 2, unit) for entry in up_sums], axis=2)
    entries = [
        sums[0],
        sums[1],
        sums[2],
        sums[3],
        both_cores(sum_qkv.reshape(-1, HEAD)),
        sums[4],
        both_cores(sum_up.reshape(heads, -1)),
    ]
    table = jnp.concatenate([entry.reshape(pairs.total, -1) for entry in entries], axis=1)
    table = jnp.pad(table, ((0, 0), (0, -table.shape[1] % 128)))
    names = list(reversed(BITS))
    for name in names[:1]:
        table = halve(table, name)
    table, out = tick(table, out, sum_two)
    layer_out = finish(finish_out_kernel, [hidden, out, out_come], jnp.stack([b_proj, b_down]), False)[0]
    table = halve(halve(table, names[1]), names[2])
    (table, layer_out), _ = tick((table, layer_out), (), sum_two, done=(sum_one, *sum_forward))
    for name in names[3:]:
        table = halve(table, name)
    low_qkv_one, low_qkv_two = sum_one.result(), sum_two.result()
    low_forward = [task.result() for task in sum_forward]

    def trade_rows(value):
        split = value.reshape(value.shape[0], 2, rows, -1)
        return pick(split, core, 1), pairs.swap(pick(split, 1 - core, 1), CORES)

    which = core.astype(jnp.int32).reshape(1)
    low = (low_qkv_one.reshape(3, 2 * rows, width), low_qkv_two[: 6 * rows].reshape(3, 2 * rows, width))
    grad_qkv = whole_rows(qkv_rows_kernel, which, [trade_rows(value) for value in low], qkv_weight.shape)
    grad_proj = low_qkv_two[6 * rows :].reshape(4, rows, width).transpose(1, 0, 2).reshape(rows, model)
    ups = [trade_rows(entry[: 2 * rows].reshape(1, 2 * rows, -1)) for entry in low_forward]
    grad_up = whole_rows(up_rows_kernel, which, ups, up_weight.shape)
    grad_down = jnp.concatenate([entry[2 * rows :] for entry in low_forward])
    outs, at = [], 0
    for entry in entries:
        size = entry.shape[0] // pairs.total
        outs.append(table[0, at : at + size])
        at += size
    return (
        layer_out[None],
        input_grad[None],
        outs[0],
        outs[1],
        outs[2],
        outs[3],
        grad_qkv,
        outs[4],
        grad_proj,
        outs[5],
        grad_up,
        outs[6],
        grad_down,
        outs[5],
    )


def placed(axes):
    rows, flat = P(axes, None), P(axes)
    whole = P(axes, None, None)
    inside = (whole, rows, whole) + (flat,) * 4 + (rows, flat) * 4
    outside = (whole, whole) + (flat,) * 4 + (rows, flat) * 4
    return inside, outside


def solution(mesh):
    dp, fsdp = mesh.shape["dp"], mesh.shape["fsdp"]
    if (dp, fsdp) == (16, 2):
        split = Mesh(mesh.devices.reshape(dp // 2, 2, fsdp), SPLIT)
        inside, outside = placed(SPLIT)
        step = partial(paired_body, Pairs(dp * fsdp))
        return jax.shard_map(step, mesh=split, in_specs=inside, out_specs=outside, check_vma=False)
    inside, outside = placed(AXES)
    step = partial(body, Grid((dp, fsdp)))
    return jax.shard_map(step, mesh=mesh, in_specs=inside, out_specs=outside, check_vma=False)
```

```python
from functools import partial

import jax
import jax.numpy as jnp
from jax import lax
from jax.experimental import pallas as pl
from jax.experimental.pallas import tpu as pltpu
from jax.sharding import Mesh
from jax.sharding import PartitionSpec as P

AXES = ("dp", "fsdp")

HEADS = 16
HEAD = 64
ROT = 16
DOCS = 8


norm_eps = 1e-05
masked_score = -1e30


def normed(values, gain):
    center = values - jnp.mean(values, axis=-1, keepdims=True)
    spread = jnp.mean(center * center, axis=-1, keepdims=True)
    return center * lax.rsqrt(spread + norm_eps) * gain


def rotate(part, cosine, sine):
    half_rot = ROT // 2
    first = part[..., :half_rot]
    second = part[..., half_rot:ROT]
    cos_wide = cosine[..., None, :]
    sin_wide = sine[..., None, :]
    return jnp.concatenate(
        [
            first * cos_wide - second * sin_wide,
            second * cos_wide + first * sin_wide,
            part[..., ROT:],
        ],
        axis=-1,
    )


def angles(segments):
    last_axis = segments.ndim - 1
    position = lax.broadcasted_iota(jnp.int32, segments.shape, last_axis)
    change = jnp.concatenate(
        [jnp.ones(segments.shape[:-1] + (1,), jnp.bool_), segments[..., 1:] != segments[..., :-1]],
        axis=-1,
    )
    first_index = lax.cummax(jnp.where(change, position, jnp.zeros_like(position)), axis=last_axis)
    place = (position - first_index).astype(jnp.float32)
    freqs = 10000.0 ** (-(jnp.arange(ROT // 2) * 2).astype(jnp.float32) / ROT)
    theta = place[..., None] * freqs
    return (jnp.cos(theta), jnp.sin(theta))


def block_mask(segments, block_start, block_rows):
    length = segments.shape[0]
    query_pos = block_start + lax.broadcasted_iota(jnp.int32, (block_rows, length), 0)
    key_pos = lax.broadcasted_iota(jnp.int32, (block_rows, length), 1)
    same = segments[block_start : block_start + block_rows][:, None] == segments[None, :]
    return ((key_pos <= query_pos) & same)[None]


def attend_forward(pieces):
    query, keys, values, segments = pieces
    length = segments.shape[0]
    block_rows = min(512, length)
    outputs = []
    log_sums = []
    for block_start in range(0, length, block_rows):
        allowed = block_mask(segments, block_start, block_rows)
        scores = jnp.einsum(
            "qhe,khe->hqk",
            query[block_start : block_start + block_rows],
            keys,
            preferred_element_type=jnp.float32,
        )
        scores = jnp.where(allowed, scores, masked_score)
        row_max = jnp.max(scores, axis=-1, keepdims=True)
        exponent = jnp.exp(scores - row_max)
        total = jnp.sum(exponent, axis=-1, keepdims=True)
        weights = (exponent / total).astype(jnp.bfloat16)
        outputs.append(
            jnp.einsum("hqk,khe->qhe", weights, values, preferred_element_type=jnp.float32)
        )
        log_sums.append(row_max + jnp.log(total))
    return (jnp.concatenate(outputs, axis=0), jnp.concatenate(log_sums, axis=1))


def attend_backward(pieces):
    query, keys, values, segments, log_sums, d_out = pieces
    length = segments.shape[0]
    block_rows = min(512, length)
    query_parts = []
    d_keys = jnp.zeros(keys.shape, jnp.float32)
    d_values = jnp.zeros(values.shape, jnp.float32)
    for block_start in range(0, length, block_rows):
        block_end = block_start + block_rows
        allowed = block_mask(segments, block_start, block_rows)
        scores = jnp.einsum(
            "qhe,khe->hqk", query[block_start:block_end], keys, preferred_element_type=jnp.float32
        )
        scores = jnp.where(allowed, scores, masked_score)
        probs = jnp.exp(scores - log_sums[:, block_start:block_end])
        d_probs = jnp.einsum(
            "qhe,khe->hqk", d_out[block_start:block_end], values, preferred_element_type=jnp.float32
        )
        inner = jnp.sum(d_probs * probs, axis=-1, keepdims=True)
        d_scores = (probs * (d_probs - inner)).astype(jnp.bfloat16)
        d_values = d_values + jnp.einsum(
            "hqk,qhe->khe",
            probs.astype(jnp.bfloat16),
            d_out[block_start:block_end],
            preferred_element_type=jnp.float32,
        )
        query_parts.append(
            jnp.einsum("hqk,khe->qhe", d_scores, keys, preferred_element_type=jnp.float32)
        )
        d_keys = d_keys + jnp.einsum(
            "hqk,qhe->khe",
            d_scores,
            query[block_start:block_end],
            preferred_element_type=jnp.float32,
        )
    return (jnp.concatenate(query_parts, axis=0), d_keys, d_values)


class Grid:
    def __init__(self, sizes):
        dp, fsdp = sizes
        self.total = dp * fsdp
        self.low = fsdp.bit_length() - 1
        self.bits = self.total.bit_length() - 1
        self.core = self.low
        self.x = self.low + 1
        self.y = self.low - 1
        stages = [(self.core, self.core), (self.x, self.y), (self.y, self.x)]
        stages += [(b, b) for b in range(self.low - 2, -1, -1)]
        stages += [(b, b) for b in range(self.x + 1, self.bits)]
        self.stages = stages

    def here(self):
        return lax.axis_index("dp") * (1 << self.low) + lax.axis_index("fsdp")

    def pairs(self, stage):
        found = []
        for device in range(self.total):
            bit = stage[(device >> self.core) & 1]
            found.append((device, device ^ (1 << bit)))
        return found

    def swap(self, value, stage):
        return lax.ppermute(value, AXES, self.pairs(stage))

    def plan(self, step):
        here = self.here()
        core = (here >> self.core) & 1
        chosen = []
        for which in (0, 1):
            bit = self.stages[step][which]
            gone = [s[which] for s in self.stages[:step]]
            chosen.append((bit - sum(1 for g in gone if g < bit), (here >> bit) & 1))
        place = jnp.where(core == 0, chosen[0][0], chosen[1][0])
        value = jnp.where(core == 0, chosen[0][1], chosen[1][1])
        return jnp.stack([place, value]).astype(jnp.int32)


def insert_bit(index, place, value):
    low = index & ((1 << place) - 1)
    return ((index >> place) << (place + 1)) | (value << place) | low


def split_kernel(plan, own_keep, own_send, keep, send):
    keep[...] = own_keep[...]
    send[...] = own_send[...]


def join_kernel(plan, own_keep, own_send, come_keep, come_send, keep, send):
    keep[...] = (own_keep[...].astype(jnp.float32) + come_keep[...].astype(jnp.float32)).astype(keep.dtype)
    send[...] = (own_send[...].astype(jnp.float32) + come_send[...].astype(jnp.float32)).astype(send.dtype)


def last_kernel(own, come, out):
    out[...] = own[...].astype(jnp.float32) + come[...].astype(jnp.float32)


def halves(plan, own, come):
    blocks, rows, columns = own.shape
    shape = jax.ShapeDtypeStruct((blocks // 2, rows, columns), own.dtype)
    keep_map = lambda i, plan: (insert_bit(i, plan[0], plan[1]), 0, 0)
    send_map = lambda i, plan: (insert_bit(i, plan[0], 1 - plan[1]), 0, 0)
    block = (1, rows, columns)
    taken = [own, own] if come is None else [own, own, come, come]
    maps = [keep_map, send_map] * (len(taken) // 2)
    cost = pl.CostEstimate(flops=own.size, transcendentals=0, bytes_accessed=len(taken) * own.size * 2)
    return pl.pallas_call(
        split_kernel if come is None else join_kernel,
        grid_spec=pltpu.PrefetchScalarGridSpec(
            num_scalar_prefetch=1,
            grid=(blocks // 2,),
            in_specs=[pl.BlockSpec(block, m) for m in maps],
            out_specs=[pl.BlockSpec(block, lambda i, plan: (i, 0, 0))] * 2,
        ),
        out_shape=(shape, shape),
        cost_estimate=cost,
    )(plan, *taken)


def scatter_sum(grid, value):
    rows = value.shape[0] // grid.total
    held = value.reshape(grid.total, rows, value.shape[1])
    come = None
    for step, stage in enumerate(grid.stages):
        keep, send = halves(grid.plan(step), held, come)
        come = grid.swap(send, stage)
        held = keep
    out = pl.pallas_call(
        last_kernel,
        out_shape=jax.ShapeDtypeStruct(held.shape, jnp.float32),
        cost_estimate=pl.CostEstimate(flops=held.size, transcendentals=0, bytes_accessed=8 * held.size),
    )(held, come)
    return out.reshape(rows, value.shape[1])


def gather_small(grid, value):
    here = grid.here()
    held = value[None]
    for bit in range(grid.bits):
        come = grid.swap(held, (bit, bit))
        mine = (here >> bit) & 1
        held = jnp.where(mine == 0, jnp.concatenate([held, come]), jnp.concatenate([come, held]))
    return held


def scatter_small(grid, value):
    here = grid.here()
    held = value
    for bit in range(grid.bits - 1, -1, -1):
        mine = (here >> bit) & 1
        half = held.shape[0] // 2
        upper = mine == 1
        send = jnp.where(upper, held[:half], held[half:])
        keep = jnp.where(upper, held[half:], held[:half])
        held = keep + grid.swap(send, (bit, bit))
    return held


def body(
    grid,
    hidden_in,
    segment_ids,
    out_grad,
    norm1_gain,
    norm1_bias,
    norm2_gain,
    norm2_bias,
    qkv_weight,
    qkv_bias,
    proj_weight,
    proj_bias,
    up_weight,
    up_bias,
    down_weight,
    down_bias,
):
    small = (norm1_gain, norm1_bias, norm2_gain, norm2_bias, qkv_bias, proj_bias, up_bias, down_bias)
    widths = [entry.shape[0] for entry in small]
    packed = jnp.concatenate(small)
    packed = jnp.pad(packed, (0, -packed.shape[0] % 128))
    spread = gather_small(grid, packed)
    pieces, at = [], 0
    for width in widths:
        pieces.append(spread[:, at : at + width].reshape(-1))
        at += width
    gain_one, shift_one, gain_two, shift_two, b_qkv, b_proj, b_up, b_down = pieces
    w_qkv, w_proj, w_up, w_down = (
        lax.all_gather(entry, AXES, axis=0, tiled=True) for entry in (qkv_weight, proj_weight, up_weight, down_weight)
    )
    seq_count, length, model_width = hidden_in.shape
    row_count = seq_count * length
    scale = HEAD ** (-0.5)
    flat = hidden_in.reshape(row_count, model_width).astype(jnp.float32)
    grad_rows = out_grad.reshape(row_count, model_width)
    valid = (segment_ids != DOCS - 1).astype(jnp.float32).reshape(row_count, 1)
    cosine, sine = angles(segment_ids)
    normed_one = (
        normed(flat, gain_one.astype(jnp.float32)) + shift_one.astype(jnp.float32)
    ).astype(jnp.bfloat16)
    mixed = jnp.dot(normed_one, w_qkv, preferred_element_type=jnp.float32) + b_qkv.astype(
        jnp.float32
    )
    raw = mixed.reshape(seq_count, length, 3, HEADS, HEAD)
    raw_query = raw[:, :, 0]
    raw_keys = raw[:, :, 1]

    def rope_pair(first_part, second_part):
        return (rotate(first_part, cosine, sine), rotate(second_part, cosine, sine))

    (turned_query, turned_keys), rope_pull = jax.vjp(rope_pair, raw_query, raw_keys)
    query = (turned_query * scale).astype(jnp.bfloat16)
    keys = turned_keys.astype(jnp.bfloat16)
    values = raw[:, :, 2].astype(jnp.bfloat16)
    heads_out, log_sums = lax.map(attend_forward, (query, keys, values, segment_ids))
    attended = (heads_out.reshape(row_count, model_width) * valid).astype(jnp.bfloat16)
    projected = jnp.dot(attended, w_proj, preferred_element_type=jnp.float32) + b_proj.astype(
        jnp.float32
    )
    normed_two = (
        normed(flat, gain_two.astype(jnp.float32)) + shift_two.astype(jnp.float32)
    ).astype(jnp.bfloat16)
    before = jnp.dot(normed_two, w_up, preferred_element_type=jnp.float32) + b_up.astype(
        jnp.float32
    )
    after = jax.nn.gelu(before, approximate=False).astype(jnp.bfloat16)
    branch = jnp.dot(after, w_down, preferred_element_type=jnp.float32) + b_down.astype(jnp.float32)
    layer_out = (
        (flat + projected + branch).astype(jnp.bfloat16).reshape(seq_count, length, model_width)
    )
    back_gain_one, back_gain_two, back_qkv, back_proj, back_up, back_down = (
        gain_one, gain_two, w_qkv, w_proj, w_up, w_down
    )
    grad_wide = grad_rows.astype(jnp.float32)
    bias_grad = jnp.sum(grad_wide, axis=0)
    grad_down = jnp.einsum("rf,rd->fd", after, grad_rows, preferred_element_type=jnp.float32)
    d_after = jnp.einsum("rd,fd->rf", grad_rows, back_down, preferred_element_type=jnp.float32)
    gelu_value, gelu_pull = jax.vjp(partial(jax.nn.gelu, approximate=False), before)
    d_before = gelu_pull(d_after)[0].astype(jnp.bfloat16)
    grad_up_bias = jnp.sum(d_before.astype(jnp.float32), axis=0)
    grad_up = jnp.einsum("rd,rf->df", normed_two, d_before, preferred_element_type=jnp.float32)
    d_normed_two = jnp.einsum("rf,df->rd", d_before, back_up, preferred_element_type=jnp.float32)
    norm_value_two, pull_two = jax.vjp(normed, flat, back_gain_two.astype(jnp.float32))
    dx_two, grad_gain_two = pull_two(d_normed_two)
    grad_shift_two = jnp.sum(d_normed_two, axis=0)
    grad_proj = jnp.einsum("rd,re->de", attended, grad_rows, preferred_element_type=jnp.float32)
    d_attended = (
        jnp.einsum("re,de->rd", grad_rows, back_proj, preferred_element_type=jnp.float32) * valid
    ).astype(jnp.bfloat16)
    d_attended = d_attended.reshape(seq_count, length, HEADS, HEAD)
    d_query, d_keys, d_values = lax.map(
        attend_backward, (query, keys, values, segment_ids, log_sums, d_attended)
    )
    d_raw_query, d_raw_keys = rope_pull((d_query * scale, d_keys))
    d_mixed = (
        jnp.stack([d_raw_query, d_raw_keys, d_values], axis=2)
        .reshape(row_count, 3 * model_width)
        .astype(jnp.bfloat16)
    )
    grad_qkv_bias = jnp.sum(d_mixed.astype(jnp.float32), axis=0)
    grad_qkv = jnp.einsum("rd,rc->dc", normed_one, d_mixed, preferred_element_type=jnp.float32)
    d_normed_one = jnp.einsum("rc,dc->rd", d_mixed, back_qkv, preferred_element_type=jnp.float32)
    norm_value_one, pull_one = jax.vjp(normed, flat, back_gain_one.astype(jnp.float32))
    dx_one, grad_gain_one = pull_one(d_normed_one)
    grad_shift_one = jnp.sum(d_normed_one, axis=0)
    input_grad = (
        (grad_wide + dx_one + dx_two).astype(jnp.bfloat16).reshape(seq_count, length, model_width)
    )
    n = grid.total
    sums = (grad_gain_one, grad_shift_one, grad_gain_two, grad_shift_two, grad_qkv_bias, bias_grad, grad_up_bias)
    vectors = jnp.concatenate([entry.reshape(n, -1) for entry in sums], axis=1)
    vectors = jnp.pad(vectors, ((0, 0), (0, -vectors.shape[1] % 128)))
    total = scatter_small(grid, vectors)
    outs, at = [], 0
    for entry in sums:
        width = entry.shape[0] // n
        outs.append(total[0, at : at + width])
        at += width
    low = [scatter_sum(grid, entry.astype(jnp.bfloat16)) for entry in (grad_qkv, grad_proj, grad_up, grad_down)]
    return (
        layer_out,
        input_grad,
        outs[0],
        outs[1],
        outs[2],
        outs[3],
        low[0],
        outs[4],
        low[1],
        outs[5],
        low[2],
        outs[6],
        low[3],
        outs[5],
    )


NT = (((1,), (1,)), ((), ()))
NN = (((1,), (0,)), ((), ()))
TN = (((0,), (0,)), ((), ()))
PAIR = 2 * HEAD
ROWS = 256
TOKENS = 512


def mul(left, right, dims):
    return lax.dot_general(left, right, dims, preferred_element_type=jnp.float32)


def params(mebibytes):
    return pltpu.CompilerParams(vmem_limit_bytes=mebibytes << 20)


def cost(flops, moved, special=0):
    return pl.CostEstimate(flops=int(flops), transcendentals=int(special), bytes_accessed=int(moved))


def fixed(shape, at=None):
    place = (0,) * len(shape) if at is None else at
    return pl.BlockSpec(shape, lambda *_: place, pipeline_mode=pl.Buffered(1))


def middle_swap(value):
    quarter = (lax.broadcasted_iota(jnp.int32, value.shape, 1) % 128) // 32
    width = value.shape[1]
    up, down = pltpu.roll(value, width - 32, 1), pltpu.roll(value, 32, 1)
    return jnp.where(quarter == 1, up, jnp.where(quarter == 2, down, value))


def norm_kernel(source, cotangent, scales, *refs):
    one, two, grads = refs[-3:]
    value = source[...].astype(jnp.float32)
    center = value - jnp.mean(value, axis=1, keepdims=True)
    spread = jnp.mean(center * center, axis=1, keepdims=True)
    hat = middle_swap(center * lax.rsqrt(spread + norm_eps))
    table = scales[...].astype(jnp.float32)
    one[...] = (hat * table[0:1] + table[1:2]).astype(jnp.bfloat16)
    two[...] = (hat * table[2:3] + table[3:4]).astype(jnp.bfloat16)
    grads[...] = cotangent[...]


def norms(sequence, source, cotangent, scales, before):
    length, width = source.shape
    steps = length // ROWS
    block = pl.BlockSpec((ROWS, width), lambda i: (i, 0))
    out = pl.BlockSpec((ROWS, width), lambda i: (sequence * steps + i, 0))
    shape = jax.ShapeDtypeStruct((2 * length, width), jnp.bfloat16)
    return pl.pallas_call(
        norm_kernel,
        grid=(steps,),
        in_specs=[block, block, fixed(scales.shape)] + [pl.BlockSpec(memory_space=pl.ANY)] * len(before),
        out_specs=[out] * 3,
        out_shape=[shape] * 3,
        input_output_aliases={3 + n: n for n in range(len(before))},
        compiler_params=params(60),
        cost_estimate=cost(20 * length * width, 10 * length * width),
    )(source, cotangent, scales, *before)


def turn(value, cosine, sine):
    lane = lax.broadcasted_iota(jnp.int32, value.shape, 1) % HEAD
    half = ROT // 2
    up, down = pltpu.roll(value, value.shape[1] - half, 1), pltpu.roll(value, half, 1)
    return value * cosine + jnp.where(lane < half, up, down) * sine


def chosen(place, chip, near, far, *index):
    spot, half = place[chip], near.shape[0]
    return jnp.where(spot < half, near[(spot % half, *index)], far[(spot % half, *index)])


def arrange(place, half, weights, ordered, ordered_proj):
    chips = 2 * weights[0].shape[0]
    for part in range(3):
        near, far = weights[2 * part : 2 * part + 2]
        rows, width = near.shape[1:]
        for chip in range(chips):
            block = chosen(place, chip, near, far)
            ordered[chip * rows : (chip + 1) * rows, part * width : (part + 1) * width] = block
    near, far = weights[6:]
    below = near.shape[1] // 4
    for chip in range(chips // 2):
        block = chosen(place, half * chips // 2 + chip, near, far)
        for n in range(4):
            ordered_proj[chip * below : (chip + 1) * below, n * width : (n + 1) * width] = block[n * below : (n + 1) * below]


def weight_specs(weights, first):
    chips, _, width = weights[0].shape
    found = [fixed((chips, 64, width), (0, first + part, 0)) for part in range(3) for _ in weights]
    return found + [fixed((chips, 128, width))] * 2


def weight_scratch(weights):
    chips, _, width = weights[0].shape
    return [pltpu.VMEM((128 * chips, 3 * width), jnp.bfloat16), pltpu.VMEM((32 * chips, 4 * width), jnp.bfloat16)]


def project_kernel(half, place, normed, grads, *refs):
    weights = refs[:8]
    bias, cosine, sine, segments, out, ordered, ordered_proj = refs[8:]
    width = out.shape[-1]

    @pl.when(pl.program_id(0) == 0)
    def _():
        arrange(place, half, weights, ordered, ordered_proj)

    for part in range(3):
        columns = slice(part * width, (part + 1) * width)
        value = mul(normed[...], ordered[:, columns], NN) + bias[part].astype(jnp.float32)
        if part == 2:
            out[part] = value.astype(out.dtype)
            continue
        for at in range(0, width, PAIR):
            turned = turn(value[:, at : at + PAIR], cosine[...], sine[...])
            out[part, :, at : at + PAIR] = (turned * (HEAD ** (-0.5) if part == 0 else 1.0)).astype(out.dtype)
    valid = (segments[...] != DOCS - 1).astype(jnp.float32)
    out[3] = (mul(grads[...], ordered_proj[...], NT) * valid).astype(out.dtype)


def project(half, place, normed, grads, weights, first, proj, bias, cosine, sine, segments):
    tokens, model = normed.shape
    width = weights[0].shape[-1]
    rows = lambda n: pl.BlockSpec((TOKENS, n), lambda i, *_: (i, 0))
    return pl.pallas_call(
        partial(project_kernel, half),
        grid_spec=pltpu.PrefetchScalarGridSpec(
            num_scalar_prefetch=1,
            grid=(tokens // TOKENS,),
            in_specs=[rows(model), rows(model)]
            + weight_specs(weights, first)
            + [fixed(bias.shape), rows(PAIR), rows(PAIR), rows(1)],
            out_specs=pl.BlockSpec((4, TOKENS, width), lambda i, *_: (0, i, 0)),
            scratch_shapes=weight_scratch(weights),
        ),
        out_shape=jax.ShapeDtypeStruct((4, tokens, width), jnp.bfloat16),
        compiler_params=params(60),
        cost_estimate=cost(8 * tokens * model * width, 6 * tokens * model),
    )(place, normed, grads, *weights * 3, *proj, bias, cosine, sine, segments)


def attention_kernel(
    q_ref, k_ref, v_ref, g_ref, cosine, sine, seg_row, seg_col, *rest
):
    out, d_out, mask, dk_sum, dv_sum = rest[-5:]
    length = q_ref.shape[1]
    blocks = length // ROWS

    @pl.when(pl.program_id(0) == 0)
    def _():
        for block in range(blocks):
            start = block * ROWS
            end = start + ROWS
            key_pos = lax.broadcasted_iota(jnp.int32, (ROWS, end), 1)
            query_pos = lax.broadcasted_iota(jnp.int32, (ROWS, end), 0) + start
            allowed = (key_pos <= query_pos) & (seg_col[start:end, :] == seg_row[0, :, :end])
            mask[start:end, :end] = jnp.where(allowed, 0.0, masked_score)

    lane = lax.broadcasted_iota(jnp.int32, (ROWS, PAIR), 1)
    for block in range(blocks - 1, -1, -1):
        start = block * ROWS
        end = start + ROWS
        rows = slice(start, end)
        keys, values = k_ref[0, :end, :], v_ref[0, :end, :]
        query, grads = q_ref[0, rows, :], g_ref[0, rows, :]
        hide = mask[rows, :end]
        pieces = []
        for head in range(2):
            mine = lane < HEAD if head == 0 else lane >= HEAD
            own_query = jnp.where(mine, query, jnp.zeros_like(query))
            own_grads = jnp.where(mine, grads, jnp.zeros_like(grads))
            scores = mul(own_query, keys, NT) + hide
            exponent = jnp.exp(scores - jnp.max(scores, axis=1, keepdims=True))
            probs = exponent * (1.0 / jnp.sum(exponent, axis=1, keepdims=True))
            low = probs.astype(jnp.bfloat16)
            mixed = mul(low, values, NN)
            d_probs = mul(own_grads, values, NT)
            inner = jnp.sum(own_grads.astype(jnp.float32) * mixed, axis=1, keepdims=True)
            d_scores = (probs * (d_probs - inner)).astype(jnp.bfloat16)
            pieces.append((mixed, mul(d_scores, keys, NN)))
            d_keys, d_values = mul(d_scores, own_query, TN), mul(low, own_grads, TN)
            if block == blocks - 1 and head == 0:
                dk_sum[:end, :] = d_keys
                dv_sum[:end, :] = d_values
            else:
                dk_sum[:end, :] += d_keys
                dv_sum[:end, :] += d_values
        mine = lane < HEAD
        valid = (seg_col[rows, :] != DOCS - 1).astype(jnp.float32)
        out[rows, :] = (jnp.where(mine, pieces[0][0], pieces[1][0]) * valid).astype(out.dtype)
        d_query = turn(jnp.where(mine, pieces[0][1], pieces[1][1]), cosine[rows, :], -sine[rows, :])
        d_out[0, rows, :] = (d_query * HEAD ** (-0.5)).astype(d_out.dtype)
    d_out[1] = turn(dk_sum[...], cosine[...], -sine[...]).astype(d_out.dtype)
    d_out[2] = dv_sum[...].astype(d_out.dtype)


def attention(sequence, parts, cosine, sine, segments, before):
    length = segments.shape[1]
    tokens, width = parts.shape[1:]
    part = lambda p: pl.BlockSpec((1, length, PAIR), lambda j: (p, sequence, j))
    table = lambda n: pl.BlockSpec((length, n), lambda j: (sequence, 0))
    anywhere = pl.BlockSpec(memory_space=pl.ANY)
    return pl.pallas_call(
        attention_kernel,
        grid=(width // PAIR,),
        in_specs=[
            part(0),
            part(1),
            part(2),
            part(3),
            table(PAIR),
            table(PAIR),
            pl.BlockSpec((1, 1, length), lambda j: (sequence, 0, 0)),
            table(1),
        ]
        + [anywhere] * len(before),
        out_specs=[
            pl.BlockSpec((length, PAIR), lambda j: (sequence, j)),
            pl.BlockSpec((3, length, PAIR), lambda j: (0, sequence, j)),
        ],
        out_shape=[
            jax.ShapeDtypeStruct((tokens, width), jnp.bfloat16),
            jax.ShapeDtypeStruct((3, tokens, width), jnp.bfloat16),
        ],
        input_output_aliases={8 + n: n for n in range(len(before))},
        scratch_shapes=[pltpu.VMEM((length, length), jnp.float32)] + [pltpu.VMEM((length, PAIR), jnp.float32)] * 2,
        compiler_params=params(20),
        cost_estimate=cost(24 * tokens * length * width, 8 * tokens * width, tokens * length * width // 200),
    )(*[parts] * 4, cosine, sine, segments[:, None, :], segments.reshape(tokens, 1), *before)


def put_out(staged, keep, send, done):
    half = keep.shape[0]
    copies = [
        pltpu.make_async_copy(staged.at[pl.ds(n * half, half)], target, done.at[n])
        for n, target in enumerate((keep, send))
    ]
    for copy in copies:
        copy.start()
    for copy in copies:
        copy.wait()


def attention_grads_kernel(place, *refs):
    normed, d_mixed = refs[:2]
    more = refs[2:-7]
    keep, send, sums, totals, proj_total, staged, done = refs[-7:]
    step, last = pl.program_id(0), pl.num_programs(0) - 1
    width = d_mixed.shape[-1]
    chips = staged.shape[0]
    parts = totals.shape[0]
    rows = totals.shape[1] // chips

    @pl.when(step == 0)
    def _():
        totals[...] = jnp.zeros_like(totals)
        sums[...] = jnp.zeros_like(sums)
        if more:
            proj_total[...] = jnp.zeros_like(proj_total)

    for part in range(parts):
        totals[part] += mul(normed[...], d_mixed[part], TN)
        sums[part] += jnp.sum(d_mixed[part].astype(jnp.float32), axis=0, keepdims=True)
    if more:
        for n, attended in enumerate(more[:2]):
            proj_total[n * width : (n + 1) * width, :] += mul(attended[...], more[2][...], TN)

    @pl.when(step == last)
    def _():
        for chip in range(chips):
            spot = place[chip]
            for part in range(parts):
                change = totals[part, chip * rows : (chip + 1) * rows, :]
                staged[spot, part * rows : (part + 1) * rows, :] = change.astype(staged.dtype)
            if more:
                below = proj_total.shape[0] // chips
                for n in range(4):
                    change = proj_total[chip * below : (chip + 1) * below, n * width : (n + 1) * width]
                    start = parts * rows + n * below
                    staged[spot, start : start + below, :] = change.astype(staged.dtype)
        put_out(staged, keep, send, done)


def attention_grads(place, normed, d_mixed, more):
    tokens, model = normed.shape
    parts, _, width = d_mixed.shape
    chips = place.shape[0]
    rows = parts * model // chips + (4 * 2 * width // chips if more else 0)
    token = lambda n: pl.BlockSpec((TOKENS, n), lambda i, *_: (i, 0))
    half = jax.ShapeDtypeStruct((chips // 2, rows, width), jnp.bfloat16)
    anywhere = pl.BlockSpec(memory_space=pl.ANY)
    return pl.pallas_call(
        attention_grads_kernel,
        grid_spec=pltpu.PrefetchScalarGridSpec(
            num_scalar_prefetch=1,
            grid=(tokens // TOKENS,),
            in_specs=[token(model), pl.BlockSpec((parts, TOKENS, width), lambda i, *_: (0, i, 0))]
            + ([token(width), token(width), token(model)] if more else []),
            out_specs=[anywhere, anywhere, pl.BlockSpec((parts, 1, width), lambda i, *_: (0, 0, 0))],
            scratch_shapes=[
                pltpu.VMEM((parts, model, width), jnp.float32),
                pltpu.VMEM((2 * width, model), jnp.float32),
                pltpu.VMEM((chips, rows, width), jnp.bfloat16),
                pltpu.SemaphoreType.DMA((2,)),
            ],
        ),
        out_shape=[half, half, jax.ShapeDtypeStruct((parts, 1, width), jnp.float32)],
        compiler_params=params(60 if more else 26),
        cost_estimate=cost(8 * tokens * model * width, 6 * tokens * model),
    )(place, normed, d_mixed, *more)


def share_out(step, steps, earlier, mine, sends, value):
    each = steps // 2 // len(sends)
    for start, end, ref, more in [(0, steps // 2, mine, earlier[:1])] + [
        (steps // 2 + n * each, steps // 2 + (n + 1) * each, send, earlier[1:]) for n, send in enumerate(sends)
    ]:

        @pl.when((step >= start) & (step < end))
        def _():
            total = value
            for one in more:
                total = total + one[...].astype(jnp.float32)
            ref[...] = total.astype(ref.dtype)


def attention_back_kernel(half, pieces, place, d_mixed, attended, *refs):
    count = 2 * (1 + pieces) + 2
    weights, before, results = refs[:8], refs[8:-count], refs[-count:-2]
    ordered, ordered_proj = refs[-2:]
    step, steps = pl.program_id(0), pl.num_programs(0)

    @pl.when(step == 0)
    def _():
        arrange(place, half, weights, ordered, ordered_proj)

    change = jnp.concatenate([d_mixed[part] for part in range(3)], axis=1)
    share_out(step, steps, before[:2], results[0], results[1 : 1 + pieces], mul(change, ordered[...], NT))
    share_out(step, steps, before[2:], results[1 + pieces], results[2 + pieces :], mul(attended[...], ordered_proj[...], NN))


def attention_back(half, pieces, place, d_mixed, attended, weights, first, proj, before):
    parts, tokens, width = d_mixed.shape
    model = 128 * weights[0].shape[0]
    steps = tokens // TOKENS
    own = pl.BlockSpec((TOKENS, model), lambda i, *_: (jnp.minimum(i, steps // 2 - 1), 0))
    other = pl.BlockSpec((TOKENS, model), lambda i, *_: (jnp.maximum(i - steps // 2, 0), 0))
    each = steps // 2 // pieces
    shape = lambda n: jax.ShapeDtypeStruct((n * TOKENS, model), jnp.bfloat16)
    sent = [
        pl.BlockSpec((TOKENS, model), lambda i, *_, n=n: (jnp.clip(i - steps // 2 - n * each, 0, each - 1), 0))
        for n in range(pieces)
    ]
    return pl.pallas_call(
        partial(attention_back_kernel, half, pieces),
        grid_spec=pltpu.PrefetchScalarGridSpec(
            num_scalar_prefetch=1,
            grid=(steps,),
            in_specs=[
                pl.BlockSpec((parts, TOKENS, width), lambda i, *_: (0, i, 0)),
                pl.BlockSpec((TOKENS, width), lambda i, *_: (i, 0)),
            ]
            + weight_specs(weights, first)
            + [own, other] * (len(before) // 2),
            out_specs=([own] + sent) * 2,
            scratch_shapes=weight_scratch(weights),
        ),
        out_shape=([shape(steps // 2)] + [shape(each)] * pieces) * 2,
        compiler_params=params(60),
        cost_estimate=cost(8 * tokens * model * width, 8 * tokens * model),
    )(place, d_mixed, attended, *weights * 3, *proj, *before)


def forward_kernel(place, normed, grads, near, far, bias, *refs):
    earlier, refs = refs[:-18], refs[-18:]
    keep, send, sums = refs[:3]
    outs = refs[3:7]
    own_normed, own_grads, up, down, after, d_before, results, staged, arrived, shared, left = refs[7:18]
    tokens, model = own_normed.shape
    hidden = up.shape[1]
    half_tokens = tokens // 2
    rows = near.shape[1] // 2
    chips = 2 * near.shape[0]
    blocks = tokens // ROWS

    def pieces(chip):
        at = pl.ds(chip * rows, rows)
        return ((0, up.at[at], 2 * chip), (rows, down.at[at], 2 * chip + 1))

    def row_loads(block):
        at = pl.ds(block * ROWS, ROWS)
        return [
            pltpu.make_async_copy(source.at[at], target.at[at], arrived.at[2 * chips + 2 * block + n])
            for n, (source, target) in enumerate(((normed, own_normed), (grads, own_grads)))
        ]

    loads = [pltpu.make_async_copy(ref, results.at[n], shared.at[n]) for n, ref in enumerate(earlier)]
    for chip in range(chips):
        spot = place[chip]
        for start, target, n in pieces(chip):
            for own, source in ((True, near), (False, far)):

                @pl.when((spot < chips // 2) == own)
                def _():
                    held = source.at[spot % (chips // 2), pl.ds(start, rows)]
                    pltpu.make_async_copy(held, target, arrived.at[n]).start()

    for block in range(blocks):
        for load in row_loads(block):
            load.start()
    for load in loads:
        load.start()
    for chip in range(chips):
        for start, target, n in pieces(chip):
            pltpu.make_async_copy(near.at[0, pl.ds(start, rows)], target, arrived.at[n]).wait()
    offset = bias[...].astype(jnp.float32)
    bias_total = jnp.zeros_like(offset)
    for block in range(blocks):
        at = slice(block * ROWS, (block + 1) * ROWS)
        for load in row_loads(block):
            load.wait()
        before = mul(own_normed[at, :], up[...], NN) + offset
        change = mul(own_grads[at, :], down[...], NT)
        share = 0.5 + 0.5 * lax.erf(before * 0.7071067811865476)
        density = jnp.exp(-0.5 * before * before) * 0.3989422804014327
        after[at, :] = (before * share).astype(after.dtype)
        low = (change * (share + before * density)).astype(d_before.dtype)
        d_before[at, :] = low
        bias_total += jnp.sum(low.astype(jnp.float32), axis=0, keepdims=True)
    sums[...] = bias_total
    for load in loads:
        load.wait()
    stores = []
    for block in range(blocks):
        at = slice(block * ROWS, (block + 1) * ROWS)
        side = 0 if block * ROWS < half_tokens else 1
        own = pl.ds(block * ROWS - side * half_tokens, ROWS)
        for which, value in enumerate((mul(after[at, :], down[...], NN), mul(d_before[at, :], up[...], NT))):
            n = 2 * which + side
            if n < len(earlier):
                value += results[n, own, :].astype(jnp.float32)
            results[n, own, :] = value.astype(results.dtype)
            store = pltpu.make_async_copy(results.at[n, own], outs[n].at[own], left.at[2 + 2 * block + which])
            store.start()
            stores.append(store)
    tile = 256
    for start in range(0, hidden, tile):
        change = mul(own_normed[...], d_before[:, start : start + tile], TN).astype(staged.dtype)
        for chip in range(chips):
            staged[place[chip], :rows, start : start + tile] = change[chip * rows : (chip + 1) * rows]
        change = mul(after[:, start : start + tile], own_grads[...], TN).astype(staged.dtype)
        for n in range(tile // rows):
            staged[place[start // rows + n], rows:, :] = change[n * rows : (n + 1) * rows]
    half = keep.shape[0]
    for n, target in enumerate((keep, send)):
        store = pltpu.make_async_copy(staged.at[pl.ds(n * half, half)], target, left.at[n])
        store.start()
        stores.append(store)
    for store in stores:
        store.wait()


def forward_chunk(place, normed, grads, weights, bias, earlier):
    tokens, model = normed.shape
    chips, both_rows, hidden = weights[0].shape
    chips *= 2
    low = lambda *shape: pltpu.VMEM(shape, jnp.bfloat16)
    blocks = jax.ShapeDtypeStruct((chips // 2, both_rows, model), jnp.bfloat16)
    anywhere = pl.BlockSpec(memory_space=pl.ANY)
    share = jax.ShapeDtypeStruct((tokens // 2, model), jnp.bfloat16)
    small = pl.BlockSpec((1, hidden), lambda i, *_: (0, 0))
    counts = (2 * chips + 2 * (tokens // ROWS), 4, 2 + 2 * (tokens // ROWS))
    return pl.pallas_call(
        forward_kernel,
        grid_spec=pltpu.PrefetchScalarGridSpec(
            num_scalar_prefetch=1,
            grid=(1,),
            in_specs=[anywhere] * 4 + [small] + [anywhere] * len(earlier),
            out_specs=[anywhere, anywhere, small] + [anywhere] * 4,
            scratch_shapes=[
                low(tokens, model),
                low(tokens, model),
                low(model, hidden),
                low(hidden, model),
                low(tokens, hidden),
                low(tokens, hidden),
                low(4, tokens // 2, model),
                low(chips, both_rows, model),
            ]
            + [pltpu.SemaphoreType.DMA((count,)) for count in counts],
        ),
        out_shape=[blocks, blocks, jax.ShapeDtypeStruct((1, hidden), jnp.float32)] + [share] * 4,
        compiler_params=params(44),
        cost_estimate=cost(12 * tokens * model * hidden, 16 * tokens * model, 2 * tokens * hidden),
    )(place, normed, grads, *weights, bias, *earlier)


def both_of(left, *right):
    come = right[0][...]
    if len(right) > 1:
        come = jnp.where(pl.program_id(0) < pl.num_programs(0) // 2, come, right[1][...])
    return left[...].astype(jnp.float32) + come.astype(jnp.float32)


def finish_out_kernel(hidden, mine, come, scales, layer_out):
    table = scales[...].astype(jnp.float32)
    total = both_of(mine, come) + table[0:1] + table[1:2]
    layer_out[...] = (hidden[...].astype(jnp.float32) + total).astype(layer_out.dtype)


def finish_grad_kernel(hidden, grads, one_mine, one_come, two_mine, two_come, scales, input_grad, sums):
    value = hidden[...].astype(jnp.float32)
    cotangent = grads[...].astype(jnp.float32)
    table = scales[...].astype(jnp.float32)
    center = value - jnp.mean(value, axis=1, keepdims=True)
    scale = lax.rsqrt(jnp.mean(center * center, axis=1, keepdims=True) + norm_eps)
    hat = center * scale
    one, two = middle_swap(both_of(one_mine, one_come)), middle_swap(both_of(two_mine, two_come))
    gained = one * table[0:1] + two * table[1:2]
    mean = jnp.mean(gained, axis=1, keepdims=True)
    slope = jnp.mean(gained * hat, axis=1, keepdims=True)
    input_grad[...] = (cotangent + (gained - mean - hat * slope) * scale).astype(input_grad.dtype)

    @pl.when(pl.program_id(0) == 0)
    def _():
        sums[...] = jnp.zeros_like(sums)

    for row, column in enumerate((one * hat, one, two * hat, two, cotangent)):
        sums[row : row + 1, :] += jnp.sum(column, axis=0, keepdims=True)


def finish(kernel, arrays, scales, with_sums):
    length, width = arrays[0].shape
    block = pl.BlockSpec((ROWS, width), lambda i: (i, 0))
    steps, specs = length // ROWS, []
    for array in arrays:
        if isinstance(array, tuple):
            specs.append(pl.BlockSpec((ROWS, width), lambda i: (jnp.minimum(i, steps // 2 - 1), 0)))
            specs.append(pl.BlockSpec((ROWS, width), lambda i: (jnp.maximum(i - steps // 2, 0), 0)))
        else:
            specs.append(block)
    arrays = jax.tree.leaves(arrays)
    shape = jax.ShapeDtypeStruct((length, width), jnp.bfloat16)
    more = [pl.BlockSpec((8, width), lambda i: (0, 0))] if with_sums else []
    return pl.pallas_call(
        kernel,
        grid=(length // ROWS,),
        in_specs=specs + [fixed(scales.shape)],
        out_specs=[block] + more,
        out_shape=[shape] + [jax.ShapeDtypeStruct((8, width), jnp.float32)] * len(more),
        compiler_params=params(60),
        cost_estimate=cost(40 * length * width, 2 * (len(arrays) + 1) * length * width),
    )(*arrays, scales)


def by_core(core, mine, come):
    return jnp.where(core == 0, mine, come), jnp.where(core == 0, come, mine)


def qkv_rows_kernel(core, mine_one, come_one, mine_two, come_two, out):
    parts, _, width = mine_one.shape
    for part in range(parts):
        for half, (mine, come) in enumerate(((mine_one, come_one), (mine_two, come_two))):
            even, odd = by_core(core[0], mine[part], come[part])
            for head in range(width // HEAD):
                at = slice(head * HEAD, (head + 1) * HEAD)
                start = (part * 2 + half) * 2 * width + head * PAIR
                out[:, start : start + PAIR] = jnp.concatenate([even[:, at], odd[:, at]], axis=1)


def up_rows_kernel(core, mine_one, come_one, mine_two, come_two, out):
    width = mine_one.shape[2]
    first, second = by_core(core[0], mine_one[0], come_one[0]), by_core(core[0], mine_two[0], come_two[0])
    for chip in range(width // 64):
        at = slice(chip * 64, (chip + 1) * 64)
        for which in range(2):
            start = ((chip // 2) * 2 + which) * 256 + (chip % 2) * 128
            out[:, start : start + 128] = jnp.concatenate([first[which][:, at], second[which][:, at]], axis=1)


def whole_rows(kernel, core, halves, shape):
    operands = [array for half in halves for array in half]
    return pl.pallas_call(
        kernel,
        grid_spec=pltpu.PrefetchScalarGridSpec(
            num_scalar_prefetch=1,
            grid=(1,),
            in_specs=[fixed(array.shape) for array in operands],
            out_specs=pl.BlockSpec(shape, lambda i, *_: (0, 0)),
        ),
        out_shape=jax.ShapeDtypeStruct(shape, jnp.float32),
        compiler_params=params(16),
        cost_estimate=cost(0, 16 * shape[0] * shape[1]),
    )(core, *operands)


BITS = {"y": 0, "core": 1, "x": 2, "z_low": 3, "z_high": 4}
SPLIT = ("zx", "core", "y")
CORES = ("core", "core")
STAGES = (("x", "y"), ("y", "x"), ("z_low", "z_low"), ("z_high", "z_high"))


class Pairs:
    def __init__(self, total):
        self.total = total

    def here(self):
        y = lax.axis_size("y")
        return (lax.axis_index("zx") * 2 + lax.axis_index("core")) * y + lax.axis_index("y")

    def bit(self, name):
        return (self.here() >> BITS[name]) & 1

    def swap(self, value, names):
        moves = []
        for device in range(self.total):
            name = names[(device >> BITS["core"]) & 1]
            moves.append((device, device ^ (1 << BITS[name])))
        return lax.ppermute(value, SPLIT, moves)

    def places(self):
        chip = jnp.arange(self.total // 2, dtype=jnp.int32)
        bits = {"y": chip & 1, "x": (chip >> 1) & 1, "z_low": (chip >> 2) & 1, "z_high": (chip >> 3) & 1}
        differs = {name: bits[name] ^ self.bit(name) for name in bits}
        place = jnp.zeros_like(chip)
        for first, second in STAGES:
            place = 2 * place + jnp.where(lax.axis_index("core") == 0, differs[first], differs[second])
        return place


class Sum:
    def __init__(self, pairs, keep, send):
        self.pairs, self.arrays, self.stage = pairs, (keep, send), 0

    def ready(self, arrays):
        if self.stage == 0:
            return arrays
        keep, come = arrays
        half = keep.shape[0] // 2
        return add_low(keep[:half], come[:half]), add_low(keep[half:], come[half:])

    def move(self, arrays):
        keep, send = arrays
        self.arrays = keep, self.pairs.swap(send, STAGES[self.stage])
        self.stage += 1

    def result(self):
        keep, come = self.arrays
        return keep[0].astype(jnp.float32) + come[0].astype(jnp.float32)


class Gather:
    def __init__(self, pairs, own):
        self.pairs, self.arrays, self.stage = pairs, (own[None],), 0

    def ready(self, arrays):
        return arrays if self.stage == 0 else (jnp.concatenate(arrays),)

    def move(self, arrays):
        self.stage += 1
        self.arrays = arrays[0], self.pairs.swap(arrays[0], STAGES[-self.stage])

    def result(self):
        return self.arrays


class Trade:
    def __init__(self, pairs, *arrays):
        self.pairs, self.arrays, self.stage = pairs, arrays, 0

    def ready(self, arrays):
        return arrays

    def move(self, arrays):
        if self.stage == 0:
            arrays = tuple(self.pairs.swap(array, CORES) for array in arrays)
        self.arrays = arrays
        self.stage += 1

    def result(self):
        return self.arrays


def hold(value, tasks):
    value, arrays = lax.optimization_barrier((value, [task.arrays for task in tasks]))
    for task, own in zip(tasks, arrays):
        task.arrays = tuple(own)
    return value


def tick(after, value, *tasks, done=()):
    if after is not None:
        after = hold(after, tasks + tuple(done))
    for task in tasks:
        task.arrays = task.ready(task.arrays)
    after, value = hold((after, value), tasks)
    for task in tasks:
        task.move(task.arrays)
    return after, value


def add_low(left, right):
    return (left.astype(jnp.float32) + right.astype(jnp.float32)).astype(jnp.bfloat16)


def wide_angles(segments):
    position = lax.broadcasted_iota(jnp.int32, segments.shape, 1)
    change = jnp.concatenate([jnp.ones_like(segments[:, :1], jnp.bool_), segments[:, 1:] != segments[:, :-1]], axis=1)
    place = position - lax.cummax(jnp.where(change, position, 0), axis=1)
    lane = jnp.arange(PAIR) % HEAD
    half = ROT // 2
    freqs = 10000.0 ** (-((lane % half) * 2).astype(jnp.float32) / ROT)
    freqs = jnp.where(lane < ROT, freqs, 0.0)
    theta = place.reshape(-1, 1).astype(jnp.float32) * freqs
    return jnp.cos(theta), jnp.sin(theta) * jnp.where(lane < half, -1.0, 1.0)


def pick(value, which, axis):
    return lax.dynamic_index_in_dim(value, which, axis, keepdims=False)


def paired_body(
    pairs,
    hidden_in,
    segment_ids,
    out_grad,
    norm1_gain,
    norm1_bias,
    norm2_gain,
    norm2_bias,
    qkv_weight,
    qkv_bias,
    proj_weight,
    proj_bias,
    up_weight,
    up_bias,
    down_weight,
    down_bias,
):
    core = lax.axis_index("core")
    heads = HEADS // 2
    rows, model = qkv_weight.shape[0], proj_weight.shape[1]
    width = heads * HEAD // 2
    unit = down_weight.shape[0] // 2
    hidden, grads = hidden_in[0], out_grad[0]

    def columns(which):
        taken = pick(qkv_weight.reshape(rows, 3, heads, 2, HEAD), which, 3).reshape(rows, 3 * 2 * width)
        more = pick(up_weight.reshape(rows, heads, 2, 2, 2, unit), which, 2).transpose(0, 3, 1, 2, 4).reshape(rows, -1)
        return jnp.concatenate([taken, more], axis=1)

    theirs = pairs.swap(columns(1 - core), CORES)
    mine = columns(core)
    both = jnp.where(core == 0, jnp.stack([mine, theirs]), jnp.stack([theirs, mine])).reshape(2 * rows, -1)
    low_qkv = both[:, : 6 * width].reshape(2 * rows, 3, 2, width).transpose(2, 1, 0, 3)
    low_proj = proj_weight.reshape(rows, 4, width).transpose(1, 0, 2).reshape(2, 2 * rows, width)
    low_up = both[:, 6 * width :].reshape(2 * rows, 2, -1).transpose(1, 0, 2)
    low_down = down_weight.reshape(2, unit, model)

    other, other_grads = pairs.swap(hidden, CORES), pairs.swap(grads, CORES)
    segments = jnp.concatenate([segment_ids, pairs.swap(segment_ids, CORES)])
    column = segments.reshape(-1, 1)
    cosine, sine = wide_angles(segments)
    place = pairs.places()

    small = (norm1_gain, norm1_bias, norm2_gain, norm2_bias, qkv_bias, proj_bias, up_bias, down_bias)
    ends = [sum(entry.shape[0] for entry in small[: n + 1]) for n in range(len(small))]
    long = ends[-1] + -ends[-1] % 128
    line = sum(jnp.pad(entry, (end - entry.shape[0], long - end)) for entry, end in zip(small, ends))
    come = pairs.swap(line, CORES)
    lines = Gather(pairs, jnp.where(core == 0, jnp.stack([line, come]), jnp.stack([come, line])).reshape(-1))
    first = Gather(pairs, jnp.concatenate([low_proj, low_qkv[0]]).reshape(-1, width))
    chunks = [Gather(pairs, jnp.concatenate([low_up[h], low_down[h]])) for h in range(2)]
    second = Gather(pairs, low_qkv[1].reshape(-1, width))
    tick(None, (), first, lines)
    tick(None, (), lines)
    tick(None, (), first, lines)
    tick(None, (), lines)
    table = jnp.concatenate(lines.result())[place]
    table = table.reshape(heads, 2, 2, -1).swapaxes(1, 2).reshape(pairs.total, -1)
    spread, at = [], 0
    for entry in small:
        size = entry.shape[0]
        spread.append(table[:, at : at + size].reshape(-1))
        at += size
    gain_one, shift_one, gain_two, shift_two, b_qkv, b_proj, b_up, b_down = spread
    own_bias = pick(b_qkv.reshape(3, heads, 2, HEAD), core, 2).reshape(3, 2, 1, width)
    own_up_bias = pick(b_up.reshape(heads, 2, 2, 2, unit), core, 1).transpose(2, 0, 1, 3).reshape(2, 1, -1)
    scales = jnp.stack([gain_one, shift_one, gain_two, shift_two])
    scales = scales.reshape(4, -1, 2, 2, rows).swapaxes(2, 3).reshape(4, model)
    _, scales = tick(None, scales, first)
    before = norms(0, hidden, grads, scales, ())
    before, (scales, segments) = tick(before, (scales, segments), first, chunks[0])
    column = segments.reshape(-1, 1)
    cosine, sine = wide_angles(segments)
    normed_one, normed_two, both_grads = norms(1, other, other_grads, scales, before)
    (normed_one, cosine, sine), _ = tick((normed_one, cosine, sine), (), chunks[0], done=(first,))
    w_first = first.result()

    parts = project(
        0, place, normed_one, both_grads, w_first, 2, w_first, own_bias[:, 0], cosine, sine, column
    )
    parts, _ = tick(parts, (), chunks[0], chunks[1])
    before = attention(0, parts, cosine, sine, segments, ())
    before, parts = tick(before, parts, chunks[0], chunks[1])
    attended_one, d_mixed = attention(1, parts, cosine, sine, segments, before)
    (attended_one, d_mixed), _ = tick((attended_one, d_mixed), (), chunks[1], second)
    keep, send, qkv_sums_one = attention_grads(place, normed_one, d_mixed, ())
    sum_one = Sum(pairs, keep, send)
    qkv_sums_one, d_mixed = tick(qkv_sums_one, d_mixed, sum_one, second)
    d1, d1_send, out, out_send = attention_back(0, 1, place, d_mixed, attended_one, w_first, 2, w_first, ())

    sum_forward, up_sums = [], []
    before = (out, out_send)
    for chunk in range(2):
        more = [] if chunk else chunks[1:]
        before, normed_two = tick(before, normed_two, *more, sum_one, second, *sum_forward, done=(chunks[chunk],))
        keep, send, sums, *before = forward_chunk(
            place,
            normed_two,
            both_grads,
            chunks[chunk].result(),
            own_up_bias[chunk],
            before,
        )
        up_sums.append(sums)
        sum_forward.append(Sum(pairs, keep, send))
    out, out_send, d2, d2_send = before

    (out, out_send, d2_send), normed_one = tick(
        (out, out_send, d2_send), normed_one, sum_one, sum_forward[0], done=(second,)
    )
    w_second = second.result()
    trade_two = Trade(pairs, d2_send)
    parts = project(
        1, place, normed_one, both_grads, w_second, 0, w_first, own_bias[:, 1], cosine, sine, column
    )
    parts, _ = tick(parts, (), sum_forward[0], sum_forward[1], trade_two, done=(sum_one,))
    before = attention(0, parts, cosine, sine, segments, ())
    before, parts = tick(before, parts, sum_forward[0], done=(trade_two,))
    attended_two, d_mixed = attention(1, parts, cosine, sine, segments, before)
    (attended_two, d_mixed), _ = tick((attended_two, d_mixed), (), sum_forward[1], done=sum_forward[:1])
    d1, d1_send, out, out_send = attention_back(
        1, 1, place, d_mixed, attended_two, w_second, 0, w_first, (d1, d1_send, out, out_send)
    )
    trade = Trade(pairs, d1_send, out_send)
    (d1, out), d_mixed = tick((d1, out), d_mixed, sum_forward[1], trade)
    keep, send, qkv_sums_two = attention_grads(place, normed_one, d_mixed, (attended_one, attended_two, both_grads))
    sum_two = Sum(pairs, keep, send)
    (qkv_sums_two, d1, out), _ = tick((qkv_sums_two, d1, out), (), sum_two, sum_forward[1], done=(trade,))
    d1_come, out_come = trade.result()
    input_grad, sums = finish(
        finish_grad_kernel,
        [hidden, grads, d1, d1_come, d2, *trade_two.result()],
        jnp.stack([gain_one, gain_two]),
        True,
    )
    (input_grad, sums, qkv_sums_one, qkv_sums_two, up_sums), _ = tick(
        (input_grad, sums, qkv_sums_one, qkv_sums_two, up_sums), (), sum_two, done=(sum_forward[1],)
    )
    def both_cores(own):
        own = own[:, None]
        none = jnp.zeros_like(own)
        return jnp.where(core == 0, jnp.concatenate([own, none], axis=1), jnp.concatenate([none, own], axis=1)).reshape(-1)

    def halve(table, name):
        upper = pairs.bit(name) == 1
        half = table.shape[0] // 2
        send = jnp.where(upper, table[:half], table[half:])
        return jnp.where(upper, table[half:], table[:half]) + pairs.swap(send, (name, name))

    sum_qkv = jnp.stack([qkv_sums_one.reshape(3, -1), qkv_sums_two.reshape(3, -1)], axis=1)
    sum_up = jnp.stack([entry.reshape(heads, 2, unit) for entry in up_sums], axis=2)
    entries = [
        sums[0],
        sums[1],
        sums[2],
        sums[3],
        both_cores(sum_qkv.reshape(-1, HEAD)),
        sums[4],
        both_cores(sum_up.reshape(heads, -1)),
    ]
    table = jnp.concatenate([entry.reshape(pairs.total, -1) for entry in entries], axis=1)
    table = jnp.pad(table, ((0, 0), (0, -table.shape[1] % 128)))
    names = list(reversed(BITS))
    for name in names[:1]:
        table = halve(table, name)
    table, out = tick(table, out, sum_two)
    layer_out = finish(finish_out_kernel, [hidden, out, out_come], jnp.stack([b_proj, b_down]), False)[0]
    table = halve(halve(table, names[1]), names[2])
    (table, layer_out), _ = tick((table, layer_out), (), sum_two, done=(sum_one, *sum_forward))
    for name in names[3:]:
        table = halve(table, name)
    low_qkv_one, low_qkv_two = sum_one.result(), sum_two.result()
    low_forward = [task.result() for task in sum_forward]

    def trade_rows(value):
        split = value.reshape(value.shape[0], 2, rows, -1)
        return pick(split, core, 1), pairs.swap(pick(split, 1 - core, 1), CORES)

    which = core.astype(jnp.int32).reshape(1)
    low = (low_qkv_one.reshape(3, 2 * rows, width), low_qkv_two[: 6 * rows].reshape(3, 2 * rows, width))
    grad_qkv = whole_rows(qkv_rows_kernel, which, [trade_rows(value) for value in low], qkv_weight.shape)
    grad_proj = low_qkv_two[6 * rows :].reshape(4, rows, width).transpose(1, 0, 2).reshape(rows, model)
    ups = [trade_rows(entry[: 2 * rows].reshape(1, 2 * rows, -1)) for entry in low_forward]
    grad_up = whole_rows(up_rows_kernel, which, ups, up_weight.shape)
    grad_down = jnp.concatenate([entry[2 * rows :] for entry in low_forward])
    outs, at = [], 0
    for entry in entries:
        size = entry.shape[0] // pairs.total
        outs.append(table[0, at : at + size])
        at += size
    return (
        layer_out[None],
        input_grad[None],
        outs[0],
        outs[1],
        outs[2],
        outs[3],
        grad_qkv,
        outs[4],
        grad_proj,
        outs[5],
        grad_up,
        outs[6],
        grad_down,
        outs[5],
    )


def placed(axes):
    rows, flat = P(axes, None), P(axes)
    whole = P(axes, None, None)
    inside = (whole, rows, whole) + (flat,) * 4 + (rows, flat) * 4
    outside = (whole, whole) + (flat,) * 4 + (rows, flat) * 4
    return inside, outside


def solution(mesh):
    dp, fsdp = mesh.shape["dp"], mesh.shape["fsdp"]
    if (dp, fsdp) == (16, 2):
        split = Mesh(mesh.devices.reshape(dp // 2, 2, fsdp), SPLIT)
        inside, outside = placed(SPLIT)
        step = partial(paired_body, Pairs(dp * fsdp))
        return jax.shard_map(step, mesh=split, in_specs=inside, out_specs=outside, check_vma=False)
    inside, outside = placed(AXES)
    step = partial(body, Grid((dp, fsdp)))
    return jax.shard_map(step, mesh=mesh, in_specs=inside, out_specs=outside, check_vma=False)
```

```python
from functools import partial

import jax
import jax.numpy as jnp
from jax import lax
from jax.experimental import pallas as pl
from jax.experimental.pallas import tpu as pltpu
from jax.sharding import Mesh
from jax.sharding import PartitionSpec as P

AXES = ("dp", "fsdp")

HEADS = 16
HEAD = 64
ROT = 16
DOCS = 8


norm_eps = 1e-05
masked_score = -1e30


def normed(values, gain):
    center = values - jnp.mean(values, axis=-1, keepdims=True)
    spread = jnp.mean(center * center, axis=-1, keepdims=True)
    return center * lax.rsqrt(spread + norm_eps) * gain


def rotate(part, cosine, sine):
    half_rot = ROT // 2
    first = part[..., :half_rot]
    second = part[..., half_rot:ROT]
    cos_wide = cosine[..., None, :]
    sin_wide = sine[..., None, :]
    return jnp.concatenate(
        [
            first * cos_wide - second * sin_wide,
            second * cos_wide + first * sin_wide,
            part[..., ROT:],
        ],
        axis=-1,
    )


def angles(segments):
    last_axis = segments.ndim - 1
    position = lax.broadcasted_iota(jnp.int32, segments.shape, last_axis)
    change = jnp.concatenate(
        [jnp.ones(segments.shape[:-1] + (1,), jnp.bool_), segments[..., 1:] != segments[..., :-1]],
        axis=-1,
    )
    first_index = lax.cummax(jnp.where(change, position, jnp.zeros_like(position)), axis=last_axis)
    place = (position - first_index).astype(jnp.float32)
    freqs = 10000.0 ** (-(jnp.arange(ROT // 2) * 2).astype(jnp.float32) / ROT)
    theta = place[..., None] * freqs
    return (jnp.cos(theta), jnp.sin(theta))


def block_mask(segments, block_start, block_rows):
    length = segments.shape[0]
    query_pos = block_start + lax.broadcasted_iota(jnp.int32, (block_rows, length), 0)
    key_pos = lax.broadcasted_iota(jnp.int32, (block_rows, length), 1)
    same = segments[block_start : block_start + block_rows][:, None] == segments[None, :]
    return ((key_pos <= query_pos) & same)[None]


def attend_forward(pieces):
    query, keys, values, segments = pieces
    length = segments.shape[0]
    block_rows = min(512, length)
    outputs = []
    log_sums = []
    for block_start in range(0, length, block_rows):
        allowed = block_mask(segments, block_start, block_rows)
        scores = jnp.einsum(
            "qhe,khe->hqk",
            query[block_start : block_start + block_rows],
            keys,
            preferred_element_type=jnp.float32,
        )
        scores = jnp.where(allowed, scores, masked_score)
        row_max = jnp.max(scores, axis=-1, keepdims=True)
        exponent = jnp.exp(scores - row_max)
        total = jnp.sum(exponent, axis=-1, keepdims=True)
        weights = (exponent / total).astype(jnp.bfloat16)
        outputs.append(
            jnp.einsum("hqk,khe->qhe", weights, values, preferred_element_type=jnp.float32)
        )
        log_sums.append(row_max + jnp.log(total))
    return (jnp.concatenate(outputs, axis=0), jnp.concatenate(log_sums, axis=1))


def attend_backward(pieces):
    query, keys, values, segments, log_sums, d_out = pieces
    length = segments.shape[0]
    block_rows = min(512, length)
    query_parts = []
    d_keys = jnp.zeros(keys.shape, jnp.float32)
    d_values = jnp.zeros(values.shape, jnp.float32)
    for block_start in range(0, length, block_rows):
        block_end = block_start + block_rows
        allowed = block_mask(segments, block_start, block_rows)
        scores = jnp.einsum(
            "qhe,khe->hqk", query[block_start:block_end], keys, preferred_element_type=jnp.float32
        )
        scores = jnp.where(allowed, scores, masked_score)
        probs = jnp.exp(scores - log_sums[:, block_start:block_end])
        d_probs = jnp.einsum(
            "qhe,khe->hqk", d_out[block_start:block_end], values, preferred_element_type=jnp.float32
        )
        inner = jnp.sum(d_probs * probs, axis=-1, keepdims=True)
        d_scores = (probs * (d_probs - inner)).astype(jnp.bfloat16)
        d_values = d_values + jnp.einsum(
            "hqk,qhe->khe",
            probs.astype(jnp.bfloat16),
            d_out[block_start:block_end],
            preferred_element_type=jnp.float32,
        )
        query_parts.append(
            jnp.einsum("hqk,khe->qhe", d_scores, keys, preferred_element_type=jnp.float32)
        )
        d_keys = d_keys + jnp.einsum(
            "hqk,qhe->khe",
            d_scores,
            query[block_start:block_end],
            preferred_element_type=jnp.float32,
        )
    return (jnp.concatenate(query_parts, axis=0), d_keys, d_values)


class Grid:
    def __init__(self, sizes):
        dp, fsdp = sizes
        self.total = dp * fsdp
        self.low = fsdp.bit_length() - 1
        self.bits = self.total.bit_length() - 1
        self.core = self.low
        self.x = self.low + 1
        self.y = self.low - 1
        stages = [(self.core, self.core), (self.x, self.y), (self.y, self.x)]
        stages += [(b, b) for b in range(self.low - 2, -1, -1)]
        stages += [(b, b) for b in range(self.x + 1, self.bits)]
        self.stages = stages

    def here(self):
        return lax.axis_index("dp") * (1 << self.low) + lax.axis_index("fsdp")

    def pairs(self, stage):
        found = []
        for device in range(self.total):
            bit = stage[(device >> self.core) & 1]
            found.append((device, device ^ (1 << bit)))
        return found

    def swap(self, value, stage):
        return lax.ppermute(value, AXES, self.pairs(stage))

    def plan(self, step):
        here = self.here()
        core = (here >> self.core) & 1
        chosen = []
        for which in (0, 1):
            bit = self.stages[step][which]
            gone = [s[which] for s in self.stages[:step]]
            chosen.append((bit - sum(1 for g in gone if g < bit), (here >> bit) & 1))
        place = jnp.where(core == 0, chosen[0][0], chosen[1][0])
        value = jnp.where(core == 0, chosen[0][1], chosen[1][1])
        return jnp.stack([place, value]).astype(jnp.int32)


def insert_bit(index, place, value):
    low = index & ((1 << place) - 1)
    return ((index >> place) << (place + 1)) | (value << place) | low


def split_kernel(plan, own_keep, own_send, keep, send):
    keep[...] = own_keep[...]
    send[...] = own_send[...]


def join_kernel(plan, own_keep, own_send, come_keep, come_send, keep, send):
    keep[...] = (own_keep[...].astype(jnp.float32) + come_keep[...].astype(jnp.float32)).astype(keep.dtype)
    send[...] = (own_send[...].astype(jnp.float32) + come_send[...].astype(jnp.float32)).astype(send.dtype)


def last_kernel(own, come, out):
    out[...] = own[...].astype(jnp.float32) + come[...].astype(jnp.float32)


def halves(plan, own, come):
    blocks, rows, columns = own.shape
    shape = jax.ShapeDtypeStruct((blocks // 2, rows, columns), own.dtype)
    keep_map = lambda i, plan: (insert_bit(i, plan[0], plan[1]), 0, 0)
    send_map = lambda i, plan: (insert_bit(i, plan[0], 1 - plan[1]), 0, 0)
    block = (1, rows, columns)
    taken = [own, own] if come is None else [own, own, come, come]
    maps = [keep_map, send_map] * (len(taken) // 2)
    cost = pl.CostEstimate(flops=own.size, transcendentals=0, bytes_accessed=len(taken) * own.size * 2)
    return pl.pallas_call(
        split_kernel if come is None else join_kernel,
        grid_spec=pltpu.PrefetchScalarGridSpec(
            num_scalar_prefetch=1,
            grid=(blocks // 2,),
            in_specs=[pl.BlockSpec(block, m) for m in maps],
            out_specs=[pl.BlockSpec(block, lambda i, plan: (i, 0, 0))] * 2,
        ),
        out_shape=(shape, shape),
        cost_estimate=cost,
    )(plan, *taken)


def scatter_sum(grid, value):
    rows = value.shape[0] // grid.total
    held = value.reshape(grid.total, rows, value.shape[1])
    come = None
    for step, stage in enumerate(grid.stages):
        keep, send = halves(grid.plan(step), held, come)
        come = grid.swap(send, stage)
        held = keep
    out = pl.pallas_call(
        last_kernel,
        out_shape=jax.ShapeDtypeStruct(held.shape, jnp.float32),
        cost_estimate=pl.CostEstimate(flops=held.size, transcendentals=0, bytes_accessed=8 * held.size),
    )(held, come)
    return out.reshape(rows, value.shape[1])


def gather_small(grid, value):
    here = grid.here()
    held = value[None]
    for bit in range(grid.bits):
        come = grid.swap(held, (bit, bit))
        mine = (here >> bit) & 1
        held = jnp.where(mine == 0, jnp.concatenate([held, come]), jnp.concatenate([come, held]))
    return held


def scatter_small(grid, value):
    here = grid.here()
    held = value
    for bit in range(grid.bits - 1, -1, -1):
        mine = (here >> bit) & 1
        half = held.shape[0] // 2
        upper = mine == 1
        send = jnp.where(upper, held[:half], held[half:])
        keep = jnp.where(upper, held[half:], held[:half])
        held = keep + grid.swap(send, (bit, bit))
    return held


def body(
    grid,
    hidden_in,
    segment_ids,
    out_grad,
    norm1_gain,
    norm1_bias,
    norm2_gain,
    norm2_bias,
    qkv_weight,
    qkv_bias,
    proj_weight,
    proj_bias,
    up_weight,
    up_bias,
    down_weight,
    down_bias,
):
    small = (norm1_gain, norm1_bias, norm2_gain, norm2_bias, qkv_bias, proj_bias, up_bias, down_bias)
    widths = [entry.shape[0] for entry in small]
    packed = jnp.concatenate(small)
    packed = jnp.pad(packed, (0, -packed.shape[0] % 128))
    spread = gather_small(grid, packed)
    pieces, at = [], 0
    for width in widths:
        pieces.append(spread[:, at : at + width].reshape(-1))
        at += width
    gain_one, shift_one, gain_two, shift_two, b_qkv, b_proj, b_up, b_down = pieces
    w_qkv, w_proj, w_up, w_down = (
        lax.all_gather(entry, AXES, axis=0, tiled=True) for entry in (qkv_weight, proj_weight, up_weight, down_weight)
    )
    seq_count, length, model_width = hidden_in.shape
    row_count = seq_count * length
    scale = HEAD ** (-0.5)
    flat = hidden_in.reshape(row_count, model_width).astype(jnp.float32)
    grad_rows = out_grad.reshape(row_count, model_width)
    valid = (segment_ids != DOCS - 1).astype(jnp.float32).reshape(row_count, 1)
    cosine, sine = angles(segment_ids)
    normed_one = (
        normed(flat, gain_one.astype(jnp.float32)) + shift_one.astype(jnp.float32)
    ).astype(jnp.bfloat16)
    mixed = jnp.dot(normed_one, w_qkv, preferred_element_type=jnp.float32) + b_qkv.astype(
        jnp.float32
    )
    raw = mixed.reshape(seq_count, length, 3, HEADS, HEAD)
    raw_query = raw[:, :, 0]
    raw_keys = raw[:, :, 1]

    def rope_pair(first_part, second_part):
        return (rotate(first_part, cosine, sine), rotate(second_part, cosine, sine))

    (turned_query, turned_keys), rope_pull = jax.vjp(rope_pair, raw_query, raw_keys)
    query = (turned_query * scale).astype(jnp.bfloat16)
    keys = turned_keys.astype(jnp.bfloat16)
    values = raw[:, :, 2].astype(jnp.bfloat16)
    heads_out, log_sums = lax.map(attend_forward, (query, keys, values, segment_ids))
    attended = (heads_out.reshape(row_count, model_width) * valid).astype(jnp.bfloat16)
    projected = jnp.dot(attended, w_proj, preferred_element_type=jnp.float32) + b_proj.astype(
        jnp.float32
    )
    normed_two = (
        normed(flat, gain_two.astype(jnp.float32)) + shift_two.astype(jnp.float32)
    ).astype(jnp.bfloat16)
    before = jnp.dot(normed_two, w_up, preferred_element_type=jnp.float32) + b_up.astype(
        jnp.float32
    )
    after = jax.nn.gelu(before, approximate=False).astype(jnp.bfloat16)
    branch = jnp.dot(after, w_down, preferred_element_type=jnp.float32) + b_down.astype(jnp.float32)
    layer_out = (
        (flat + projected + branch).astype(jnp.bfloat16).reshape(seq_count, length, model_width)
    )
    back_gain_one, back_gain_two, back_qkv, back_proj, back_up, back_down = (
        gain_one, gain_two, w_qkv, w_proj, w_up, w_down
    )
    grad_wide = grad_rows.astype(jnp.float32)
    bias_grad = jnp.sum(grad_wide, axis=0)
    grad_down = jnp.einsum("rf,rd->fd", after, grad_rows, preferred_element_type=jnp.float32)
    d_after = jnp.einsum("rd,fd->rf", grad_rows, back_down, preferred_element_type=jnp.float32)
    gelu_value, gelu_pull = jax.vjp(partial(jax.nn.gelu, approximate=False), before)
    d_before = gelu_pull(d_after)[0].astype(jnp.bfloat16)
    grad_up_bias = jnp.sum(d_before.astype(jnp.float32), axis=0)
    grad_up = jnp.einsum("rd,rf->df", normed_two, d_before, preferred_element_type=jnp.float32)
    d_normed_two = jnp.einsum("rf,df->rd", d_before, back_up, preferred_element_type=jnp.float32)
    norm_value_two, pull_two = jax.vjp(normed, flat, back_gain_two.astype(jnp.float32))
    dx_two, grad_gain_two = pull_two(d_normed_two)
    grad_shift_two = jnp.sum(d_normed_two, axis=0)
    grad_proj = jnp.einsum("rd,re->de", attended, grad_rows, preferred_element_type=jnp.float32)
    d_attended = (
        jnp.einsum("re,de->rd", grad_rows, back_proj, preferred_element_type=jnp.float32) * valid
    ).astype(jnp.bfloat16)
    d_attended = d_attended.reshape(seq_count, length, HEADS, HEAD)
    d_query, d_keys, d_values = lax.map(
        attend_backward, (query, keys, values, segment_ids, log_sums, d_attended)
    )
    d_raw_query, d_raw_keys = rope_pull((d_query * scale, d_keys))
    d_mixed = (
        jnp.stack([d_raw_query, d_raw_keys, d_values], axis=2)
        .reshape(row_count, 3 * model_width)
        .astype(jnp.bfloat16)
    )
    grad_qkv_bias = jnp.sum(d_mixed.astype(jnp.float32), axis=0)
    grad_qkv = jnp.einsum("rd,rc->dc", normed_one, d_mixed, preferred_element_type=jnp.float32)
    d_normed_one = jnp.einsum("rc,dc->rd", d_mixed, back_qkv, preferred_element_type=jnp.float32)
    norm_value_one, pull_one = jax.vjp(normed, flat, back_gain_one.astype(jnp.float32))
    dx_one, grad_gain_one = pull_one(d_normed_one)
    grad_shift_one = jnp.sum(d_normed_one, axis=0)
    input_grad = (
        (grad_wide + dx_one + dx_two).astype(jnp.bfloat16).reshape(seq_count, length, model_width)
    )
    n = grid.total
    sums = (grad_gain_one, grad_shift_one, grad_gain_two, grad_shift_two, grad_qkv_bias, bias_grad, grad_up_bias)
    vectors = jnp.concatenate([entry.reshape(n, -1) for entry in sums], axis=1)
    vectors = jnp.pad(vectors, ((0, 0), (0, -vectors.shape[1] % 128)))
    total = scatter_small(grid, vectors)
    outs, at = [], 0
    for entry in sums:
        width = entry.shape[0] // n
        outs.append(total[0, at : at + width])
        at += width
    low = [scatter_sum(grid, entry.astype(jnp.bfloat16)) for entry in (grad_qkv, grad_proj, grad_up, grad_down)]
    return (
        layer_out,
        input_grad,
        outs[0],
        outs[1],
        outs[2],
        outs[3],
        low[0],
        outs[4],
        low[1],
        outs[5],
        low[2],
        outs[6],
        low[3],
        outs[5],
    )


NT = (((1,), (1,)), ((), ()))
NN = (((1,), (0,)), ((), ()))
TN = (((0,), (0,)), ((), ()))
PAIR = 2 * HEAD
ROWS = 256
TOKENS = 512
QUERIES = 512


def mul(left, right, dims):
    return lax.dot_general(left, right, dims, preferred_element_type=jnp.float32)


def params(mebibytes):
    return pltpu.CompilerParams(vmem_limit_bytes=mebibytes << 20)


def cost(flops, moved, special=0):
    return pl.CostEstimate(flops=int(flops), transcendentals=int(special), bytes_accessed=int(moved))


def fixed(shape, at=None):
    place = (0,) * len(shape) if at is None else at
    return pl.BlockSpec(shape, lambda *_: place, pipeline_mode=pl.Buffered(1))


def middle_swap(value):
    quarter = (lax.broadcasted_iota(jnp.int32, value.shape, 1) % 128) // 32
    width = value.shape[1]
    up, down = pltpu.roll(value, width - 32, 1), pltpu.roll(value, 32, 1)
    return jnp.where(quarter == 1, up, jnp.where(quarter == 2, down, value))


def norm_kernel(source, cotangent, scales, *refs):
    one, two, grads = refs[-3:]
    value = source[...].astype(jnp.float32)
    center = value - jnp.mean(value, axis=1, keepdims=True)
    spread = jnp.mean(center * center, axis=1, keepdims=True)
    hat = middle_swap(center * lax.rsqrt(spread + norm_eps))
    table = scales[...].astype(jnp.float32)
    one[...] = (hat * table[0:1] + table[1:2]).astype(jnp.bfloat16)
    two[...] = (hat * table[2:3] + table[3:4]).astype(jnp.bfloat16)
    grads[...] = cotangent[...]


def norms(sequence, source, cotangent, scales, before):
    length, width = source.shape
    steps = length // ROWS
    block = pl.BlockSpec((ROWS, width), lambda i: (i, 0))
    out = pl.BlockSpec((ROWS, width), lambda i: (sequence * steps + i, 0))
    shape = jax.ShapeDtypeStruct((2 * length, width), jnp.bfloat16)
    return pl.pallas_call(
        norm_kernel,
        grid=(steps,),
        in_specs=[block, block, fixed(scales.shape)] + [pl.BlockSpec(memory_space=pl.ANY)] * len(before),
        out_specs=[out] * 3,
        out_shape=[shape] * 3,
        input_output_aliases={3 + n: n for n in range(len(before))},
        compiler_params=params(60),
        cost_estimate=cost(20 * length * width, 10 * length * width),
    )(source, cotangent, scales, *before)


def turn(value, cosine, sine):
    lane = lax.broadcasted_iota(jnp.int32, value.shape, 1) % HEAD
    half = ROT // 2
    up, down = pltpu.roll(value, value.shape[1] - half, 1), pltpu.roll(value, half, 1)
    return value * cosine + jnp.where(lane < half, up, down) * sine


def chosen(place, chip, near, far, *index):
    spot, half = place[chip], near.shape[0]
    return jnp.where(spot < half, near[(spot % half, *index)], far[(spot % half, *index)])


def arrange(place, half, weights, ordered, ordered_proj):
    chips = 2 * weights[0].shape[0]
    for part in range(3):
        near, far = weights[2 * part : 2 * part + 2]
        rows, width = near.shape[1:]
        for chip in range(chips):
            block = chosen(place, chip, near, far)
            ordered[chip * rows : (chip + 1) * rows, part * width : (part + 1) * width] = block
    near, far = weights[6:]
    below = near.shape[1] // 4
    for chip in range(chips // 2):
        block = chosen(place, half * chips // 2 + chip, near, far)
        for n in range(4):
            ordered_proj[chip * below : (chip + 1) * below, n * width : (n + 1) * width] = block[n * below : (n + 1) * below]


def weight_specs(weights, first):
    chips, _, width = weights[0].shape
    found = [fixed((chips, 64, width), (0, first + part, 0)) for part in range(3) for _ in weights]
    return found + [fixed((chips, 128, width))] * 2


def weight_scratch(weights):
    chips, _, width = weights[0].shape
    return [pltpu.VMEM((128 * chips, 3 * width), jnp.bfloat16), pltpu.VMEM((32 * chips, 4 * width), jnp.bfloat16)]


def project_kernel(half, place, normed, grads, *refs):
    weights = refs[:8]
    bias, cosine, sine, segments, out, ordered, ordered_proj = refs[8:]
    width = out.shape[-1]

    @pl.when(pl.program_id(0) == 0)
    def _():
        arrange(place, half, weights, ordered, ordered_proj)

    for part in range(3):
        columns = slice(part * width, (part + 1) * width)
        value = mul(normed[...], ordered[:, columns], NN) + bias[part].astype(jnp.float32)
        if part == 2:
            out[part] = value.astype(out.dtype)
            continue
        for at in range(0, width, PAIR):
            turned = turn(value[:, at : at + PAIR], cosine[...], sine[...])
            out[part, :, at : at + PAIR] = (turned * (HEAD ** (-0.5) if part == 0 else 1.0)).astype(out.dtype)
    valid = (segments[...] != DOCS - 1).astype(jnp.float32)
    out[3] = (mul(grads[...], ordered_proj[...], NT) * valid).astype(out.dtype)


def project(half, place, normed, grads, weights, first, proj, bias, cosine, sine, segments):
    tokens, model = normed.shape
    width = weights[0].shape[-1]
    rows = lambda n: pl.BlockSpec((TOKENS, n), lambda i, *_: (i, 0))
    return pl.pallas_call(
        partial(project_kernel, half),
        grid_spec=pltpu.PrefetchScalarGridSpec(
            num_scalar_prefetch=1,
            grid=(tokens // TOKENS,),
            in_specs=[rows(model), rows(model)]
            + weight_specs(weights, first)
            + [fixed(bias.shape), rows(PAIR), rows(PAIR), rows(1)],
            out_specs=pl.BlockSpec((4, TOKENS, width), lambda i, *_: (0, i, 0)),
            scratch_shapes=weight_scratch(weights),
        ),
        out_shape=jax.ShapeDtypeStruct((4, tokens, width), jnp.bfloat16),
        compiler_params=params(60),
        cost_estimate=cost(8 * tokens * model * width, 6 * tokens * model),
    )(place, normed, grads, *weights * 3, *proj, bias, cosine, sine, segments)


def attention_kernel(
    q_ref, k_ref, v_ref, g_ref, cosine, sine, seg_row, seg_col, *rest
):
    out, d_out, mask, dk_sum, dv_sum = rest[-5:]
    length = q_ref.shape[1]
    blocks = length // QUERIES

    @pl.when(pl.program_id(0) == 0)
    def _():
        for block in range(blocks):
            start = block * QUERIES
            end = start + QUERIES
            key_pos = lax.broadcasted_iota(jnp.int32, (QUERIES, end), 1)
            query_pos = lax.broadcasted_iota(jnp.int32, (QUERIES, end), 0) + start
            allowed = (key_pos <= query_pos) & (seg_col[start:end, :] == seg_row[0, :, :end])
            mask[start:end, :end] = jnp.where(allowed, 0.0, masked_score)

    lane = lax.broadcasted_iota(jnp.int32, (QUERIES, PAIR), 1)
    for block in range(blocks - 1, -1, -1):
        start = block * QUERIES
        end = start + QUERIES
        rows = slice(start, end)
        keys, values = k_ref[0, :end, :], v_ref[0, :end, :]
        query, grads = q_ref[0, rows, :], g_ref[0, rows, :]
        hide = mask[rows, :end]
        pieces = []
        for head in range(2):
            mine = lane < HEAD if head == 0 else lane >= HEAD
            own_query = jnp.where(mine, query, jnp.zeros_like(query))
            own_grads = jnp.where(mine, grads, jnp.zeros_like(grads))
            scores = mul(own_query, keys, NT) + hide
            exponent = jnp.exp(scores - jnp.max(scores, axis=1, keepdims=True))
            probs = exponent * (1.0 / jnp.sum(exponent, axis=1, keepdims=True))
            low = probs.astype(jnp.bfloat16)
            mixed = mul(low, values, NN)
            d_probs = mul(own_grads, values, NT)
            inner = jnp.sum(own_grads.astype(jnp.float32) * mixed, axis=1, keepdims=True)
            d_scores = (probs * (d_probs - inner)).astype(jnp.bfloat16)
            pieces.append((mixed, mul(d_scores, keys, NN)))
            d_keys, d_values = mul(d_scores, own_query, TN), mul(low, own_grads, TN)
            if block == blocks - 1 and head == 0:
                dk_sum[:end, :] = d_keys
                dv_sum[:end, :] = d_values
            else:
                dk_sum[:end, :] += d_keys
                dv_sum[:end, :] += d_values
        mine = lane < HEAD
        valid = (seg_col[rows, :] != DOCS - 1).astype(jnp.float32)
        out[rows, :] = (jnp.where(mine, pieces[0][0], pieces[1][0]) * valid).astype(out.dtype)
        d_query = turn(jnp.where(mine, pieces[0][1], pieces[1][1]), cosine[rows, :], -sine[rows, :])
        d_out[0, rows, :] = (d_query * HEAD ** (-0.5)).astype(d_out.dtype)
    d_out[1] = turn(dk_sum[...], cosine[...], -sine[...]).astype(d_out.dtype)
    d_out[2] = dv_sum[...].astype(d_out.dtype)


def attention(sequence, parts, cosine, sine, segments, before):
    length = segments.shape[1]
    tokens, width = parts.shape[1:]
    part = lambda p: pl.BlockSpec((1, length, PAIR), lambda j: (p, sequence, j))
    table = lambda n: pl.BlockSpec((length, n), lambda j: (sequence, 0))
    anywhere = pl.BlockSpec(memory_space=pl.ANY)
    return pl.pallas_call(
        attention_kernel,
        grid=(width // PAIR,),
        in_specs=[
            part(0),
            part(1),
            part(2),
            part(3),
            table(PAIR),
            table(PAIR),
            pl.BlockSpec((1, 1, length), lambda j: (sequence, 0, 0)),
            table(1),
        ]
        + [anywhere] * len(before),
        out_specs=[
            pl.BlockSpec((length, PAIR), lambda j: (sequence, j)),
            pl.BlockSpec((3, length, PAIR), lambda j: (0, sequence, j)),
        ],
        out_shape=[
            jax.ShapeDtypeStruct((tokens, width), jnp.bfloat16),
            jax.ShapeDtypeStruct((3, tokens, width), jnp.bfloat16),
        ],
        input_output_aliases={8 + n: n for n in range(len(before))},
        scratch_shapes=[pltpu.VMEM((length, length), jnp.float32)] + [pltpu.VMEM((length, PAIR), jnp.float32)] * 2,
        compiler_params=params(32),
        cost_estimate=cost(24 * tokens * length * width, 8 * tokens * width, tokens * length * width // 200),
    )(*[parts] * 4, cosine, sine, segments[:, None, :], segments.reshape(tokens, 1), *before)


def put_out(staged, keep, send, done):
    half = keep.shape[0]
    copies = [
        pltpu.make_async_copy(staged.at[pl.ds(n * half, half)], target, done.at[n])
        for n, target in enumerate((keep, send))
    ]
    for copy in copies:
        copy.start()
    for copy in copies:
        copy.wait()


def attention_grads_kernel(place, *refs):
    normed, d_mixed = refs[:2]
    more = refs[2:-7]
    keep, send, sums, totals, proj_total, staged, done = refs[-7:]
    step, last = pl.program_id(0), pl.num_programs(0) - 1
    width = d_mixed.shape[-1]
    chips = staged.shape[0]
    parts = totals.shape[0]
    rows = totals.shape[1] // chips

    @pl.when(step == 0)
    def _():
        totals[...] = jnp.zeros_like(totals)
        sums[...] = jnp.zeros_like(sums)
        if more:
            proj_total[...] = jnp.zeros_like(proj_total)

    for part in range(parts):
        totals[part] += mul(normed[...], d_mixed[part], TN)
        sums[part] += jnp.sum(d_mixed[part].astype(jnp.float32), axis=0, keepdims=True)
    if more:
        for n, attended in enumerate(more[:2]):
            proj_total[n * width : (n + 1) * width, :] += mul(attended[...], more[2][...], TN)

    @pl.when(step == last)
    def _():
        for chip in range(chips):
            spot = place[chip]
            for part in range(parts):
                change = totals[part, chip * rows : (chip + 1) * rows, :]
                staged[spot, part * rows : (part + 1) * rows, :] = change.astype(staged.dtype)
            if more:
                below = proj_total.shape[0] // chips
                for n in range(4):
                    change = proj_total[chip * below : (chip + 1) * below, n * width : (n + 1) * width]
                    start = parts * rows + n * below
                    staged[spot, start : start + below, :] = change.astype(staged.dtype)
        put_out(staged, keep, send, done)


def attention_grads(place, normed, d_mixed, more):
    tokens, model = normed.shape
    parts, _, width = d_mixed.shape
    chips = place.shape[0]
    rows = parts * model // chips + (4 * 2 * width // chips if more else 0)
    token = lambda n: pl.BlockSpec((TOKENS, n), lambda i, *_: (i, 0))
    half = jax.ShapeDtypeStruct((chips // 2, rows, width), jnp.bfloat16)
    anywhere = pl.BlockSpec(memory_space=pl.ANY)
    return pl.pallas_call(
        attention_grads_kernel,
        grid_spec=pltpu.PrefetchScalarGridSpec(
            num_scalar_prefetch=1,
            grid=(tokens // TOKENS,),
            in_specs=[token(model), pl.BlockSpec((parts, TOKENS, width), lambda i, *_: (0, i, 0))]
            + ([token(width), token(width), token(model)] if more else []),
            out_specs=[anywhere, anywhere, pl.BlockSpec((parts, 1, width), lambda i, *_: (0, 0, 0))],
            scratch_shapes=[
                pltpu.VMEM((parts, model, width), jnp.float32),
                pltpu.VMEM((2 * width, model), jnp.float32),
                pltpu.VMEM((chips, rows, width), jnp.bfloat16),
                pltpu.SemaphoreType.DMA((2,)),
            ],
        ),
        out_shape=[half, half, jax.ShapeDtypeStruct((parts, 1, width), jnp.float32)],
        compiler_params=params(60 if more else 26),
        cost_estimate=cost(8 * tokens * model * width, 6 * tokens * model),
    )(place, normed, d_mixed, *more)


def share_out(step, steps, earlier, mine, sends, value):
    each = steps // 2 // len(sends)
    for start, end, ref, more in [(0, steps // 2, mine, earlier[:1])] + [
        (steps // 2 + n * each, steps // 2 + (n + 1) * each, send, earlier[1:]) for n, send in enumerate(sends)
    ]:

        @pl.when((step >= start) & (step < end))
        def _():
            total = value
            for one in more:
                total = total + one[...].astype(jnp.float32)
            ref[...] = total.astype(ref.dtype)


def attention_back_kernel(half, pieces, place, d_mixed, attended, *refs):
    count = 2 * (1 + pieces) + 2
    weights, before, results = refs[:8], refs[8:-count], refs[-count:-2]
    ordered, ordered_proj = refs[-2:]
    step, steps = pl.program_id(0), pl.num_programs(0)

    @pl.when(step == 0)
    def _():
        arrange(place, half, weights, ordered, ordered_proj)

    change = jnp.concatenate([d_mixed[part] for part in range(3)], axis=1)
    share_out(step, steps, before[:2], results[0], results[1 : 1 + pieces], mul(change, ordered[...], NT))
    share_out(step, steps, before[2:], results[1 + pieces], results[2 + pieces :], mul(attended[...], ordered_proj[...], NN))


def attention_back(half, pieces, place, d_mixed, attended, weights, first, proj, before):
    parts, tokens, width = d_mixed.shape
    model = 128 * weights[0].shape[0]
    steps = tokens // TOKENS
    own = pl.BlockSpec((TOKENS, model), lambda i, *_: (jnp.minimum(i, steps // 2 - 1), 0))
    other = pl.BlockSpec((TOKENS, model), lambda i, *_: (jnp.maximum(i - steps // 2, 0), 0))
    each = steps // 2 // pieces
    shape = lambda n: jax.ShapeDtypeStruct((n * TOKENS, model), jnp.bfloat16)
    sent = [
        pl.BlockSpec((TOKENS, model), lambda i, *_, n=n: (jnp.clip(i - steps // 2 - n * each, 0, each - 1), 0))
        for n in range(pieces)
    ]
    return pl.pallas_call(
        partial(attention_back_kernel, half, pieces),
        grid_spec=pltpu.PrefetchScalarGridSpec(
            num_scalar_prefetch=1,
            grid=(steps,),
            in_specs=[
                pl.BlockSpec((parts, TOKENS, width), lambda i, *_: (0, i, 0)),
                pl.BlockSpec((TOKENS, width), lambda i, *_: (i, 0)),
            ]
            + weight_specs(weights, first)
            + [own, other] * (len(before) // 2),
            out_specs=([own] + sent) * 2,
            scratch_shapes=weight_scratch(weights),
        ),
        out_shape=([shape(steps // 2)] + [shape(each)] * pieces) * 2,
        compiler_params=params(60),
        cost_estimate=cost(8 * tokens * model * width, 8 * tokens * model),
    )(place, d_mixed, attended, *weights * 3, *proj, *before)


def forward_kernel(place, normed, grads, near, far, bias, *refs):
    earlier, refs = refs[:-18], refs[-18:]
    keep, send, sums = refs[:3]
    outs = refs[3:7]
    own_normed, own_grads, up, down, after, d_before, results, staged, arrived, shared, left = refs[7:18]
    tokens, model = own_normed.shape
    hidden = up.shape[1]
    half_tokens = tokens // 2
    rows = near.shape[1] // 2
    chips = 2 * near.shape[0]
    blocks = tokens // ROWS

    def pieces(chip):
        at = pl.ds(chip * rows, rows)
        return ((0, up.at[at], 2 * chip), (rows, down.at[at], 2 * chip + 1))

    def row_loads(block):
        at = pl.ds(block * ROWS, ROWS)
        return [
            pltpu.make_async_copy(source.at[at], target.at[at], arrived.at[2 * chips + 2 * block + n])
            for n, (source, target) in enumerate(((normed, own_normed), (grads, own_grads)))
        ]

    loads = [pltpu.make_async_copy(ref, results.at[n], shared.at[n]) for n, ref in enumerate(earlier)]
    for chip in range(chips):
        spot = place[chip]
        for start, target, n in pieces(chip):
            for own, source in ((True, near), (False, far)):

                @pl.when((spot < chips // 2) == own)
                def _():
                    held = source.at[spot % (chips // 2), pl.ds(start, rows)]
                    pltpu.make_async_copy(held, target, arrived.at[n]).start()

    for block in range(blocks):
        for load in row_loads(block):
            load.start()
    for load in loads:
        load.start()
    for chip in range(chips):
        for start, target, n in pieces(chip):
            pltpu.make_async_copy(near.at[0, pl.ds(start, rows)], target, arrived.at[n]).wait()
    offset = bias[...].astype(jnp.float32)
    bias_total = jnp.zeros_like(offset)
    for block in range(blocks):
        at = slice(block * ROWS, (block + 1) * ROWS)
        for load in row_loads(block):
            load.wait()
        before = mul(own_normed[at, :], up[...], NN) + offset
        change = mul(own_grads[at, :], down[...], NT)
        share = 0.5 + 0.5 * lax.erf(before * 0.7071067811865476)
        density = jnp.exp(-0.5 * before * before) * 0.3989422804014327
        after[at, :] = (before * share).astype(after.dtype)
        low = (change * (share + before * density)).astype(d_before.dtype)
        d_before[at, :] = low
        bias_total += jnp.sum(low.astype(jnp.float32), axis=0, keepdims=True)
    sums[...] = bias_total
    for load in loads:
        load.wait()
    stores = []
    for block in range(blocks):
        at = slice(block * ROWS, (block + 1) * ROWS)
        side = 0 if block * ROWS < half_tokens else 1
        own = pl.ds(block * ROWS - side * half_tokens, ROWS)
        for which, value in enumerate((mul(after[at, :], down[...], NN), mul(d_before[at, :], up[...], NT))):
            n = 2 * which + side
            if n < len(earlier):
                value += results[n, own, :].astype(jnp.float32)
            results[n, own, :] = value.astype(results.dtype)
            store = pltpu.make_async_copy(results.at[n, own], outs[n].at[own], left.at[2 + 2 * block + which])
            store.start()
            stores.append(store)
    tile = 256
    for start in range(0, hidden, tile):
        change = mul(own_normed[...], d_before[:, start : start + tile], TN).astype(staged.dtype)
        for chip in range(chips):
            staged[place[chip], :rows, start : start + tile] = change[chip * rows : (chip + 1) * rows]
        change = mul(after[:, start : start + tile], own_grads[...], TN).astype(staged.dtype)
        for n in range(tile // rows):
            staged[place[start // rows + n], rows:, :] = change[n * rows : (n + 1) * rows]
    half = keep.shape[0]
    for n, target in enumerate((keep, send)):
        store = pltpu.make_async_copy(staged.at[pl.ds(n * half, half)], target, left.at[n])
        store.start()
        stores.append(store)
    for store in stores:
        store.wait()


def forward_chunk(place, normed, grads, weights, bias, earlier):
    tokens, model = normed.shape
    chips, both_rows, hidden = weights[0].shape
    chips *= 2
    low = lambda *shape: pltpu.VMEM(shape, jnp.bfloat16)
    blocks = jax.ShapeDtypeStruct((chips // 2, both_rows, model), jnp.bfloat16)
    anywhere = pl.BlockSpec(memory_space=pl.ANY)
    share = jax.ShapeDtypeStruct((tokens // 2, model), jnp.bfloat16)
    small = pl.BlockSpec((1, hidden), lambda i, *_: (0, 0))
    counts = (2 * chips + 2 * (tokens // ROWS), 4, 2 + 2 * (tokens // ROWS))
    return pl.pallas_call(
        forward_kernel,
        grid_spec=pltpu.PrefetchScalarGridSpec(
            num_scalar_prefetch=1,
            grid=(1,),
            in_specs=[anywhere] * 4 + [small] + [anywhere] * len(earlier),
            out_specs=[anywhere, anywhere, small] + [anywhere] * 4,
            scratch_shapes=[
                low(tokens, model),
                low(tokens, model),
                low(model, hidden),
                low(hidden, model),
                low(tokens, hidden),
                low(tokens, hidden),
                low(4, tokens // 2, model),
                low(chips, both_rows, model),
            ]
            + [pltpu.SemaphoreType.DMA((count,)) for count in counts],
        ),
        out_shape=[blocks, blocks, jax.ShapeDtypeStruct((1, hidden), jnp.float32)] + [share] * 4,
        compiler_params=params(44),
        cost_estimate=cost(12 * tokens * model * hidden, 16 * tokens * model, 2 * tokens * hidden),
    )(place, normed, grads, *weights, bias, *earlier)


def both_of(left, *right):
    come = right[0][...]
    if len(right) > 1:
        come = jnp.where(pl.program_id(0) < pl.num_programs(0) // 2, come, right[1][...])
    return left[...].astype(jnp.float32) + come.astype(jnp.float32)


def finish_out_kernel(hidden, mine, come, scales, layer_out):
    table = scales[...].astype(jnp.float32)
    total = both_of(mine, come) + table[0:1] + table[1:2]
    layer_out[...] = (hidden[...].astype(jnp.float32) + total).astype(layer_out.dtype)


def finish_grad_kernel(hidden, grads, one_mine, one_come, two_mine, two_come, scales, input_grad, sums):
    value = hidden[...].astype(jnp.float32)
    cotangent = grads[...].astype(jnp.float32)
    table = scales[...].astype(jnp.float32)
    center = value - jnp.mean(value, axis=1, keepdims=True)
    scale = lax.rsqrt(jnp.mean(center * center, axis=1, keepdims=True) + norm_eps)
    hat = center * scale
    one, two = middle_swap(both_of(one_mine, one_come)), middle_swap(both_of(two_mine, two_come))
    gained = one * table[0:1] + two * table[1:2]
    mean = jnp.mean(gained, axis=1, keepdims=True)
    slope = jnp.mean(gained * hat, axis=1, keepdims=True)
    input_grad[...] = (cotangent + (gained - mean - hat * slope) * scale).astype(input_grad.dtype)

    @pl.when(pl.program_id(0) == 0)
    def _():
        sums[...] = jnp.zeros_like(sums)

    for row, column in enumerate((one * hat, one, two * hat, two, cotangent)):
        sums[row : row + 1, :] += jnp.sum(column, axis=0, keepdims=True)


def finish(kernel, arrays, scales, with_sums):
    length, width = arrays[0].shape
    block = pl.BlockSpec((ROWS, width), lambda i: (i, 0))
    steps, specs = length // ROWS, []
    for array in arrays:
        if isinstance(array, tuple):
            specs.append(pl.BlockSpec((ROWS, width), lambda i: (jnp.minimum(i, steps // 2 - 1), 0)))
            specs.append(pl.BlockSpec((ROWS, width), lambda i: (jnp.maximum(i - steps // 2, 0), 0)))
        else:
            specs.append(block)
    arrays = jax.tree.leaves(arrays)
    shape = jax.ShapeDtypeStruct((length, width), jnp.bfloat16)
    more = [pl.BlockSpec((8, width), lambda i: (0, 0))] if with_sums else []
    return pl.pallas_call(
        kernel,
        grid=(length // ROWS,),
        in_specs=specs + [fixed(scales.shape)],
        out_specs=[block] + more,
        out_shape=[shape] + [jax.ShapeDtypeStruct((8, width), jnp.float32)] * len(more),
        compiler_params=params(60),
        cost_estimate=cost(40 * length * width, 2 * (len(arrays) + 1) * length * width),
    )(*arrays, scales)


def by_core(core, mine, come):
    return jnp.where(core == 0, mine, come), jnp.where(core == 0, come, mine)


def qkv_rows_kernel(core, mine_one, come_one, mine_two, come_two, out):
    parts, _, width = mine_one.shape
    for part in range(parts):
        for half, (mine, come) in enumerate(((mine_one, come_one), (mine_two, come_two))):
            even, odd = by_core(core[0], mine[part], come[part])
            for head in range(width // HEAD):
                at = slice(head * HEAD, (head + 1) * HEAD)
                start = (part * 2 + half) * 2 * width + head * PAIR
                out[:, start : start + PAIR] = jnp.concatenate([even[:, at], odd[:, at]], axis=1)


def up_rows_kernel(core, mine_one, come_one, mine_two, come_two, out):
    width = mine_one.shape[2]
    first, second = by_core(core[0], mine_one[0], come_one[0]), by_core(core[0], mine_two[0], come_two[0])
    for chip in range(width // 64):
        at = slice(chip * 64, (chip + 1) * 64)
        for which in range(2):
            start = ((chip // 2) * 2 + which) * 256 + (chip % 2) * 128
            out[:, start : start + 128] = jnp.concatenate([first[which][:, at], second[which][:, at]], axis=1)


def whole_rows(kernel, core, halves, shape):
    operands = [array for half in halves for array in half]
    return pl.pallas_call(
        kernel,
        grid_spec=pltpu.PrefetchScalarGridSpec(
            num_scalar_prefetch=1,
            grid=(1,),
            in_specs=[fixed(array.shape) for array in operands],
            out_specs=pl.BlockSpec(shape, lambda i, *_: (0, 0)),
        ),
        out_shape=jax.ShapeDtypeStruct(shape, jnp.float32),
        compiler_params=params(16),
        cost_estimate=cost(0, 16 * shape[0] * shape[1]),
    )(core, *operands)


BITS = {"y": 0, "core": 1, "x": 2, "z_low": 3, "z_high": 4}
SPLIT = ("zx", "core", "y")
CORES = ("core", "core")
STAGES = (("x", "y"), ("y", "x"), ("z_low", "z_low"), ("z_high", "z_high"))


class Pairs:
    def __init__(self, total):
        self.total = total

    def here(self):
        y = lax.axis_size("y")
        return (lax.axis_index("zx") * 2 + lax.axis_index("core")) * y + lax.axis_index("y")

    def bit(self, name):
        return (self.here() >> BITS[name]) & 1

    def swap(self, value, names):
        moves = []
        for device in range(self.total):
            name = names[(device >> BITS["core"]) & 1]
            moves.append((device, device ^ (1 << BITS[name])))
        return lax.ppermute(value, SPLIT, moves)

    def places(self):
        chip = jnp.arange(self.total // 2, dtype=jnp.int32)
        bits = {"y": chip & 1, "x": (chip >> 1) & 1, "z_low": (chip >> 2) & 1, "z_high": (chip >> 3) & 1}
        differs = {name: bits[name] ^ self.bit(name) for name in bits}
        place = jnp.zeros_like(chip)
        for first, second in STAGES:
            place = 2 * place + jnp.where(lax.axis_index("core") == 0, differs[first], differs[second])
        return place


class Sum:
    def __init__(self, pairs, keep, send):
        self.pairs, self.arrays, self.stage = pairs, (keep, send), 0

    def ready(self, arrays):
        if self.stage == 0:
            return arrays
        keep, come = arrays
        half = keep.shape[0] // 2
        return add_low(keep[:half], come[:half]), add_low(keep[half:], come[half:])

    def move(self, arrays):
        keep, send = arrays
        self.arrays = keep, self.pairs.swap(send, STAGES[self.stage])
        self.stage += 1

    def result(self):
        keep, come = self.arrays
        return keep[0].astype(jnp.float32) + come[0].astype(jnp.float32)


class Gather:
    def __init__(self, pairs, own):
        self.pairs, self.arrays, self.stage = pairs, (own[None],), 0

    def ready(self, arrays):
        return arrays if self.stage == 0 else (jnp.concatenate(arrays),)

    def move(self, arrays):
        self.stage += 1
        self.arrays = arrays[0], self.pairs.swap(arrays[0], STAGES[-self.stage])

    def result(self):
        return self.arrays


class Trade:
    def __init__(self, pairs, *arrays):
        self.pairs, self.arrays, self.stage = pairs, arrays, 0

    def ready(self, arrays):
        return arrays

    def move(self, arrays):
        if self.stage == 0:
            arrays = tuple(self.pairs.swap(array, CORES) for array in arrays)
        self.arrays = arrays
        self.stage += 1

    def result(self):
        return self.arrays


def hold(value, tasks):
    value, arrays = lax.optimization_barrier((value, [task.arrays for task in tasks]))
    for task, own in zip(tasks, arrays):
        task.arrays = tuple(own)
    return value


def tick(after, value, *tasks, done=()):
    if after is not None:
        after = hold(after, tasks + tuple(done))
    for task in tasks:
        task.arrays = task.ready(task.arrays)
    after, value = hold((after, value), tasks)
    for task in tasks:
        task.move(task.arrays)
    return after, value


def add_low(left, right):
    return (left.astype(jnp.float32) + right.astype(jnp.float32)).astype(jnp.bfloat16)


def wide_angles(segments):
    position = lax.broadcasted_iota(jnp.int32, segments.shape, 1)
    change = jnp.concatenate([jnp.ones_like(segments[:, :1], jnp.bool_), segments[:, 1:] != segments[:, :-1]], axis=1)
    place = position - lax.cummax(jnp.where(change, position, 0), axis=1)
    lane = jnp.arange(PAIR) % HEAD
    half = ROT // 2
    freqs = 10000.0 ** (-((lane % half) * 2).astype(jnp.float32) / ROT)
    freqs = jnp.where(lane < ROT, freqs, 0.0)
    theta = place.reshape(-1, 1).astype(jnp.float32) * freqs
    return jnp.cos(theta), jnp.sin(theta) * jnp.where(lane < half, -1.0, 1.0)


def pick(value, which, axis):
    return lax.dynamic_index_in_dim(value, which, axis, keepdims=False)


def paired_body(
    pairs,
    hidden_in,
    segment_ids,
    out_grad,
    norm1_gain,
    norm1_bias,
    norm2_gain,
    norm2_bias,
    qkv_weight,
    qkv_bias,
    proj_weight,
    proj_bias,
    up_weight,
    up_bias,
    down_weight,
    down_bias,
):
    core = lax.axis_index("core")
    heads = HEADS // 2
    rows, model = qkv_weight.shape[0], proj_weight.shape[1]
    width = heads * HEAD // 2
    unit = down_weight.shape[0] // 2
    hidden, grads = hidden_in[0], out_grad[0]

    def columns(which):
        taken = pick(qkv_weight.reshape(rows, 3, heads, 2, HEAD), which, 3).reshape(rows, 3 * 2 * width)
        more = pick(up_weight.reshape(rows, heads, 2, 2, 2, unit), which, 2).transpose(0, 3, 1, 2, 4).reshape(rows, -1)
        return jnp.concatenate([taken, more], axis=1)

    theirs = pairs.swap(columns(1 - core), CORES)
    mine = columns(core)
    both = jnp.where(core == 0, jnp.stack([mine, theirs]), jnp.stack([theirs, mine])).reshape(2 * rows, -1)
    low_qkv = both[:, : 6 * width].reshape(2 * rows, 3, 2, width).transpose(2, 1, 0, 3)
    low_proj = proj_weight.reshape(rows, 4, width).transpose(1, 0, 2).reshape(2, 2 * rows, width)
    low_up = both[:, 6 * width :].reshape(2 * rows, 2, -1).transpose(1, 0, 2)
    low_down = down_weight.reshape(2, unit, model)

    other, other_grads = pairs.swap(hidden, CORES), pairs.swap(grads, CORES)
    segments = jnp.concatenate([segment_ids, pairs.swap(segment_ids, CORES)])
    column = segments.reshape(-1, 1)
    cosine, sine = wide_angles(segments)
    place = pairs.places()

    small = (norm1_gain, norm1_bias, norm2_gain, norm2_bias, qkv_bias, proj_bias, up_bias, down_bias)
    ends = [sum(entry.shape[0] for entry in small[: n + 1]) for n in range(len(small))]
    long = ends[-1] + -ends[-1] % 128
    line = sum(jnp.pad(entry, (end - entry.shape[0], long - end)) for entry, end in zip(small, ends))
    come = pairs.swap(line, CORES)
    lines = Gather(pairs, jnp.where(core == 0, jnp.stack([line, come]), jnp.stack([come, line])).reshape(-1))
    first = Gather(pairs, jnp.concatenate([low_proj, low_qkv[0]]).reshape(-1, width))
    chunks = [Gather(pairs, jnp.concatenate([low_up[h], low_down[h]])) for h in range(2)]
    second = Gather(pairs, low_qkv[1].reshape(-1, width))
    tick(None, (), first, lines)
    tick(None, (), lines)
    tick(None, (), first, lines)
    tick(None, (), lines)
    table = jnp.concatenate(lines.result())[place]
    table = table.reshape(heads, 2, 2, -1).swapaxes(1, 2).reshape(pairs.total, -1)
    spread, at = [], 0
    for entry in small:
        size = entry.shape[0]
        spread.append(table[:, at : at + size].reshape(-1))
        at += size
    gain_one, shift_one, gain_two, shift_two, b_qkv, b_proj, b_up, b_down = spread
    own_bias = pick(b_qkv.reshape(3, heads, 2, HEAD), core, 2).reshape(3, 2, 1, width)
    own_up_bias = pick(b_up.reshape(heads, 2, 2, 2, unit), core, 1).transpose(2, 0, 1, 3).reshape(2, 1, -1)
    scales = jnp.stack([gain_one, shift_one, gain_two, shift_two])
    scales = scales.reshape(4, -1, 2, 2, rows).swapaxes(2, 3).reshape(4, model)
    _, scales = tick(None, scales, first)
    before = norms(0, hidden, grads, scales, ())
    before, (scales, segments) = tick(before, (scales, segments), first, chunks[0])
    column = segments.reshape(-1, 1)
    cosine, sine = wide_angles(segments)
    normed_one, normed_two, both_grads = norms(1, other, other_grads, scales, before)
    (normed_one, cosine, sine), _ = tick((normed_one, cosine, sine), (), chunks[0], done=(first,))
    w_first = first.result()

    parts = project(
        0, place, normed_one, both_grads, w_first, 2, w_first, own_bias[:, 0], cosine, sine, column
    )
    parts, _ = tick(parts, (), chunks[0], chunks[1])
    before = attention(0, parts, cosine, sine, segments, ())
    before, parts = tick(before, parts, chunks[0], chunks[1])
    attended_one, d_mixed = attention(1, parts, cosine, sine, segments, before)
    (attended_one, d_mixed), _ = tick((attended_one, d_mixed), (), chunks[1], second)
    keep, send, qkv_sums_one = attention_grads(place, normed_one, d_mixed, ())
    sum_one = Sum(pairs, keep, send)
    qkv_sums_one, d_mixed = tick(qkv_sums_one, d_mixed, sum_one, second)
    d1, d1_send, out, out_send = attention_back(0, 1, place, d_mixed, attended_one, w_first, 2, w_first, ())

    sum_forward, up_sums = [], []
    before = (out, out_send)
    for chunk in range(2):
        more = [] if chunk else chunks[1:]
        before, normed_two = tick(before, normed_two, *more, sum_one, second, *sum_forward, done=(chunks[chunk],))
        keep, send, sums, *before = forward_chunk(
            place,
            normed_two,
            both_grads,
            chunks[chunk].result(),
            own_up_bias[chunk],
            before,
        )
        up_sums.append(sums)
        sum_forward.append(Sum(pairs, keep, send))
    out, out_send, d2, d2_send = before

    (out, out_send, d2_send), normed_one = tick(
        (out, out_send, d2_send), normed_one, sum_one, sum_forward[0], done=(second,)
    )
    w_second = second.result()
    trade_two = Trade(pairs, d2_send)
    parts = project(
        1, place, normed_one, both_grads, w_second, 0, w_first, own_bias[:, 1], cosine, sine, column
    )
    parts, _ = tick(parts, (), sum_forward[0], sum_forward[1], trade_two, done=(sum_one,))
    before = attention(0, parts, cosine, sine, segments, ())
    before, parts = tick(before, parts, sum_forward[0], done=(trade_two,))
    attended_two, d_mixed = attention(1, parts, cosine, sine, segments, before)
    (attended_two, d_mixed), _ = tick((attended_two, d_mixed), (), sum_forward[1], done=sum_forward[:1])
    d1, d1_send, out, out_send = attention_back(
        1, 1, place, d_mixed, attended_two, w_second, 0, w_first, (d1, d1_send, out, out_send)
    )
    trade = Trade(pairs, d1_send, out_send)
    (d1, out), d_mixed = tick((d1, out), d_mixed, sum_forward[1], trade)
    keep, send, qkv_sums_two = attention_grads(place, normed_one, d_mixed, (attended_one, attended_two, both_grads))
    sum_two = Sum(pairs, keep, send)
    (qkv_sums_two, d1, out), _ = tick((qkv_sums_two, d1, out), (), sum_two, sum_forward[1], done=(trade,))
    d1_come, out_come = trade.result()
    input_grad, sums = finish(
        finish_grad_kernel,
        [hidden, grads, d1, d1_come, d2, *trade_two.result()],
        jnp.stack([gain_one, gain_two]),
        True,
    )
    (input_grad, sums, qkv_sums_one, qkv_sums_two, up_sums), _ = tick(
        (input_grad, sums, qkv_sums_one, qkv_sums_two, up_sums), (), sum_two, done=(sum_forward[1],)
    )
    def both_cores(own):
        own = own[:, None]
        none = jnp.zeros_like(own)
        return jnp.where(core == 0, jnp.concatenate([own, none], axis=1), jnp.concatenate([none, own], axis=1)).reshape(-1)

    def halve(table, name):
        upper = pairs.bit(name) == 1
        half = table.shape[0] // 2
        send = jnp.where(upper, table[:half], table[half:])
        return jnp.where(upper, table[half:], table[:half]) + pairs.swap(send, (name, name))

    sum_qkv = jnp.stack([qkv_sums_one.reshape(3, -1), qkv_sums_two.reshape(3, -1)], axis=1)
    sum_up = jnp.stack([entry.reshape(heads, 2, unit) for entry in up_sums], axis=2)
    entries = [
        sums[0],
        sums[1],
        sums[2],
        sums[3],
        both_cores(sum_qkv.reshape(-1, HEAD)),
        sums[4],
        both_cores(sum_up.reshape(heads, -1)),
    ]
    table = jnp.concatenate([entry.reshape(pairs.total, -1) for entry in entries], axis=1)
    table = jnp.pad(table, ((0, 0), (0, -table.shape[1] % 128)))
    names = list(reversed(BITS))
    for name in names[:1]:
        table = halve(table, name)
    table, out = tick(table, out, sum_two)
    layer_out = finish(finish_out_kernel, [hidden, out, out_come], jnp.stack([b_proj, b_down]), False)[0]
    table = halve(halve(table, names[1]), names[2])
    (table, layer_out), _ = tick((table, layer_out), (), sum_two, done=(sum_one, *sum_forward))
    for name in names[3:]:
        table = halve(table, name)
    low_qkv_one, low_qkv_two = sum_one.result(), sum_two.result()
    low_forward = [task.result() for task in sum_forward]

    def trade_rows(value):
        split = value.reshape(value.shape[0], 2, rows, -1)
        return pick(split, core, 1), pairs.swap(pick(split, 1 - core, 1), CORES)

    which = core.astype(jnp.int32).reshape(1)
    low = (low_qkv_one.reshape(3, 2 * rows, width), low_qkv_two[: 6 * rows].reshape(3, 2 * rows, width))
    grad_qkv = whole_rows(qkv_rows_kernel, which, [trade_rows(value) for value in low], qkv_weight.shape)
    grad_proj = low_qkv_two[6 * rows :].reshape(4, rows, width).transpose(1, 0, 2).reshape(rows, model)
    ups = [trade_rows(entry[: 2 * rows].reshape(1, 2 * rows, -1)) for entry in low_forward]
    grad_up = whole_rows(up_rows_kernel, which, ups, up_weight.shape)
    grad_down = jnp.concatenate([entry[2 * rows :] for entry in low_forward])
    outs, at = [], 0
    for entry in entries:
        size = entry.shape[0] // pairs.total
        outs.append(table[0, at : at + size])
        at += size
    return (
        layer_out[None],
        input_grad[None],
        outs[0],
        outs[1],
        outs[2],
        outs[3],
        grad_qkv,
        outs[4],
        grad_proj,
        outs[5],
        grad_up,
        outs[6],
        grad_down,
        outs[5],
    )


def placed(axes):
    rows, flat = P(axes, None), P(axes)
    whole = P(axes, None, None)
    inside = (whole, rows, whole) + (flat,) * 4 + (rows, flat) * 4
    outside = (whole, whole) + (flat,) * 4 + (rows, flat) * 4
    return inside, outside


def solution(mesh):
    dp, fsdp = mesh.shape["dp"], mesh.shape["fsdp"]
    if (dp, fsdp) == (16, 2):
        split = Mesh(mesh.devices.reshape(dp // 2, 2, fsdp), SPLIT)
        inside, outside = placed(SPLIT)
        step = partial(paired_body, Pairs(dp * fsdp))
        return jax.shard_map(step, mesh=split, in_specs=inside, out_specs=outside, check_vma=False)
    inside, outside = placed(AXES)
    step = partial(body, Grid((dp, fsdp)))
    return jax.shard_map(step, mesh=mesh, in_specs=inside, out_specs=outside, check_vma=False)
```
